256 devices in a mesh: rows: 64 (over z, x, core), tm: 4 (over y).
Axes of the slice: x: 4, y: 4, z: 8, core: 2. Of those that a mesh axis runs over, the one named last changes fastest.
Arguments:
- frames: bfloat16 [16, 128, 256, 256], P('tm', 'rows'), may hold values from -45 to 45, as said below
- norm_gain: float32 [256], replicated, may hold values from 0.1 to 1.9
- conv_weight: bfloat16 [3, 3, 3, 256, 256], replicated, may hold values from -0.078125 to 0.078125
- conv_bias: float32 [256], replicated, may hold values from -3 to 3
- latent_grad: bfloat16 [16, 64, 128, 256], P('tm', None, 'rows'), may hold values from -6 to 6
Outputs:
- latent: bfloat16 [16, 64, 128, 256], P('tm', None, 'rows')
- frames_grad: bfloat16 [16, 128, 256, 256], P('tm', 'rows')
- weight_grad: float32 [3, 3, 3, 256, 256], P(None, None, None, 'tm')
- gain_grad: float32 [256], P('tm')
- bias_grad: float32 [256], P('tm')
The draws below stay inside these ranges and needn't reach their ends.
Inputs may be any that keep to these rules, and one draw needn't show every extreme that they name: `frames`: features of the clip.
All inputs are finite; a program needn't handle non-finite values.
Results may differ from the reference program's by a relative error of at most 0.0045.
Values may be sent and summed in bfloat16 or wider, within the bound.
A program may use at most 128 MiB of HBM per device.

```python
import math
import jax
import jax.numpy as jnp
from jax import lax

C = 256
FRAMES = 16
LAT_ROWS = 64
LAT_COLS = 128
ROWS = 128
COLS = 256


def draw_frames(key, part):
    key_base, key_cell, key_chan = jax.random.split(key, 3)
    shape = (FRAMES, ROWS, COLS, C)
    cell_scale = jnp.exp(jax.random.uniform(key_cell, (FRAMES, ROWS, COLS, 1), jnp.float32, math.log(0.3), math.log(3.0)))
    chan_scale = jnp.exp(jax.random.uniform(key_chan, (C,), jnp.float32, math.log(0.3), math.log(3.0)))
    base = jnp.clip(jax.random.normal(key_base, shape, jnp.float32), -5.0, 5.0)
    return (base * cell_scale * chan_scale).astype(jnp.bfloat16)


def shard_levels(key, extent, pieces, low, largest):
    def one(axis_at, parts):
        heights = jax.random.uniform(jax.random.fold_in(jax.random.fold_in(key, 6), axis_at), (parts,), jnp.float32, low / len(pieces), largest / len(pieces))
        return jnp.repeat(jnp.exp(heights), extent[axis_at] // parts).reshape((-1,) + (1,) * (len(extent) - axis_at - 1))

    gain = one(*pieces[0])
    for cut in pieces[1:]:
        gain = gain * one(*cut)
    return gain


def noise(rng, shape, width, bound, pieces=(), kind=jnp.bfloat16):
    result = jax.random.normal(rng, shape, jnp.float32) * width
    if len(pieces) > 0:
        result = shard_levels(rng, shape, pieces, -0.22, 0.18) * result
    return jnp.clip(result, min=-bound, max=bound).astype(kind)


def setup_inputs(seed: int = 0) -> dict:
    streams_of = jax.random.split(jax.random.key(seed), 6)
    frames = draw_frames(jax.random.fold_in(streams_of[5], 71), 0)
    norm_gain = jnp.clip(1.0 + 0.18 * jax.random.normal(streams_of[1], (C,), jnp.float32), 0.1, 1.9)
    conv_weight = noise(streams_of[2], (3, 3, 3, C, C), (27 * C) ** -0.5, 0.078125)
    conv_bias = noise(streams_of[3], (C,), 0.5, 3.0, (), jnp.float32)
    latent_grad = noise(streams_of[4], (FRAMES, LAT_ROWS, LAT_COLS, C), 1.0, 6.0, ((0, 4), (2, 64)))
    return {"frames": frames, "norm_gain": norm_gain, "conv_weight": conv_weight, "conv_bias": conv_bias, "latent_grad": latent_grad}


def reference(frames, norm_gain, conv_weight, conv_bias, latent_grad):
    signal = frames.astype(jnp.float32)
    inv_rms = lax.rsqrt(lax.optimization_barrier(jnp.mean(signal * signal, axis=-1, keepdims=True)) + 1e-06)
    unit = signal * inv_rms
    normed = unit * norm_gain
    hidden = jax.nn.silu(normed).astype(jnp.bfloat16)
    frame_count, row_count, col_count, channels = hidden.shape
    lat_rows = row_count // 2
    lat_cols = col_count // 2
    padded = jnp.pad(hidden, ((2, 0), (0, 1), (0, 1), (0, 0)))
    grad_flat = latent_grad.reshape(-1, channels)
    running = jnp.zeros((frame_count * lat_rows * lat_cols, channels), jnp.float32)
    spread_sum = jnp.zeros((frame_count + 2, row_count + 2, col_count + 2, channels), jnp.float32)
    blocks = []
    for tap_t in range(3):
        for tap_r in range(3):
            for tap_c in range(3):
                weight_tap = conv_weight[tap_t, tap_r, tap_c]
                window_piece = padded[tap_t:tap_t + frame_count, tap_r:tap_r + 2 * lat_rows:2, tap_c:tap_c + 2 * lat_cols:2]
                window_piece = window_piece.reshape(-1, channels)
                running = running + jnp.dot(window_piece, weight_tap, preferred_element_type=jnp.float32)
                blocks.append(jnp.dot(window_piece.T, grad_flat, preferred_element_type=jnp.float32))
                back_term = jnp.dot(grad_flat, weight_tap.T, preferred_element_type=jnp.float32)
                back_term = back_term.reshape(frame_count, lat_rows, lat_cols, channels)
                spread_sum = spread_sum.at[tap_t:tap_t + frame_count, tap_r:tap_r + 2 * lat_rows:2, tap_c:tap_c + 2 * lat_cols:2].add(back_term)
    latent = (running + conv_bias).reshape(frame_count, lat_rows, lat_cols, channels).astype(jnp.bfloat16)
    weight_grad = jnp.stack(blocks).reshape(3, 3, 3, channels, channels)
    bias_grad = lax.optimization_barrier(jnp.sum(grad_flat.astype(jnp.float32), axis=0))
    hidden_grad = spread_sum[2:, :row_count, :col_count]
    sigma = jax.nn.sigmoid(normed)
    normed_grad = hidden_grad * sigma * (1.0 + normed * (1.0 - sigma))
    gain_grad = lax.optimization_barrier(jnp.sum(normed_grad * unit, axis=(0, 1, 2)))
    unit_grad = normed_grad * norm_gain
    frames_grad = inv_rms * (unit_grad - unit * lax.optimization_barrier(jnp.mean(unit_grad * unit, axis=-1, keepdims=True)))
    return (latent, frames_grad.astype(jnp.bfloat16), weight_grad, gain_grad, bias_grad)
```

```python
import functools

import jax
import jax.numpy as jnp
from jax import lax
from jax.experimental import pallas as pl
from jax.experimental.pallas import tpu as pltpu
from jax.sharding import PartitionSpec as P

F32 = jnp.float32
BF16 = jnp.bfloat16
MESH = pl.DeviceIdType.MESH
EPS = 1e-06
NX, NZ, NY = 4, 8, 4
CHUNKS, TAPS = 7, 4


def shifted(value, axis, steps):
    count = lax.axis_size(axis)
    leading, last = (max(0, -steps), min(count, count - steps))
    return lax.ppermute(value, axis, [(source, source + steps) for source in range(leading, last)])


def dot_nt(left, right):
    return lax.dot_general(left, right, (((1,), (1,)), ((), ())), preferred_element_type=F32)


def dot_nn(left, right):
    return lax.dot_general(left, right, (((1,), (0,)), ((), ())), preferred_element_type=F32)


def inverse_rms(signal):
    return lax.rsqrt(jnp.mean(signal * signal, axis=-1, keepdims=True) + EPS)


def section_kernel(
    frames, early, below, gain, weight, bias, grad, grad_above,
    latent, frames_grad, parts,
    columns, turned, grad_next, spread, tile, gain_sum,
):
    gain_row = gain[...]
    row_at = lax.broadcasted_iota(jnp.int32, (128, 256), 0)

    def hidden_tile(source, at, row, keep):
        for piece in range(4):
            rows = pl.ds(piece * 64, 64)
            signal = source[rows, :].astype(F32)
            normed = signal * inverse_rms(signal) * gain_row
            hidden = normed / (1.0 + jnp.exp(-normed))
            tile[row, 0, rows, :] = hidden[:, :128]
            tile[row, 1, rows, :] = hidden[:, 128:]
        even = jnp.concatenate([tile[row, half, pl.ds(0, 128, stride=2), :] for half in range(2)], axis=1)
        odd = jnp.concatenate([tile[row, half, pl.ds(1, 128, stride=2), :] for half in range(2)], axis=1)
        after = jnp.where(row_at == 127, 0.0, pltpu.roll(even, 127, 0))
        where = pl.ds(pl.multiple_of(at * 128, 128), 128)
        columns[where, pl.ds(row * 768, 256)] = even.astype(BF16)
        columns[where, pl.ds(row * 768 + 256, 256)] = odd.astype(BF16)
        columns[where, pl.ds(row * 768 + 512, 256)] = after.astype(BF16)
        if keep:
            lanes = pl.ds(pl.multiple_of((at - 2) * 128, 128), 128)
            turned[2 * row, :, lanes] = even.T.astype(BF16)
            turned[2 * row + 1, :, lanes] = odd.T.astype(BF16)

    @pl.loop(0, 2)
    def _(at):
        hidden_tile(early.at[at, 0], at, 0, False)
        hidden_tile(early.at[at, 1], at, 1, False)

    @pl.loop(2, 6)
    def _(at):
        hidden_tile(frames.at[at - 2, 0], at, 0, True)
        hidden_tile(frames.at[at - 2, 1], at, 1, True)

    @pl.loop(0, 6)
    def _(at):
        hidden_tile(below.at[at], at, 2, False)
        where = pl.ds(pl.multiple_of(at * 128, 128), 128)
        for which, source in enumerate((grad, grad_above)):
            moved = pltpu.roll(source[where, :].astype(F32), 1, 0)
            grad_next[which, where, :] = jnp.where(row_at == 0, 0.0, moved).astype(BF16)

    spread[0] = jnp.broadcast_to(bias[...], (512, 256))

    @pl.loop(0, 3)
    def _(tap):
        where = pl.ds(pl.multiple_of(tap * 128, 128), 512)
        spread[0] += dot_nn(columns[where, :], weight[tap].reshape(2304, 256))

    latent[...] = spread[0].astype(BF16)
    spread[...] = jnp.zeros_like(spread)
    gain_sum[...] = jnp.zeros_like(gain_sum)

    @pl.loop(0, 3)
    def _(tap):
        where = pl.ds(pl.multiple_of((2 - tap) * 128, 128), 512)
        here, here_next = grad[where, :], grad_next[0, where, :]
        above, above_next = grad_above[where, :], grad_next[1, where, :]
        spread[0] += dot_nt(here, weight[tap, 0]) + dot_nt(here_next, weight[tap, 2])
        spread[0] += dot_nt(above, weight[tap, 6]) + dot_nt(above_next, weight[tap, 8])
        spread[1] += dot_nt(here, weight[tap, 1]) + dot_nt(above, weight[tap, 7])
        spread[2] += dot_nt(here, weight[tap, 3]) + dot_nt(here_next, weight[tap, 5])
        spread[3] += dot_nt(here, weight[tap, 4])
        for spot in range(9):
            tap_r, tap_c = spot // 3, spot % 3
            left = turned[2 * (tap_r % 2) + tap_c % 2]
            if tap_r == 2:
                right = above_next if tap_c == 2 else above
            else:
                right = here_next if tap_c == 2 else here
            block = dot_nn(left, right).astype(BF16)
            parts[0, tap * 9 + spot] = block[:, :128]
            parts[1, tap * 9 + spot] = block[:, 128:]

    @pl.loop(0, 4)
    def _(at):
        where = pl.ds(pl.multiple_of(at * 128, 128), 128)
        for row in range(2):
            for half in range(2):
                lanes = pl.ds(half * 128, 128)
                tile[row, half, pl.ds(0, 128, stride=2), :] = spread[2 * row, where, lanes]
                tile[row, half, pl.ds(1, 128, stride=2), :] = spread[2 * row + 1, where, lanes]
            for piece in range(4):
                rows = pl.ds(piece * 64, 64)
                signal = frames[at, row, rows, :].astype(F32)
                inv = inverse_rms(signal)
                unit = signal * inv
                normed = unit * gain_row
                sigma = 1.0 / (1.0 + jnp.exp(-normed))
                arrived = jnp.concatenate([tile[row, half, rows, :] for half in range(2)], axis=1)
                normed_grad = arrived * sigma * (1.0 + normed * (1.0 - sigma))
                gain_sum[...] += jnp.sum((normed_grad * unit).reshape(8, 8, 256), axis=0)
                unit_grad = normed_grad * gain_row
                mean = jnp.mean(unit_grad * unit, axis=-1, keepdims=True)
                frames_grad[at, row, rows, :] = (inv * (unit_grad - unit * mean)).astype(BF16)

    gain_local = jnp.sum(gain_sum[...], axis=0, keepdims=True)
    bias_local = jnp.sum(grad[pl.ds(0, 512), :].astype(F32), axis=0, keepdims=True)
    spot = lax.broadcasted_iota(jnp.int32, (256, 256), 0) % 64
    gain_rest = gain_local - gain_local.astype(BF16).astype(F32)
    bias_rest = bias_local - bias_local.astype(BF16).astype(F32)
    small = jnp.where(spot == 0, gain_local, jnp.where(spot == 1, bias_local, 0.0))
    small = jnp.where(spot == 2, gain_rest, jnp.where(spot == 3, bias_rest, small)).astype(BF16)
    parts[0, 27] = small[:, :128]
    parts[1, 27] = small[:, 128:]


def section(frames, early, below, gain, weight, bias, grad, grad_above):
    return pl.pallas_call(
        section_kernel,
        out_shape=(
            jax.ShapeDtypeStruct((512, 256), BF16),
            jax.ShapeDtypeStruct((4, 2, 256, 256), BF16),
            jax.ShapeDtypeStruct((2, 28, 256, 128), BF16),
        ),
        in_specs=[pl.BlockSpec(memory_space=pltpu.VMEM)] * 8,
        out_specs=[pl.BlockSpec(memory_space=pltpu.VMEM)] * 3,
        scratch_shapes=[
            pltpu.VMEM((768, 2304), BF16),
            pltpu.VMEM((4, 256, 512), BF16),
            pltpu.VMEM((2, 768, 256), BF16),
            pltpu.VMEM((4, 512, 256), F32),
            pltpu.VMEM((3, 2, 256, 128), F32),
            pltpu.VMEM((8, 256), F32),
        ],
        cost_estimate=pl.CostEstimate(flops=5_500_000_000, bytes_accessed=12_000_000, transcendentals=2_000_000),
    )(frames, early, below, gain, weight, bias, grad, grad_above)


def reduce_kernel(
    parts, latent, result, latent_out, other, mine, first_plus, first_minus, second_plus, second_minus,
    mid, first_plus2, first_minus2, second_plus2, second_minus2,
    low, arrive, total, block, latent_mid,
    core_sem, ring_sem, ring2_sem, z_sem, zback_sem, x_sem, pair_sem, lat_sem,
):
    rows_at = lax.axis_index("rows")
    y = lax.axis_index("tm")
    core, x, z = rows_at % 2, (rows_at // 2) % NX, rows_at // (2 * NX)
    slab = rows_at % (2 * NX)

    def row_of(z_at, x_at, core_at):
        return z_at * (2 * NX) + x_at * 2 + core_at

    sibling = (row_of(z, x, 1 - core), y)

    def along(axis, step):
        if axis == "y":
            return (rows_at, (y + step) % NY)
        if axis == "x":
            return (row_of(z, (x + step) % NX, core), y)
        if axis == "slab":
            return (z * (2 * NX) + (slab + step) % (2 * NX), y)
        return (row_of((z + step) % NZ, x, core), y)

    barrier = pltpu.get_barrier_semaphore()
    friends = [along("slab", step) for step in range(1, 2 * NX)]
    friends += [along("y", 1), along("y", 3)]
    friends += [along("z", step) for step in range(1, NZ)]
    for friend in friends:
        pl.semaphore_signal(barrier, inc=1, device_id=friend, device_id_type=MESH)
    pl.semaphore_wait(barrier, len(friends))

    def copy_to(source, target, sems, at, device):
        return pltpu.make_async_remote_copy(
            src_ref=source, dst_ref=target, send_sem=sems.at[(0, *at)], recv_sem=sems.at[(1, *at)],
            device_id=device, device_id_type=MESH,
        )

    def send(*args):
        copy = copy_to(*args)
        copy.start()
        return copy

    pair = []
    for chunk in range(CHUNKS):
        spots = pl.ds(chunk * TAPS, TAPS)
        pair.append(send(parts.at[1 - core, spots], other.at[spots], core_sem, (chunk,), sibling))
    outer = [
        send(latent.at[(z + step) % NZ], latent_mid.at[z], lat_sem, (0, step), along("z", step))
        for step in range(1, NZ)
    ]
    latent_mid[z] = latent[z]
    started = pair + outer

    def axes_of(chunk):
        return ("y", "x") if chunk % 2 == 0 else ("x", "y")

    def here(axis, step):
        return (y + step) % NY if axis == "y" else (x + step) % NX

    def piece(ref, chunk, stage, at, taps):
        if stage == 0 and axes_of(chunk)[0] == "x":
            return ref.at[chunk, taps, slice(None), at]
        return ref.at[chunk, taps, at]

    FIRST, LAST, ALL = pl.ds(0, 2), pl.ds(2, 2), pl.ds(0, 4)
    banks = (
        (mine, first_plus, first_minus, second_plus, second_minus, ring_sem, BF16),
        (mid, first_plus2, first_minus2, second_plus2, second_minus2, ring2_sem, F32),
    )

    def ring_open(chunk, stage):
        source, plus, minus, _, _, sems, _ = banks[stage]
        axis = axes_of(chunk)[stage]
        far = here(axis, 2)
        return [
            send(piece(source, chunk, stage, far, FIRST), plus.at[chunk], sems, (chunk, 0), along(axis, 1)),
            send(piece(source, chunk, stage, far, LAST), minus.at[chunk], sems, (chunk, 1), along(axis, 3)),
        ]

    def ring_next(chunk, stage, opened):
        source, plus, minus, plus_in, minus_in, sems, kind = banks[stage]
        axis = axes_of(chunk)[stage]
        opened[0].wait_recv()
        ahead = piece(source, chunk, stage, here(axis, 1), FIRST)
        ahead[...] = (ahead[...].astype(F32) + plus[chunk].astype(F32)).astype(kind)
        one = send(piece(source, chunk, stage, here(axis, 1), ALL), plus_in.at[chunk], sems, (chunk, 2), along(axis, 1))
        opened[1].wait_recv()
        behind = piece(source, chunk, stage, here(axis, 3), LAST)
        behind[...] = (behind[...].astype(F32) + minus[chunk].astype(F32)).astype(kind)
        two = send(piece(source, chunk, stage, here(axis, 3), ALL), minus_in.at[chunk], sems, (chunk, 3), along(axis, 3))
        return [one, two]

    def ring_close(chunk, stage, sent):
        source, _, _, plus_in, minus_in, _, _ = banks[stage]
        axis = axes_of(chunk)[stage]
        sent[0].wait_recv()
        sent[1].wait_recv()
        own = piece(source, chunk, stage, here(axis, 0), ALL)[...].astype(F32)
        (mid, low)[stage][chunk] = own + plus_in[chunk].astype(F32) + minus_in[chunk].astype(F32)

    def to_owner(chunk):
        step = (chunk - z + NZ) % NZ
        return pltpu.make_async_remote_copy(
            src_ref=low.at[chunk], dst_ref=arrive.at[step], send_sem=z_sem.at[0, chunk], recv_sem=z_sem.at[1, step],
            device_id=(row_of(chunk, x, core), y), device_id_type=MESH,
        )

    opened, sent, opened2, sent2 = {}, {}, {}, {}
    for chunk in range(CHUNKS):
        pair[chunk].wait_recv()
        spots = pl.ds(chunk * TAPS, TAPS)
        summed = parts[core, spots].astype(F32) + other[spots].astype(F32)
        mine[chunk] = summed.astype(BF16).reshape(TAPS, NY, NX, 16, 128)
        opened[chunk] = ring_open(chunk, 0)
    for chunk in range(CHUNKS):
        sent[chunk] = ring_next(chunk, 0, opened[chunk])
    for copy in outer:
        copy.wait_recv()
    inner = [
        send(latent_mid.at[:, (slab + step) % (2 * NX)], latent_out.at[:, slab], lat_sem, (1, step), along("slab", step))
        for step in range(1, 2 * NX)
    ]
    latent_out[:, slab] = latent_mid[:, slab]
    for chunk in range(CHUNKS):
        ring_close(chunk, 0, sent[chunk])
        opened2[chunk] = ring_open(chunk, 1)
    for chunk in range(CHUNKS):
        sent2[chunk] = ring_next(chunk, 1, opened2[chunk])
    for chunk in range(CHUNKS):
        ring_close(chunk, 1, sent2[chunk])

        @pl.when(z != chunk)
        def _():
            to_owner(chunk).start()

    started += inner
    for table in (opened, sent, opened2, sent2):
        for chunk in range(CHUNKS):
            started += table[chunk]

    def back(step):
        return copy_to(total.at[z], total.at[z], zback_sem, (step,), along("z", step))

    @pl.when(z < CHUNKS)
    def _():
        summed = low[z]
        for step in range(1, NZ):
            pltpu.make_async_remote_copy(
                src_ref=low.at[0], dst_ref=arrive.at[step], send_sem=z_sem.at[0, 0], recv_sem=z_sem.at[1, step],
                device_id=sibling, device_id_type=MESH,
            ).wait_recv()
            summed += arrive[step]
        total[z] = summed.astype(BF16)
        for step in range(1, NZ):
            back(step).start()

    right, left, across = (x + 1) % NX, (x + 3) % NX, (x + 2) % NX
    order = (0, 1, 7, 2, 6, 3, 5, 4)

    def to_right(step, at):
        return copy_to(total.at[at], block.at[x, at], x_sem, (0, step), along("x", 1))

    def to_left(step, at):
        return copy_to(total.at[at], block.at[x, at], x_sem, (1, step), along("x", 3))

    def on_right(step, at):
        half = block.at[left, at, FIRST]
        return copy_to(half, half, x_sem, (2, step), along("x", 1))

    def on_left(step, at):
        half = block.at[right, at, LAST]
        return copy_to(half, half, x_sem, (3, step), along("x", 3))

    def across_core(which, step, at):
        source = total.at[at] if which == 0 else block.at[(left, right, across)[which - 1], at]
        where = (x, left, right, across)[which]
        return copy_to(source, result.at[core, where, at], pair_sem, (which, step), sibling)

    def each(body):
        for step in order:
            at = (z - step + NZ) % NZ

            @pl.when(at < CHUNKS)
            def _():
                body(step, at)

    def fan_one(step, at):
        if step:
            back(step).wait_recv()
        to_right(step, at).start()
        to_left(step, at).start()
        across_core(0, step, at).start()
        result[core, x, at] = total[at]

    def fan_two(step, at):
        to_right(step, at).wait_recv()
        on_right(step, at).start()
        across_core(1, step, at).start()
        result[core, left, at] = block[left, at]
        to_left(step, at).wait_recv()
        on_left(step, at).start()
        across_core(2, step, at).start()
        result[core, right, at] = block[right, at]

    def fan_three(step, at):
        on_right(step, at).wait_recv()
        on_left(step, at).wait_recv()
        across_core(3, step, at).start()
        result[core, across, at] = block[across, at]

    def fan_last(step, at):
        for which in range(4):
            across_core(which, step, at).wait()
        to_right(step, at).wait_send()
        to_left(step, at).wait_send()
        on_right(step, at).wait_send()
        on_left(step, at).wait_send()

    each(fan_one)
    each(fan_two)
    each(fan_three)
    for copy in inner:
        copy.wait_recv()
    for copy in started:
        copy.wait_send()
    each(fan_last)

    for chunk in range(CHUNKS):

        @pl.when(z != chunk)
        def _():
            to_owner(chunk).wait_send()

    @pl.when(z < CHUNKS)
    def _():
        for step in range(1, NZ):
            back(step).wait_send()


def reduce_all(parts, latent):
    dma = pltpu.SemaphoreType.DMA
    return pl.pallas_call(
        reduce_kernel,
        out_shape=(
            jax.ShapeDtypeStruct((2, NX, CHUNKS, TAPS, 16, 128), BF16),
            jax.ShapeDtypeStruct((NZ, 2 * NX, 8, 256), BF16),
        ),
        in_specs=[pl.BlockSpec(memory_space=pltpu.VMEM)] * 2,
        out_specs=[pl.BlockSpec(memory_space=pltpu.VMEM)] * 2,
        scratch_shapes=[
            pltpu.VMEM((CHUNKS * TAPS, 256, 128), BF16),
            pltpu.VMEM((CHUNKS, TAPS, NY, NX, 16, 128), BF16),
            pltpu.VMEM((CHUNKS, 2, 4, 16, 128), BF16),
            pltpu.VMEM((CHUNKS, 2, 4, 16, 128), BF16),
            pltpu.VMEM((CHUNKS, TAPS, 4, 16, 128), BF16),
            pltpu.VMEM((CHUNKS, TAPS, 4, 16, 128), BF16),
            pltpu.VMEM((CHUNKS, TAPS, 4, 16, 128), F32),
            pltpu.VMEM((CHUNKS, 2, 16, 128), F32),
            pltpu.VMEM((CHUNKS, 2, 16, 128), F32),
            pltpu.VMEM((CHUNKS, TAPS, 16, 128), F32),
            pltpu.VMEM((CHUNKS, TAPS, 16, 128), F32),
            pltpu.VMEM((NZ, TAPS, 16, 128), F32),
            pltpu.VMEM((NZ, TAPS, 16, 128), F32),
            pltpu.VMEM((NZ, TAPS, 16, 128), BF16),
            pltpu.VMEM((NX, NZ, TAPS, 16, 128), BF16),
            pltpu.VMEM((NZ, 2 * NX, 8, 256), BF16),
            dma((2, CHUNKS)),
            dma((2, CHUNKS, 4)),
            dma((2, CHUNKS, 4)),
            dma((2, NZ)),
            dma((2, NZ)),
            dma((2, 4, NZ)),
            dma((2, 4, NZ)),
            dma((2, 2, NZ)),
        ],
        compiler_params=pltpu.CompilerParams(collective_id=1, has_side_effects=True),
        cost_estimate=pl.CostEstimate(flops=20_000_000, bytes_accessed=6_000_000, transcendentals=0),
    )(parts, latent)


def finish_kernel(total, weight_grad, small):
    for core in range(2):
        lanes = pl.ds(core * 128, 128)
        for x in range(NX):
            rows = pl.ds(x * 16, 16)
            for tap in range(27):
                weight_grad[tap, rows, lanes] = total[core, x, tap // TAPS, tap % TAPS].astype(F32)
        sums = total[core, 0, 6, 3].astype(F32)
        small[:, lanes] = sums[0:8] + pltpu.roll(sums[0:8], 6, 0)


def finish(total):
    return pl.pallas_call(
        finish_kernel,
        out_shape=(jax.ShapeDtypeStruct((27, 64, 256), F32), jax.ShapeDtypeStruct((8, 256), F32)),
        in_specs=[pl.BlockSpec(memory_space=pltpu.VMEM)],
        out_specs=[pl.BlockSpec(memory_space=pltpu.VMEM)] * 2,
    )(total)


def on_device(frames, norm_gain, conv_weight, conv_bias, latent_grad):
    early = shifted(frames[2:], "tm", 1)
    below = shifted(jnp.concatenate([early[:, 0], frames[:, 0]], axis=0), "rows", -1)
    grad_rows = lax.all_to_all(latent_grad, "rows", split_axis=1, concat_axis=2, tiled=True)
    grad_rows = grad_rows.reshape(512, 256)
    grad = jnp.concatenate([grad_rows, shifted(grad_rows[:256], "tm", -1)], axis=0)
    grad_above = shifted(grad, "rows", 1)
    latent_rows, frames_grad, parts = section(
        frames, early, below, norm_gain.reshape(1, 256), conv_weight.reshape(3, 9, 256, 256),
        conv_bias.reshape(1, 256), grad, grad_above,
    )
    blocks = latent_rows.reshape(4, 64, 2, 256).transpose(1, 0, 2, 3).reshape(NZ, 2 * NX, 8, 256)
    total, latent_blocks = reduce_all(parts, blocks)
    latent = latent_blocks.reshape(64, 4, 2, 256).transpose(1, 0, 2, 3)
    weight_grad, small = finish(total)
    own = lax.dynamic_slice_in_dim(small, lax.axis_index("tm") * 64, 64, axis=1)
    return latent, frames_grad, weight_grad.reshape(3, 3, 3, 64, 256), own[0], own[1]


def solution(mesh):
    placed = (P("tm", "rows", None, None), P(), P(), P(), P("tm", None, "rows", None))
    return jax.shard_map(
        on_device,
        mesh=mesh,
        in_specs=placed,
        out_specs=(
            P("tm", None, "rows", None),
            P("tm", "rows", None, None),
            P(None, None, None, "tm", None),
            P("tm"),
            P("tm"),
        ),
        check_vma=False,
    )
```

```python
import jax
import jax.numpy as jnp
from jax import lax
from jax.experimental import pallas as pl
from jax.experimental.pallas import tpu as pltpu
from jax.sharding import PartitionSpec as P

F32 = jnp.float32
BF16 = jnp.bfloat16
MESH = pl.DeviceIdType.MESH
EPS = 1e-06
NX, NZ, NY = 4, 8, 4
CHUNKS, TAPS = 7, 4


def dot_nt(left, right):
    return lax.dot_general(left, right, (((1,), (1,)), ((), ())), preferred_element_type=F32)


def dot_nn(left, right):
    return lax.dot_general(left, right, (((1,), (0,)), ((), ())), preferred_element_type=F32)


def inverse_rms(signal):
    return lax.rsqrt(jnp.mean(signal * signal, axis=-1, keepdims=True) + EPS)


def section_kernel(
    frames, early, below, gain, weight, bias, grad, grad_above,
    latent, frames_grad, parts,
    columns, turned, grad_next, spread, tile, gain_sum,
):
    gain_row = gain[...]
    row_at = lax.broadcasted_iota(jnp.int32, (128, 256), 0)

    def hidden_tile(source, at, row, keep):
        for piece in range(4):
            rows = pl.ds(piece * 64, 64)
            signal = source[rows, :].astype(F32)
            normed = signal * inverse_rms(signal) * gain_row
            hidden = normed / (1.0 + jnp.exp(-normed))
            tile[row, 0, rows, :] = hidden[:, :128]
            tile[row, 1, rows, :] = hidden[:, 128:]
        even = jnp.concatenate([tile[row, half, pl.ds(0, 128, stride=2), :] for half in range(2)], axis=1)
        odd = jnp.concatenate([tile[row, half, pl.ds(1, 128, stride=2), :] for half in range(2)], axis=1)
        after = jnp.where(row_at == 127, 0.0, pltpu.roll(even, 127, 0))
        where = pl.ds(pl.multiple_of(at * 128, 128), 128)
        columns[where, pl.ds(row * 768, 256)] = even.astype(BF16)
        columns[where, pl.ds(row * 768 + 256, 256)] = odd.astype(BF16)
        columns[where, pl.ds(row * 768 + 512, 256)] = after.astype(BF16)
        if keep:
            lanes = pl.ds(pl.multiple_of((at - 2) * 128, 128), 128)
            turned[2 * row, :, lanes] = even.T.astype(BF16)
            turned[2 * row + 1, :, lanes] = odd.T.astype(BF16)

    @pl.loop(0, 2)
    def _(at):
        hidden_tile(early.at[at, 0], at, 0, False)
        hidden_tile(early.at[at, 1], at, 1, False)

    @pl.loop(2, 6)
    def _(at):
        hidden_tile(frames.at[at - 2, 0], at, 0, True)
        hidden_tile(frames.at[at - 2, 1], at, 1, True)

    @pl.loop(0, 6)
    def _(at):
        hidden_tile(below.at[at], at, 2, False)
        where = pl.ds(pl.multiple_of(at * 128, 128), 128)
        for which, source in enumerate((grad, grad_above)):
            moved = pltpu.roll(source[where, :].astype(F32), 1, 0)
            grad_next[which, where, :] = jnp.where(row_at == 0, 0.0, moved).astype(BF16)

    spread[0] = jnp.broadcast_to(bias[...], (512, 256))

    @pl.loop(0, 3)
    def _(tap):
        where = pl.ds(pl.multiple_of(tap * 128, 128), 512)
        spread[0] += dot_nn(columns[where, :], weight[tap].reshape(2304, 256))

    latent[...] = spread[0].astype(BF16)
    spread[...] = jnp.zeros_like(spread)
    gain_sum[...] = jnp.zeros_like(gain_sum)

    @pl.loop(0, 3)
    def _(tap):
        where = pl.ds(pl.multiple_of((2 - tap) * 128, 128), 512)
        here, here_next = grad[where, :], grad_next[0, where, :]
        above, above_next = grad_above[where, :], grad_next[1, where, :]
        spread[0] += dot_nt(here, weight[tap, 0]) + dot_nt(here_next, weight[tap, 2])
        spread[0] += dot_nt(above, weight[tap, 6]) + dot_nt(above_next, weight[tap, 8])
        spread[1] += dot_nt(here, weight[tap, 1]) + dot_nt(above, weight[tap, 7])
        spread[2] += dot_nt(here, weight[tap, 3]) + dot_nt(here_next, weight[tap, 5])
        spread[3] += dot_nt(here, weight[tap, 4])
        for spot in range(9):
            tap_r, tap_c = spot // 3, spot % 3
            left = turned[2 * (tap_r % 2) + tap_c % 2]
            if tap_r == 2:
                right = above_next if tap_c == 2 else above
            else:
                right = here_next if tap_c == 2 else here
            block = dot_nn(left, right).astype(BF16)
            parts[0, tap * 9 + spot] = block[:, :128]
            parts[1, tap * 9 + spot] = block[:, 128:]

    @pl.loop(0, 4)
    def _(at):
        where = pl.ds(pl.multiple_of(at * 128, 128), 128)
        for row in range(2):
            for half in range(2):
                lanes = pl.ds(half * 128, 128)
                tile[row, half, pl.ds(0, 128, stride=2), :] = spread[2 * row, where, lanes]
                tile[row, half, pl.ds(1, 128, stride=2), :] = spread[2 * row + 1, where, lanes]
            for piece in range(4):
                rows = pl.ds(piece * 64, 64)
                signal = frames[at, row, rows, :].astype(F32)
                inv = inverse_rms(signal)
                unit = signal * inv
                normed = unit * gain_row
                sigma = 1.0 / (1.0 + jnp.exp(-normed))
                arrived = jnp.concatenate([tile[row, half, rows, :] for half in range(2)], axis=1)
                normed_grad = arrived * sigma * (1.0 + normed * (1.0 - sigma))
                gain_sum[...] += jnp.sum((normed_grad * unit).reshape(8, 8, 256), axis=0)
                unit_grad = normed_grad * gain_row
                mean = jnp.mean(unit_grad * unit, axis=-1, keepdims=True)
                frames_grad[at, row, rows, :] = (inv * (unit_grad - unit * mean)).astype(BF16)

    gain_local = jnp.sum(gain_sum[...], axis=0, keepdims=True)
    bias_local = jnp.sum(grad[pl.ds(0, 512), :].astype(F32), axis=0, keepdims=True)
    spot = lax.broadcasted_iota(jnp.int32, (256, 256), 0) % 64
    gain_rest = gain_local - gain_local.astype(BF16).astype(F32)
    bias_rest = bias_local - bias_local.astype(BF16).astype(F32)
    small = jnp.where(spot == 0, gain_local, jnp.where(spot == 1, bias_local, 0.0))
    small = jnp.where(spot == 2, gain_rest, jnp.where(spot == 3, bias_rest, small)).astype(BF16)
    parts[0, 27] = small[:, :128]
    parts[1, 27] = small[:, 128:]


def section(frames, early, below, gain, weight, bias, grad, grad_above):
    return pl.pallas_call(
        section_kernel,
        out_shape=(
            jax.ShapeDtypeStruct((512, 256), BF16),
            jax.ShapeDtypeStruct((4, 2, 256, 256), BF16),
            jax.ShapeDtypeStruct((2, 28, 256, 128), BF16),
        ),
        in_specs=[pl.BlockSpec(memory_space=pltpu.VMEM)] * 8,
        out_specs=[pl.BlockSpec(memory_space=pltpu.VMEM)] * 3,
        scratch_shapes=[
            pltpu.VMEM((768, 2304), BF16),
            pltpu.VMEM((4, 256, 512), BF16),
            pltpu.VMEM((2, 768, 256), BF16),
            pltpu.VMEM((4, 512, 256), F32),
            pltpu.VMEM((3, 2, 256, 128), F32),
            pltpu.VMEM((8, 256), F32),
        ],
        cost_estimate=pl.CostEstimate(flops=5_500_000_000, bytes_accessed=12_000_000, transcendentals=2_000_000),
    )(frames, early, below, gain, weight, bias, grad, grad_above)


def reduce_kernel(
    parts, latent, result, latent_out, other, mine, first_plus, first_minus, second_plus, second_minus,
    mid, first_plus2, first_minus2, second_plus2, second_minus2,
    low, arrive, total, block, latent_mid,
    core_sem, ring_sem, ring2_sem, z_sem, zback_sem, x_sem, pair_sem, lat_sem,
):
    rows_at = lax.axis_index("rows")
    y = lax.axis_index("tm")
    core, x, z = rows_at % 2, (rows_at // 2) % NX, rows_at // (2 * NX)
    slab = rows_at % (2 * NX)

    def row_of(z_at, x_at, core_at):
        return z_at * (2 * NX) + x_at * 2 + core_at

    sibling = (row_of(z, x, 1 - core), y)

    def along(axis, step):
        if axis == "y":
            return (rows_at, (y + step) % NY)
        if axis == "x":
            return (row_of(z, (x + step) % NX, core), y)
        if axis == "slab":
            return (z * (2 * NX) + (slab + step) % (2 * NX), y)
        return (row_of((z + step) % NZ, x, core), y)

    barrier = pltpu.get_barrier_semaphore()
    friends = [along("slab", step) for step in range(1, 2 * NX)]
    friends += [along("y", 1), along("y", 3)]
    friends += [along("z", step) for step in range(1, NZ)]
    for friend in friends:
        pl.semaphore_signal(barrier, inc=1, device_id=friend, device_id_type=MESH)
    pl.semaphore_wait(barrier, len(friends))

    def copy_to(source, target, sems, at, device):
        return pltpu.make_async_remote_copy(
            src_ref=source, dst_ref=target, send_sem=sems.at[(0, *at)], recv_sem=sems.at[(1, *at)],
            device_id=device, device_id_type=MESH,
        )

    def send(*args):
        copy = copy_to(*args)
        copy.start()
        return copy

    pair = []
    for chunk in range(CHUNKS):
        spots = pl.ds(chunk * TAPS, TAPS)
        pair.append(send(parts.at[1 - core, spots], other.at[spots], core_sem, (chunk,), sibling))
    outer = [
        send(latent.at[(z + step) % NZ], latent_mid.at[z], lat_sem, (0, step), along("z", step))
        for step in range(1, NZ)
    ]
    latent_mid[z] = latent[z]
    started = pair + outer

    def axes_of(chunk):
        return ("y", "x") if chunk % 2 == 0 else ("x", "y")

    def here(axis, step):
        return (y + step) % NY if axis == "y" else (x + step) % NX

    def piece(ref, chunk, stage, at, taps):
        if stage == 0 and axes_of(chunk)[0] == "x":
            return ref.at[chunk, taps, slice(None), at]
        return ref.at[chunk, taps, at]

    FIRST, LAST, ALL = pl.ds(0, 2), pl.ds(2, 2), pl.ds(0, 4)
    banks = (
        (mine, first_plus, first_minus, second_plus, second_minus, ring_sem, BF16),
        (mid, first_plus2, first_minus2, second_plus2, second_minus2, ring2_sem, F32),
    )

    def ring_open(chunk, stage):
        source, plus, minus, _, _, sems, _ = banks[stage]
        axis = axes_of(chunk)[stage]
        far = here(axis, 2)
        return [
            send(piece(source, chunk, stage, far, FIRST), plus.at[chunk], sems, (chunk, 0), along(axis, 1)),
            send(piece(source, chunk, stage, far, LAST), minus.at[chunk], sems, (chunk, 1), along(axis, 3)),
        ]

    def ring_next(chunk, stage, opened):
        source, plus, minus, plus_in, minus_in, sems, kind = banks[stage]
        axis = axes_of(chunk)[stage]
        opened[0].wait_recv()
        ahead = piece(source, chunk, stage, here(axis, 1), FIRST)
        ahead[...] = (ahead[...].astype(F32) + plus[chunk].astype(F32)).astype(kind)
        one = send(piece(source, chunk, stage, here(axis, 1), ALL), plus_in.at[chunk], sems, (chunk, 2), along(axis, 1))
        opened[1].wait_recv()
        behind = piece(source, chunk, stage, here(axis, 3), LAST)
        behind[...] = (behind[...].astype(F32) + minus[chunk].astype(F32)).astype(kind)
        two = send(piece(source, chunk, stage, here(axis, 3), ALL), minus_in.at[chunk], sems, (chunk, 3), along(axis, 3))
        return [one, two]

    def ring_close(chunk, stage, sent):
        source, _, _, plus_in, minus_in, _, _ = banks[stage]
        axis = axes_of(chunk)[stage]
        sent[0].wait_recv()
        sent[1].wait_recv()
        own = piece(source, chunk, stage, here(axis, 0), ALL)[...].astype(F32)
        (mid, low)[stage][chunk] = own + plus_in[chunk].astype(F32) + minus_in[chunk].astype(F32)

    def to_owner(chunk):
        step = (chunk - z + NZ) % NZ
        return pltpu.make_async_remote_copy(
            src_ref=low.at[chunk], dst_ref=arrive.at[step], send_sem=z_sem.at[0, chunk], recv_sem=z_sem.at[1, step],
            device_id=(row_of(chunk, x, core), y), device_id_type=MESH,
        )

    opened, sent, opened2, sent2 = {}, {}, {}, {}
    for chunk in range(CHUNKS):
        pair[chunk].wait_recv()
        spots = pl.ds(chunk * TAPS, TAPS)
        summed = parts[core, spots].astype(F32) + other[spots].astype(F32)
        mine[chunk] = summed.astype(BF16).reshape(TAPS, NY, NX, 16, 128)
        opened[chunk] = ring_open(chunk, 0)
    for chunk in range(CHUNKS):
        sent[chunk] = ring_next(chunk, 0, opened[chunk])
    for copy in outer:
        copy.wait_recv()
    inner = [
        send(latent_mid.at[:, (slab + step) % (2 * NX)], latent_out.at[:, slab], lat_sem, (1, step), along("slab", step))
        for step in range(1, 2 * NX)
    ]
    latent_out[:, slab] = latent_mid[:, slab]
    for chunk in range(CHUNKS):
        ring_close(chunk, 0, sent[chunk])
        opened2[chunk] = ring_open(chunk, 1)
    for chunk in range(CHUNKS):
        sent2[chunk] = ring_next(chunk, 1, opened2[chunk])
    for chunk in range(CHUNKS):
        ring_close(chunk, 1, sent2[chunk])

        @pl.when(z != chunk)
        def _():
            to_owner(chunk).start()

    started += inner
    for table in (opened, sent, opened2, sent2):
        for chunk in range(CHUNKS):
            started += table[chunk]

    def back(step):
        return copy_to(total.at[z], total.at[z], zback_sem, (step,), along("z", step))

    @pl.when(z < CHUNKS)
    def _():
        summed = low[z]
        for step in range(1, NZ):
            pltpu.make_async_remote_copy(
                src_ref=low.at[0], dst_ref=arrive.at[step], send_sem=z_sem.at[0, 0], recv_sem=z_sem.at[1, step],
                device_id=sibling, device_id_type=MESH,
            ).wait_recv()
            summed += arrive[step]
        total[z] = summed.astype(BF16)
        for step in range(1, NZ):
            back(step).start()

    right, left, across = (x + 1) % NX, (x + 3) % NX, (x + 2) % NX
    order = (0, 1, 7, 2, 6, 3, 5, 4)

    def to_right(step, at):
        return copy_to(total.at[at], block.at[x, at], x_sem, (0, step), along("x", 1))

    def to_left(step, at):
        return copy_to(total.at[at], block.at[x, at], x_sem, (1, step), along("x", 3))

    def on_right(step, at):
        half = block.at[left, at, FIRST]
        return copy_to(half, half, x_sem, (2, step), along("x", 1))

    def on_left(step, at):
        half = block.at[right, at, LAST]
        return copy_to(half, half, x_sem, (3, step), along("x", 3))

    def across_core(which, step, at):
        source = total.at[at] if which == 0 else block.at[(left, right, across)[which - 1], at]
        where = (x, left, right, across)[which]
        return copy_to(source, result.at[core, where, at], pair_sem, (which, step), sibling)

    def each(body):
        for step in order:
            at = (z - step + NZ) % NZ

            @pl.when(at < CHUNKS)
            def _():
                body(step, at)

    def fan_one(step, at):
        if step:
            back(step).wait_recv()
        to_right(step, at).start()
        to_left(step, at).start()
        across_core(0, step, at).start()
        result[core, x, at] = total[at]

    def fan_two(step, at):
        to_right(step, at).wait_recv()
        on_right(step, at).start()
        across_core(1, step, at).start()
        result[core, left, at] = block[left, at]
        to_left(step, at).wait_recv()
        on_left(step, at).start()
        across_core(2, step, at).start()
        result[core, right, at] = block[right, at]

    def fan_three(step, at):
        on_right(step, at).wait_recv()
        on_left(step, at).wait_recv()
        across_core(3, step, at).start()
        result[core, across, at] = block[across, at]

    def fan_last(step, at):
        for which in range(4):
            across_core(which, step, at).wait()
        to_right(step, at).wait_send()
        to_left(step, at).wait_send()
        on_right(step, at).wait_send()
        on_left(step, at).wait_send()

    each(fan_one)
    each(fan_two)
    each(fan_three)
    for copy in inner:
        copy.wait_recv()
    for copy in started:
        copy.wait_send()
    each(fan_last)

    for chunk in range(CHUNKS):

        @pl.when(z != chunk)
        def _():
            to_owner(chunk).wait_send()

    @pl.when(z < CHUNKS)
    def _():
        for step in range(1, NZ):
            back(step).wait_send()


def reduce_all(parts, latent):
    dma = pltpu.SemaphoreType.DMA
    return pl.pallas_call(
        reduce_kernel,
        out_shape=(
            jax.ShapeDtypeStruct((2, NX, CHUNKS, TAPS, 16, 128), BF16),
            jax.ShapeDtypeStruct((NZ, 2 * NX, 8, 256), BF16),
        ),
        in_specs=[pl.BlockSpec(memory_space=pltpu.VMEM)] * 2,
        out_specs=[pl.BlockSpec(memory_space=pltpu.VMEM)] * 2,
        scratch_shapes=[
            pltpu.VMEM((CHUNKS * TAPS, 256, 128), BF16),
            pltpu.VMEM((CHUNKS, TAPS, NY, NX, 16, 128), BF16),
            pltpu.VMEM((CHUNKS, 2, 4, 16, 128), BF16),
            pltpu.VMEM((CHUNKS, 2, 4, 16, 128), BF16),
            pltpu.VMEM((CHUNKS, TAPS, 4, 16, 128), BF16),
            pltpu.VMEM((CHUNKS, TAPS, 4, 16, 128), BF16),
            pltpu.VMEM((CHUNKS, TAPS, 4, 16, 128), F32),
            pltpu.VMEM((CHUNKS, 2, 16, 128), F32),
            pltpu.VMEM((CHUNKS, 2, 16, 128), F32),
            pltpu.VMEM((CHUNKS, TAPS, 16, 128), F32),
            pltpu.VMEM((CHUNKS, TAPS, 16, 128), F32),
            pltpu.VMEM((NZ, TAPS, 16, 128), F32),
            pltpu.VMEM((NZ, TAPS, 16, 128), F32),
            pltpu.VMEM((NZ, TAPS, 16, 128), BF16),
            pltpu.VMEM((NX, NZ, TAPS, 16, 128), BF16),
            pltpu.VMEM((NZ, 2 * NX, 8, 256), BF16),
            dma((2, CHUNKS)),
            dma((2, CHUNKS, 4)),
            dma((2, CHUNKS, 4)),
            dma((2, NZ)),
            dma((2, NZ)),
            dma((2, 4, NZ)),
            dma((2, 4, NZ)),
            dma((2, 2, NZ)),
        ],
        compiler_params=pltpu.CompilerParams(collective_id=1, has_side_effects=True),
        cost_estimate=pl.CostEstimate(flops=20_000_000, bytes_accessed=6_000_000, transcendentals=0),
    )(parts, latent)


def finish_kernel(total, weight_grad, small):
    for core in range(2):
        lanes = pl.ds(core * 128, 128)
        for x in range(NX):
            rows = pl.ds(x * 16, 16)
            for tap in range(27):
                weight_grad[tap, rows, lanes] = total[core, x, tap // TAPS, tap % TAPS].astype(F32)
        sums = total[core, 0, 6, 3].astype(F32)
        small[:, lanes] = sums[0:8] + pltpu.roll(sums[0:8], 6, 0)


def finish(total):
    return pl.pallas_call(
        finish_kernel,
        out_shape=(jax.ShapeDtypeStruct((27, 64, 256), F32), jax.ShapeDtypeStruct((8, 256), F32)),
        in_specs=[pl.BlockSpec(memory_space=pltpu.VMEM)],
        out_specs=[pl.BlockSpec(memory_space=pltpu.VMEM)] * 2,
    )(total)


def gather_kernel(
    blocks, frames, grad, grad_above, early, below,
    middle, landed, flat, woven, z_sem, slab_sem, near_sem,
):
    rows_at = lax.axis_index("rows")
    y = lax.axis_index("tm")
    slab, z = rows_at % (2 * NX), rows_at // (2 * NX)
    count = NZ * 2 * NX

    def along(axis, step):
        if axis == "y":
            return (rows_at, (y + step + NY) % NY)
        if axis == "slab":
            return (z * (2 * NX) + (slab + step) % (2 * NX), y)
        if axis == "row":
            return ((rows_at + step + count) % count, y)
        return (((z + step) % NZ) * (2 * NX) + slab, y)

    barrier = pltpu.get_barrier_semaphore()
    friends = [along("z", step) for step in range(1, NZ)] + [along("slab", step) for step in range(1, 2 * NX)]
    friends += [along("y", 1), along("y", -1), along("row", 1), along("row", -1)]
    for friend in friends:
        pl.semaphore_signal(barrier, inc=1, device_id=friend, device_id_type=MESH)
    pl.semaphore_wait(barrier, len(friends))

    def copy_to(source, target, sems, at, device):
        return pltpu.make_async_remote_copy(
            src_ref=source, dst_ref=target, send_sem=sems.at[0, at], recv_sem=sems.at[1, at],
            device_id=device, device_id_type=MESH,
        )

    outer = [
        copy_to(blocks.at[(z + step) % NZ], middle.at[z], z_sem, step, along("z", step)) for step in range(1, NZ)
    ]
    inner = [
        copy_to(middle.at[:, (slab + step) % (2 * NX)], landed.at[:, slab], slab_sem, step, along("slab", step))
        for step in range(1, 2 * NX)
    ]
    early_on = copy_to(frames.at[pl.ds(2, 2)], early, near_sem, 0, along("y", 1))
    below_own = copy_to(frames.at[:, 0], below.at[pl.ds(2, 4)], near_sem, 1, along("row", -1))
    below_early = copy_to(early.at[:, 0], below.at[pl.ds(0, 2)], near_sem, 2, along("row", -1))
    ahead, own, late = pl.ds(0, 256), pl.ds(0, 512), pl.ds(512, 256)
    grad_late = copy_to(grad.at[ahead], grad.at[late], near_sem, 3, along("y", -1))
    above_own = copy_to(grad.at[own], grad_above.at[own], near_sem, 4, along("row", 1))
    above_late = copy_to(grad.at[late], grad_above.at[late], near_sem, 5, along("row", 1))
    first_time, last_time, first_row, last_row = y == 0, y == NY - 1, rows_at == 0, rows_at == count - 1

    for copy in outer:
        copy.start()

    @pl.when(jnp.logical_not(last_time))
    def _():
        early_on.start()

    @pl.when(jnp.logical_not(first_row))
    def _():
        below_own.start()

    middle[z] = blocks[z]

    @pl.when(first_time)
    def _():
        early[...] = jnp.zeros_like(early)

    @pl.when(last_row)
    def _():
        below[...] = jnp.zeros_like(below)

    @pl.when(first_row)
    def _():
        grad_above[...] = jnp.zeros_like(grad_above)

    @pl.when(last_time)
    def _():
        grad[late, :] = jnp.zeros((256, 256), BF16)

    for copy in outer:
        copy.wait_recv()
    for copy in inner:
        copy.start()
    landed[:, slab] = middle[:, slab]
    for copy in inner:
        copy.wait_recv()

    for half in range(2):
        lanes = pl.ds(half * 128, 128)
        flat[half] = landed[:, :, :, lanes].astype(F32).reshape(512, 128)
    for frame in range(4):
        for half in range(2):
            for side in range(2):
                woven[frame, half, pl.ds(side, 64, stride=2), :] = flat[half, pl.ds(2 * frame + side, 64, stride=8), :]
            grad[pl.ds(frame * 128, 128), pl.ds(half * 128, 128)] = woven[frame, half].astype(BF16)

    @pl.when(jnp.logical_not(first_time))
    def _():
        grad_late.start()

    @pl.when(jnp.logical_not(last_row))
    def _():
        above_own.start()

    @pl.when(jnp.logical_not(first_time))
    def _():
        early_on.wait_recv()

    @pl.when(jnp.logical_not(first_row))
    def _():
        below_early.start()

    @pl.when(jnp.logical_not(last_time))
    def _():
        grad_late.wait_recv()

    @pl.when(jnp.logical_not(last_row))
    def _():
        above_late.start()

    @pl.when(jnp.logical_not(first_row))
    def _():
        above_own.wait_recv()
        above_late.wait_recv()
        below_own.wait_send()
        below_early.wait_send()

    @pl.when(jnp.logical_not(last_row))
    def _():
        below_own.wait_recv()
        below_early.wait_recv()
        above_own.wait_send()
        above_late.wait_send()

    @pl.when(jnp.logical_not(first_time))
    def _():
        grad_late.wait_send()

    @pl.when(jnp.logical_not(last_time))
    def _():
        early_on.wait_send()

    for copy in outer + inner:
        copy.wait_send()


def gather(blocks, frames):
    dma = pltpu.SemaphoreType.DMA
    return pl.pallas_call(
        gather_kernel,
        out_shape=(
            jax.ShapeDtypeStruct((768, 256), BF16),
            jax.ShapeDtypeStruct((768, 256), BF16),
            jax.ShapeDtypeStruct((2, 2, 256, 256), BF16),
            jax.ShapeDtypeStruct((6, 256, 256), BF16),
        ),
        in_specs=[pl.BlockSpec(memory_space=pltpu.VMEM)] * 2,
        out_specs=[pl.BlockSpec(memory_space=pltpu.VMEM)] * 4,
        scratch_shapes=[
            pltpu.VMEM((NZ, 2 * NX, 8, 256), BF16),
            pltpu.VMEM((NZ, 2 * NX, 8, 256), BF16),
            pltpu.VMEM((2, 512, 128), F32),
            pltpu.VMEM((4, 2, 128, 128), F32),
            dma((2, NZ)),
            dma((2, 2 * NX)),
            dma((2, 6)),
        ],
        compiler_params=pltpu.CompilerParams(collective_id=2, has_side_effects=True),
        cost_estimate=pl.CostEstimate(flops=1_000_000, bytes_accessed=4_000_000, transcendentals=0),
    )(blocks, frames)


def on_device(frames, norm_gain, conv_weight, conv_bias, latent_grad):
    blocks = latent_grad.transpose(1, 0, 2, 3).reshape(NZ, 2 * NX, 8, 256)
    grad, grad_above, early, below = gather(blocks, frames)
    latent_rows, frames_grad, parts = section(
        frames, early, below, norm_gain.reshape(1, 256), conv_weight.reshape(3, 9, 256, 256),
        conv_bias.reshape(1, 256), grad, grad_above,
    )
    blocks = latent_rows.reshape(4, 64, 2, 256).transpose(1, 0, 2, 3).reshape(NZ, 2 * NX, 8, 256)
    total, latent_blocks = reduce_all(parts, blocks)
    latent = latent_blocks.reshape(64, 4, 2, 256).transpose(1, 0, 2, 3)
    weight_grad, small = finish(total)
    own = lax.dynamic_slice_in_dim(small, lax.axis_index("tm") * 64, 64, axis=1)
    return latent, frames_grad, weight_grad.reshape(3, 3, 3, 64, 256), own[0], own[1]


def solution(mesh):
    placed = (P("tm", "rows", None, None), P(), P(), P(), P("tm", None, "rows", None))
    return jax.shard_map(
        on_device,
        mesh=mesh,
        in_specs=placed,
        out_specs=(
            P("tm", None, "rows", None),
            P("tm", "rows", None, None),
            P(None, None, None, "tm", None),
            P("tm"),
            P("tm"),
        ),
        check_vma=False,
    )
```

```python
import jax
import jax.numpy as jnp
from jax import lax
from jax.experimental import pallas as pl
from jax.experimental.pallas import tpu as pltpu
from jax.sharding import PartitionSpec as P

F32 = jnp.float32
BF16 = jnp.bfloat16
MESH = pl.DeviceIdType.MESH
EPS = 1e-06
NX, NZ, NY = 4, 8, 4
CHUNKS, TAPS = 7, 4


def dot_nt(left, right):
    return lax.dot_general(left, right, (((1,), (1,)), ((), ())), preferred_element_type=F32)


def dot_nn(left, right):
    return lax.dot_general(left, right, (((1,), (0,)), ((), ())), preferred_element_type=F32)


def inverse_rms(signal):
    return lax.rsqrt(jnp.mean(signal * signal, axis=-1, keepdims=True) + EPS)


def whole_kernel(
    latent_grad, frames, gain, weight_far, bias,
    frames_grad, latent, result,
    weight, blocks, middle, landed, flat, woven, grad, grad_above, early, below,
    columns, turned, grad_next, spread, tile, gain_sum, parts,
    other, mine, first_plus, first_minus, second_plus, second_minus,
    mid, first_plus2, first_minus2, second_plus2, second_minus2,
    low, arrive, total, block, latent_in, latent_mid, latent_out,
    weight_sem, gz_sem, gs_sem, near_sem,
    core_sem, ring_sem, ring2_sem, z_sem, zback_sem, x_sem, pair_sem, lat_sem,
):
    rows_at = lax.axis_index("rows")
    y = lax.axis_index("tm")
    core, x, z = rows_at % 2, (rows_at // 2) % NX, rows_at // (2 * NX)
    slab = rows_at % (2 * NX)
    count = NZ * 2 * NX

    def row_of(z_at, x_at, core_at):
        return z_at * (2 * NX) + x_at * 2 + core_at

    sibling = (row_of(z, x, 1 - core), y)

    def along(axis, step):
        if axis == "y":
            return (rows_at, (y + step + NY) % NY)
        if axis == "x":
            return (row_of(z, (x + step) % NX, core), y)
        if axis == "slab":
            return (z * (2 * NX) + (slab + step) % (2 * NX), y)
        if axis == "row":
            return ((rows_at + step + count) % count, y)
        return (row_of((z + step) % NZ, x, core), y)

    weight_in = pltpu.make_async_copy(weight_far, weight, weight_sem.at[0])
    weight_in.start()

    barrier = pltpu.get_barrier_semaphore()
    friends = [along("z", step) for step in range(1, NZ)] + [along("slab", step) for step in range(1, 2 * NX)]
    friends += [along("y", 1), along("y", -1), along("row", 1), along("row", -1)]
    for friend in friends:
        pl.semaphore_signal(barrier, inc=1, device_id=friend, device_id_type=MESH)

    def unweave(target):
        for frame in range(4):
            for half in range(2):
                for side in range(2):
                    flat[half, pl.ds(2 * frame + side, 64, stride=8), :] = woven[frame, half, pl.ds(side, 64, stride=2), :]
        for half in range(2):
            target[:, :, :, pl.ds(half * 128, 128)] = flat[half].reshape(NZ, 2 * NX, 8, 128).astype(BF16)

    def weave(source, put):
        for half in range(2):
            flat[half] = source[:, :, :, pl.ds(half * 128, 128)].astype(F32).reshape(512, 128)
        for frame in range(4):
            for half in range(2):
                for side in range(2):
                    woven[frame, half, pl.ds(side, 64, stride=2), :] = flat[half, pl.ds(2 * frame + side, 64, stride=8), :]
                put(frame, half, woven[frame, half].astype(BF16))

    for frame in range(4):
        for half in range(2):
            woven[frame, half] = latent_grad[frame, :, pl.ds(half * 128, 128)].astype(F32)
    unweave(blocks)

    pl.semaphore_wait(barrier, len(friends))

    def copy_to(source, target, sems, at, device):
        return pltpu.make_async_remote_copy(
            src_ref=source, dst_ref=target, send_sem=sems.at[(0, *at)], recv_sem=sems.at[(1, *at)],
            device_id=device, device_id_type=MESH,
        )

    def send(*args):
        copy = copy_to(*args)
        copy.start()
        return copy

    ahead, own, late = pl.ds(0, 256), pl.ds(0, 512), pl.ds(512, 256)
    early_on = copy_to(frames.at[pl.ds(2, 2)], early, near_sem, (0,), along("y", 1))
    below_own = copy_to(frames.at[:, 0], below.at[pl.ds(2, 4)], near_sem, (1,), along("row", -1))
    below_early = copy_to(early.at[:, 0], below.at[pl.ds(0, 2)], near_sem, (2,), along("row", -1))
    grad_late = copy_to(grad.at[ahead], grad.at[late], near_sem, (3,), along("y", -1))
    above_own = copy_to(grad.at[own], grad_above.at[own], near_sem, (4,), along("row", 1))
    above_late = copy_to(grad.at[late], grad_above.at[late], near_sem, (5,), along("row", 1))
    has_past, has_future = y > 0, y < NY - 1
    has_above, has_below = rows_at > 0, rows_at < count - 1

    def only(condition, *actions):
        @pl.when(condition)
        def _():
            for action in actions:
                action()

    g_outer = [
        send(blocks.at[(z + step) % NZ], middle.at[z], gz_sem, (step,), along("z", step)) for step in range(1, NZ)
    ]
    only(has_future, early_on.start)
    only(has_above, below_own.start)
    middle[z] = blocks[z]

    @pl.when(jnp.logical_not(has_past))
    def _():
        early[...] = jnp.zeros_like(early)

    @pl.when(jnp.logical_not(has_below))
    def _():
        below[...] = jnp.zeros_like(below)

    @pl.when(jnp.logical_not(has_above))
    def _():
        grad_above[...] = jnp.zeros_like(grad_above)

    @pl.when(jnp.logical_not(has_future))
    def _():
        grad[late, :] = jnp.zeros((256, 256), BF16)

    gain_row = gain[...]
    row_at = lax.broadcasted_iota(jnp.int32, (128, 256), 0)

    def hidden_tile(source, at, row, keep):
        for piece_at in range(4):
            rows = pl.ds(piece_at * 64, 64)
            signal = source[rows, :].astype(F32)
            normed = signal * inverse_rms(signal) * gain_row
            hidden = normed / (1.0 + jnp.exp(-normed))
            tile[row, 0, rows, :] = hidden[:, :128]
            tile[row, 1, rows, :] = hidden[:, 128:]
        even = jnp.concatenate([tile[row, half, pl.ds(0, 128, stride=2), :] for half in range(2)], axis=1)
        odd = jnp.concatenate([tile[row, half, pl.ds(1, 128, stride=2), :] for half in range(2)], axis=1)
        after = jnp.where(row_at == 127, 0.0, pltpu.roll(even, 127, 0))
        where = pl.ds(pl.multiple_of(at * 128, 128), 128)
        columns[where, pl.ds(row * 768, 256)] = even.astype(BF16)
        columns[where, pl.ds(row * 768 + 256, 256)] = odd.astype(BF16)
        columns[where, pl.ds(row * 768 + 512, 256)] = after.astype(BF16)
        if keep:
            lanes = pl.ds(pl.multiple_of((at - 2) * 128, 128), 128)
            turned[2 * row, :, lanes] = even.T.astype(BF16)
            turned[2 * row + 1, :, lanes] = odd.T.astype(BF16)

    @pl.loop(2, 6)
    def _(at):
        hidden_tile(frames.at[at - 2, 0], at, 0, True)
        hidden_tile(frames.at[at - 2, 1], at, 1, True)

    for copy in g_outer:
        copy.wait_recv()
    g_inner = [
        send(middle.at[:, (slab + step) % (2 * NX)], landed.at[:, slab], gs_sem, (step,), along("slab", step))
        for step in range(1, 2 * NX)
    ]
    landed[:, slab] = middle[:, slab]
    spread[...] = jnp.zeros_like(spread)
    gain_sum[...] = jnp.zeros_like(gain_sum)
    weight_in.wait()
    for copy in g_inner:
        copy.wait_recv()

    def put_grad(frame, half, value):
        grad[pl.ds(frame * 128, 128), pl.ds(half * 128, 128)] = value

    weave(landed, put_grad)
    only(has_past, grad_late.start)
    only(has_below, above_own.start)

    def step_on(which, source, frames_at):
        for at in frames_at:
            where = pl.ds(at * 128, 128)
            moved = pltpu.roll(source[where, :].astype(F32), 1, 0)
            grad_next[which, where, :] = jnp.where(row_at == 0, 0.0, moved).astype(BF16)

    def weight_taps(chunk):
        for tap in range(chunk * TAPS, min(27, chunk * TAPS + TAPS)):
            tap_t, tap_r, tap_c = tap // 9, tap // 3 % 3, tap % 3
            where = pl.ds((2 - tap_t) * 128, 512)
            left = turned[2 * (tap_r % 2) + tap_c % 2]
            if tap_c == 2:
                right = grad_next[1 if tap_r == 2 else 0, where, :]
            else:
                right = (grad_above if tap_r == 2 else grad)[where, :]
            product = dot_nn(left, right).astype(BF16)
            parts[0, tap] = product[:, :128]
            parts[1, tap] = product[:, 128:]

    pair = {}

    def pair_send(chunk):
        spots = pl.ds(chunk * TAPS, TAPS)
        pair[chunk] = send(parts.at[1 - core, spots], other.at[spots], core_sem, (chunk,), sibling)

    def axes_of(chunk):
        return ("y", "x") if chunk % 2 == 0 else ("x", "y")

    def here(axis, step):
        return (y + step) % NY if axis == "y" else (x + step) % NX

    def piece(ref, chunk, stage, at, taps):
        if stage == 0 and axes_of(chunk)[0] == "x":
            return ref.at[chunk, taps, slice(None), at]
        return ref.at[chunk, taps, at]

    FIRST, LAST, ALL = pl.ds(0, 2), pl.ds(2, 2), pl.ds(0, 4)
    banks = (
        (mine, first_plus, first_minus, second_plus, second_minus, ring_sem, BF16),
        (mid, first_plus2, first_minus2, second_plus2, second_minus2, ring2_sem, F32),
    )

    def ring_open(chunk, stage):
        source, plus, minus, _, _, sems, _ = banks[stage]
        axis = axes_of(chunk)[stage]
        far = here(axis, 2)
        return [
            send(piece(source, chunk, stage, far, FIRST), plus.at[chunk], sems, (chunk, 0), along(axis, 1)),
            send(piece(source, chunk, stage, far, LAST), minus.at[chunk], sems, (chunk, 1), along(axis, 3)),
        ]

    def ring_next(chunk, stage, opened):
        source, plus, minus, plus_in, minus_in, sems, kind = banks[stage]
        axis = axes_of(chunk)[stage]
        opened[0].wait_recv()
        ahead = piece(source, chunk, stage, here(axis, 1), FIRST)
        ahead[...] = (ahead[...].astype(F32) + plus[chunk].astype(F32)).astype(kind)
        one = send(piece(source, chunk, stage, here(axis, 1), ALL), plus_in.at[chunk], sems, (chunk, 2), along(axis, 1))
        opened[1].wait_recv()
        behind = piece(source, chunk, stage, here(axis, 3), LAST)
        behind[...] = (behind[...].astype(F32) + minus[chunk].astype(F32)).astype(kind)
        two = send(piece(source, chunk, stage, here(axis, 3), ALL), minus_in.at[chunk], sems, (chunk, 3), along(axis, 3))
        return [one, two]

    def ring_close(chunk, stage, sent):
        source, _, _, plus_in, minus_in, _, _ = banks[stage]
        axis = axes_of(chunk)[stage]
        sent[0].wait_recv()
        sent[1].wait_recv()
        own = piece(source, chunk, stage, here(axis, 0), ALL)[...].astype(F32)
        (mid, low)[stage][chunk] = own + plus_in[chunk].astype(F32) + minus_in[chunk].astype(F32)

    def to_owner(chunk):
        step = (chunk - z + NZ) % NZ
        return pltpu.make_async_remote_copy(
            src_ref=low.at[chunk], dst_ref=arrive.at[step], send_sem=z_sem.at[0, chunk], recv_sem=z_sem.at[1, step],
            device_id=(row_of(chunk, x, core), y), device_id_type=MESH,
        )

    opened, sent, opened2, sent2 = {}, {}, {}, {}

    def pair_close(chunk):
        pair[chunk].wait_recv()
        spots = pl.ds(chunk * TAPS, TAPS)
        summed = parts[core, spots].astype(F32) + other[spots].astype(F32)
        mine[chunk] = summed.astype(BF16).reshape(TAPS, NY, NX, 16, 128)
        opened[chunk] = ring_open(chunk, 0)

    def next_one(*chunks):
        for chunk in chunks:
            sent[chunk] = ring_next(chunk, 0, opened[chunk])

    def close_one(*chunks):
        for chunk in chunks:
            ring_close(chunk, 0, sent[chunk])
            opened2[chunk] = ring_open(chunk, 1)

    def next_two(*chunks):
        for chunk in chunks:
            sent2[chunk] = ring_next(chunk, 1, opened2[chunk])

    def close_two(*chunks):
        for chunk in chunks:
            ring_close(chunk, 1, sent2[chunk])
            only(z != chunk, to_owner(chunk).start)

    step_on(0, grad, range(4))
    weight_taps(5)
    pair_send(5)
    only(has_future, grad_late.wait_recv)
    only(has_below, above_late.start)
    step_on(0, grad, (4, 5))
    weight_taps(0)
    pair_send(0)
    pair_close(5)
    only(has_above, above_own.wait_recv, above_late.wait_recv)
    step_on(1, grad_above, range(6))
    before = 0
    for chunk in (3, 1, 2, 4):
        weight_taps(chunk)
        pair_send(chunk)
        pair_close(before)
        before = chunk
    only(has_past, early_on.wait_recv)
    only(has_above, below_early.start)

    def back_taps(tap):
        where = pl.ds((2 - tap) * 128, 512)
        here_g, here_next = grad[where, :], grad_next[0, where, :]
        above, above_next = grad_above[where, :], grad_next[1, where, :]
        spread[0] += dot_nt(here_g, weight[tap, 0]) + dot_nt(here_next, weight[tap, 2])
        spread[0] += dot_nt(above, weight[tap, 6]) + dot_nt(above_next, weight[tap, 8])
        spread[1] += dot_nt(here_g, weight[tap, 1]) + dot_nt(above, weight[tap, 7])
        spread[2] += dot_nt(here_g, weight[tap, 3]) + dot_nt(here_next, weight[tap, 5])
        spread[3] += dot_nt(here_g, weight[tap, 4])

    def frame_back(first, last):
        @pl.loop(first, last)
        def _(at):
            where = pl.ds(pl.multiple_of(at * 128, 128), 128)
            for row in range(2):
                for half in range(2):
                    lanes = pl.ds(half * 128, 128)
                    tile[row, half, pl.ds(0, 128, stride=2), :] = spread[2 * row, where, lanes]
                    tile[row, half, pl.ds(1, 128, stride=2), :] = spread[2 * row + 1, where, lanes]
                for piece_at in range(4):
                    rows = pl.ds(piece_at * 64, 64)
                    signal = frames[at, row, rows, :].astype(F32)
                    inv = inverse_rms(signal)
                    unit = signal * inv
                    normed = unit * gain_row
                    sigma = 1.0 / (1.0 + jnp.exp(-normed))
                    arrived = jnp.concatenate([tile[row, half, rows, :] for half in range(2)], axis=1)
                    normed_grad = arrived * sigma * (1.0 + normed * (1.0 - sigma))
                    gain_sum[...] += jnp.sum((normed_grad * unit).reshape(8, 8, 256), axis=0)
                    unit_grad = normed_grad * gain_row
                    mean = jnp.mean(unit_grad * unit, axis=-1, keepdims=True)
                    frames_grad[at, row, rows, :] = (inv * (unit_grad - unit * mean)).astype(BF16)

    back_taps(0)
    pair_close(before)
    next_one(5, 0)
    back_taps(1)
    next_one(3, 1)
    back_taps(2)
    next_one(2, 4)
    frame_back(0, 2)
    close_one(5, 0)
    frame_back(2, 4)

    gain_local = jnp.sum(gain_sum[...], axis=0, keepdims=True)
    bias_local = jnp.sum(grad[pl.ds(0, 512), :].astype(F32), axis=0, keepdims=True)
    gain_rest = gain_local - gain_local.astype(BF16).astype(F32)
    bias_rest = bias_local - bias_local.astype(BF16).astype(F32)
    spot = lax.broadcasted_iota(jnp.int32, (256, 256), 0) % 64
    small = jnp.where(spot == 0, gain_local, jnp.where(spot == 1, bias_local, 0.0))
    small = jnp.where(spot == 2, gain_rest, jnp.where(spot == 3, bias_rest, small)).astype(BF16)
    parts[0, 27] = small[:, :128]
    parts[1, 27] = small[:, 128:]
    weight_taps(6)
    pair_send(6)
    close_one(3, 1)

    @pl.loop(0, 2)
    def _(at):
        hidden_tile(early.at[at, 0], at, 0, False)
        hidden_tile(early.at[at, 1], at, 1, False)

    pair_close(6)
    close_one(2, 4)
    next_two(5, 0)
    only(has_below, below_own.wait_recv, below_early.wait_recv)

    @pl.loop(0, 6)
    def _(at):
        hidden_tile(below.at[at], at, 2, False)

    next_one(6)
    next_two(3, 1)
    spread[0] = jnp.broadcast_to(bias[...], (512, 256))

    @pl.loop(0, 3)
    def _(tap):
        where = pl.ds(pl.multiple_of(tap * 128, 128), 512)
        spread[0] += dot_nn(columns[where, :], weight[tap].reshape(2304, 256))

    next_two(2, 4)
    close_one(6)
    close_two(5, 0, 3, 1)
    for frame in range(4):
        for half in range(2):
            woven[frame, half] = spread[0, pl.ds(frame * 128, 128), pl.ds(half * 128, 128)]
    unweave(latent_in)
    outer = [
        send(latent_in.at[(z + step) % NZ], latent_mid.at[z], lat_sem, (0, step), along("z", step))
        for step in range(1, NZ)
    ]
    latent_mid[z] = latent_in[z]
    next_two(6)
    close_two(2, 4, 6)
    started = list(pair.values()) + outer + g_outer + g_inner
    for table in (opened, sent, opened2, sent2):
        for chunk in range(CHUNKS):
            started += table[chunk]

    def back(step):
        return copy_to(total.at[z], total.at[z], zback_sem, (step,), along("z", step))

    @pl.when(z < CHUNKS)
    def _():
        summed = low[z]
        for step in range(1, NZ):
            pltpu.make_async_remote_copy(
                src_ref=low.at[0], dst_ref=arrive.at[step], send_sem=z_sem.at[0, 0], recv_sem=z_sem.at[1, step],
                device_id=sibling, device_id_type=MESH,
            ).wait_recv()
            summed += arrive[step]
        total[z] = summed.astype(BF16)
        for step in range(1, NZ):
            back(step).start()

    right, left, across = (x + 1) % NX, (x + 3) % NX, (x + 2) % NX
    order = (0, 1, 7, 2, 6, 3, 5, 4)

    def to_right(step, at):
        return copy_to(total.at[at], block.at[x, at], x_sem, (0, step), along("x", 1))

    def to_left(step, at):
        return copy_to(total.at[at], block.at[x, at], x_sem, (1, step), along("x", 3))

    def on_right(step, at):
        half = block.at[left, at, FIRST]
        return copy_to(half, half, x_sem, (2, step), along("x", 1))

    def on_left(step, at):
        half = block.at[right, at, LAST]
        return copy_to(half, half, x_sem, (3, step), along("x", 3))

    def across_core(which, step, at):
        source = total.at[at] if which == 0 else block.at[(left, right, across)[which - 1], at]
        where = (x, left, right, across)[which]
        return copy_to(source, result.at[core, where, at], pair_sem, (which, step), sibling)

    def each(body):
        for step in order:
            at = (z - step + NZ) % NZ

            @pl.when(at < CHUNKS)
            def _():
                body(step, at)

    def fan_one(step, at):
        if step:
            back(step).wait_recv()
        to_right(step, at).start()
        to_left(step, at).start()
        across_core(0, step, at).start()
        result[core, x, at] = total[at]

    def fan_two(step, at):
        to_right(step, at).wait_recv()
        on_right(step, at).start()
        across_core(1, step, at).start()
        result[core, left, at] = block[left, at]
        to_left(step, at).wait_recv()
        on_left(step, at).start()
        across_core(2, step, at).start()
        result[core, right, at] = block[right, at]

    def fan_three(step, at):
        on_right(step, at).wait_recv()
        on_left(step, at).wait_recv()
        across_core(3, step, at).start()
        result[core, across, at] = block[across, at]

    def fan_last(step, at):
        for which in range(4):
            across_core(which, step, at).wait()
        to_right(step, at).wait_send()
        to_left(step, at).wait_send()
        on_right(step, at).wait_send()
        on_left(step, at).wait_send()

    for copy in outer:
        copy.wait_recv()
    inner = [
        send(latent_mid.at[:, (slab + step) % (2 * NX)], latent_out.at[:, slab], lat_sem, (1, step), along("slab", step))
        for step in range(1, 2 * NX)
    ]
    latent_out[:, slab] = latent_mid[:, slab]
    each(fan_one)
    each(fan_two)
    for copy in inner:
        copy.wait_recv()

    def put_latent(frame, half, value):
        latent[frame, :, pl.ds(half * 128, 128)] = value

    weave(latent_out, put_latent)
    each(fan_three)
    for copy in started + inner:
        copy.wait_send()
    each(fan_last)
    only(has_future, early_on.wait_send)
    only(has_above, below_own.wait_send, below_early.wait_send)
    only(has_past, grad_late.wait_send)
    only(has_below, above_own.wait_send, above_late.wait_send)
    for chunk in range(CHUNKS):
        only(z != chunk, to_owner(chunk).wait_send)

    @pl.when(z < CHUNKS)
    def _():
        for step in range(1, NZ):
            back(step).wait_send()


def whole(latent_grad, frames, gain, weight, bias):
    dma, vmem = pltpu.SemaphoreType.DMA, pltpu.VMEM
    inside = pl.BlockSpec(memory_space=pltpu.VMEM)
    return pl.pallas_call(
        whole_kernel,
        out_shape=(
            jax.ShapeDtypeStruct((4, 2, 256, 256), BF16),
            jax.ShapeDtypeStruct((4, 128, 256), BF16),
            jax.ShapeDtypeStruct((2, NX, CHUNKS, TAPS, 16, 128), BF16),
        ),
        in_specs=[inside, inside, inside, pl.BlockSpec(memory_space=pl.ANY), inside],
        out_specs=[inside] * 3,
        scratch_shapes=[
            vmem((3, 9, 256, 256), BF16),
            vmem((NZ, 2 * NX, 8, 256), BF16),
            vmem((NZ, 2 * NX, 8, 256), BF16),
            vmem((NZ, 2 * NX, 8, 256), BF16),
            vmem((2, 512, 128), F32),
            vmem((4, 2, 128, 128), F32),
            vmem((768, 256), BF16),
            vmem((768, 256), BF16),
            vmem((2, 2, 256, 256), BF16),
            vmem((6, 256, 256), BF16),
            vmem((768, 2304), BF16),
            vmem((4, 256, 512), BF16),
            vmem((2, 768, 256), BF16),
            vmem((4, 512, 256), F32),
            vmem((3, 2, 256, 128), F32),
            vmem((8, 256), F32),
            vmem((2, 28, 256, 128), BF16),
            vmem((CHUNKS * TAPS, 256, 128), BF16),
            vmem((CHUNKS, TAPS, NY, NX, 16, 128), BF16),
            vmem((CHUNKS, 2, 4, 16, 128), BF16),
            vmem((CHUNKS, 2, 4, 16, 128), BF16),
            vmem((CHUNKS, TAPS, 4, 16, 128), BF16),
            vmem((CHUNKS, TAPS, 4, 16, 128), BF16),
            vmem((CHUNKS, TAPS, 4, 16, 128), F32),
            vmem((CHUNKS, 2, 16, 128), F32),
            vmem((CHUNKS, 2, 16, 128), F32),
            vmem((CHUNKS, TAPS, 16, 128), F32),
            vmem((CHUNKS, TAPS, 16, 128), F32),
            vmem((NZ, TAPS, 16, 128), F32),
            vmem((NZ, TAPS, 16, 128), F32),
            vmem((NZ, TAPS, 16, 128), BF16),
            vmem((NX, NZ, TAPS, 16, 128), BF16),
            vmem((NZ, 2 * NX, 8, 256), BF16),
            vmem((NZ, 2 * NX, 8, 256), BF16),
            vmem((NZ, 2 * NX, 8, 256), BF16),
            dma((1,)),
            dma((2, NZ)),
            dma((2, 2 * NX)),
            dma((2, 6)),
            dma((2, CHUNKS)),
            dma((2, CHUNKS, 4)),
            dma((2, CHUNKS, 4)),
            dma((2, NZ)),
            dma((2, NZ)),
            dma((2, 4, NZ)),
            dma((2, 4, NZ)),
            dma((2, 2, NZ)),
        ],
        compiler_params=pltpu.CompilerParams(collective_id=1, has_side_effects=True),
        cost_estimate=pl.CostEstimate(flops=5_500_000_000, bytes_accessed=12_000_000, transcendentals=2_000_000),
    )(latent_grad, frames, gain, weight, bias)


def finish_kernel(total, weight_grad, small):
    for core in range(2):
        lanes = pl.ds(core * 128, 128)
        for x in range(NX):
            rows = pl.ds(x * 16, 16)
            for tap in range(27):
                weight_grad[tap, rows, lanes] = total[core, x, tap // TAPS, tap % TAPS].astype(F32)
        sums = total[core, 0, 6, 3].astype(F32)
        row = sums[0:8] + pltpu.roll(sums[0:8], 6, 0)
        for side in range(2):

            @pl.when(lax.axis_index("tm") == 2 * core + side)
            def _():
                small[...] = row[:, 64 * side : 64 * side + 64]


def finish(total):
    return pl.pallas_call(
        finish_kernel,
        out_shape=(jax.ShapeDtypeStruct((27, 64, 256), F32), jax.ShapeDtypeStruct((8, 64), F32)),
        in_specs=[pl.BlockSpec(memory_space=pltpu.VMEM)],
        out_specs=[pl.BlockSpec(memory_space=pltpu.VMEM)] * 2,
    )(total)


def on_device(frames, norm_gain, conv_weight, conv_bias, latent_grad):
    frames_grad, latent, total = whole(
        latent_grad.reshape(4, 128, 256), frames, norm_gain.reshape(1, 256),
        conv_weight.reshape(3, 9, 256, 256), conv_bias.reshape(1, 256),
    )
    weight_grad, small = finish(total)
    return (
        latent.reshape(4, 64, 2, 256), frames_grad, weight_grad.reshape(3, 3, 3, 64, 256), small[0], small[1],
    )


def solution(mesh):
    placed = (P("tm", "rows", None, None), P(), P(), P(), P("tm", None, "rows", None))
    return jax.shard_map(
        on_device,
        mesh=mesh,
        in_specs=placed,
        out_specs=(
            P("tm", None, "rows", None),
            P("tm", "rows", None, None),
            P(None, None, None, "tm", None),
            P("tm"),
            P("tm"),
        ),
        check_vma=False,
    )
```

```python
import jax
import jax.numpy as jnp
from jax import lax
from jax.experimental import pallas as pl
from jax.experimental.pallas import tpu as pltpu
from jax.sharding import PartitionSpec as P

F32 = jnp.float32
BF16 = jnp.bfloat16
MESH = pl.DeviceIdType.MESH
EPS = 1e-06
NX, NZ, NY = 4, 8, 4
CHUNKS, TAPS = 7, 4


def dot_nt(left, right):
    return lax.dot_general(left, right, (((1,), (1,)), ((), ())), preferred_element_type=F32)


def dot_nn(left, right):
    return lax.dot_general(left, right, (((1,), (0,)), ((), ())), preferred_element_type=F32)


def inverse_rms(signal):
    return lax.rsqrt(jnp.mean(signal * signal, axis=-1, keepdims=True) + EPS)


def whole_kernel(
    latent_grad, frames, gain, weight_far, bias,
    frames_grad, latent, result,
    weight, blocks, middle, landed, flat, woven, grad, grad_above, early, below,
    columns, turned, grad_next, spread, tile, gain_sum, parts,
    other, mine, first_plus, first_minus, second_plus, second_minus,
    mid, first_plus2, first_minus2, second_plus2, second_minus2,
    low, arrive, total, block, latent_in, latent_mid, latent_out,
    weight_sem, gz_sem, gs_sem, near_sem,
    core_sem, ring_sem, ring2_sem, z_sem, zback_sem, x_sem, pair_sem, lz_sem, ls_sem,
):
    rows_at = lax.axis_index("rows")
    y = lax.axis_index("tm")
    core, x, z = rows_at % 2, (rows_at // 2) % NX, rows_at // (2 * NX)
    slab = rows_at % (2 * NX)
    count = NZ * 2 * NX

    def row_of(z_at, x_at, core_at):
        return z_at * (2 * NX) + x_at * 2 + core_at

    sibling = (row_of(z, x, 1 - core), y)

    def along(axis, step):
        if axis == "y":
            return (rows_at, (y + step + NY) % NY)
        if axis == "x":
            return (row_of(z, (x + step) % NX, core), y)
        if axis == "slab":
            return (z * (2 * NX) + (slab + step) % (2 * NX), y)
        if axis == "row":
            return ((rows_at + step + count) % count, y)
        return (row_of((z + step) % NZ, x, core), y)

    weight_in = pltpu.make_async_copy(weight_far, weight, weight_sem.at[0])
    weight_in.start()

    barrier = pltpu.get_barrier_semaphore()
    friends = [along("z", step) for step in range(1, NZ)] + [along("slab", step) for step in range(1, 2 * NX)]
    friends += [along("y", 1), along("y", -1), along("row", 1), along("row", -1)]
    for friend in friends:
        pl.semaphore_signal(barrier, inc=1, device_id=friend, device_id_type=MESH)

    def unweave(target):
        for frame in range(4):
            for half in range(2):
                for side in range(2):
                    flat[half, pl.ds(2 * frame + side, 64, stride=8), :] = woven[frame, half, pl.ds(side, 64, stride=2), :]
        for half in range(2):
            target[:, :, :, pl.ds(half * 128, 128)] = flat[half].reshape(NZ, 2 * NX, 8, 128).astype(BF16)

    def weave(source, put):
        for half in range(2):
            flat[half] = source[:, :, :, pl.ds(half * 128, 128)].astype(F32).reshape(512, 128)
        for frame in range(4):
            for half in range(2):
                for side in range(2):
                    woven[frame, half, pl.ds(side, 64, stride=2), :] = flat[half, pl.ds(2 * frame + side, 64, stride=8), :]
                put(frame, half, woven[frame, half].astype(BF16))

    for frame in range(4):
        for half in range(2):
            woven[frame, half] = latent_grad[frame, :, :, pl.ds(half * 128, 128)].reshape(128, 128).astype(F32)
    unweave(blocks)

    pl.semaphore_wait(barrier, len(friends))

    def copy_to(source, target, sems, at, device):
        return pltpu.make_async_remote_copy(
            src_ref=source, dst_ref=target, send_sem=sems.at[(0, *at)], recv_sem=sems.at[(1, *at)],
            device_id=device, device_id_type=MESH,
        )

    def send(*args):
        copy = copy_to(*args)
        copy.start()
        return copy

    ahead, own, late = pl.ds(0, 256), pl.ds(0, 512), pl.ds(512, 256)
    early_on = copy_to(frames.at[pl.ds(2, 2)], early, near_sem, (0,), along("y", 1))
    below_own = copy_to(frames.at[:, 0], below.at[pl.ds(2, 4)], near_sem, (1,), along("row", -1))
    below_early = copy_to(early.at[:, 0], below.at[pl.ds(0, 2)], near_sem, (2,), along("row", -1))
    grad_late = copy_to(grad.at[ahead], grad.at[late], near_sem, (3,), along("y", -1))
    above_own = copy_to(grad.at[own], grad_above.at[own], near_sem, (4,), along("row", 1))
    above_late = copy_to(grad.at[late], grad_above.at[late], near_sem, (5,), along("row", 1))
    has_past, has_future = y > 0, y < NY - 1
    has_above, has_below = rows_at > 0, rows_at < count - 1

    def only(condition, *actions):
        @pl.when(condition)
        def _():
            for action in actions:
                action()

    order = (0, 1, 7, 2, 6, 3, 5, 4)

    def hop_one(source, between, sems):
        return [
            send(source.at[(z + step) % NZ], between.at[z], sems, (step,), along("z", step)) for step in order[1:]
        ]

    def hop_two(between, target, sems, step):
        at = (z - step + NZ) % NZ
        return [
            send(between.at[at, (slab + move) % (2 * NX)], target.at[at, slab], sems, (step, move), along("slab", move))
            for move in range(1, 2 * NX)
        ]

    g_outer = hop_one(blocks, middle, gz_sem)
    only(has_future, early_on.start)
    only(has_above, below_own.start)
    middle[z] = blocks[z]
    g_inner = hop_two(middle, landed, gs_sem, 0)

    @pl.when(jnp.logical_not(has_past))
    def _():
        early[...] = jnp.zeros_like(early)

    @pl.when(jnp.logical_not(has_below))
    def _():
        below[...] = jnp.zeros_like(below)

    @pl.when(jnp.logical_not(has_above))
    def _():
        grad_above[...] = jnp.zeros_like(grad_above)

    @pl.when(jnp.logical_not(has_future))
    def _():
        grad[late, :] = jnp.zeros((256, 256), BF16)

    gain_row = gain[...]
    row_at = lax.broadcasted_iota(jnp.int32, (128, 256), 0)

    def hidden_tile(source, at, row, keep):
        for piece_at in range(4):
            rows = pl.ds(piece_at * 64, 64)
            signal = source[rows, :].astype(F32)
            normed = signal * inverse_rms(signal) * gain_row
            hidden = normed / (1.0 + jnp.exp(-normed))
            tile[row, 0, rows, :] = hidden[:, :128]
            tile[row, 1, rows, :] = hidden[:, 128:]
        even = jnp.concatenate([tile[row, half, pl.ds(0, 128, stride=2), :] for half in range(2)], axis=1)
        odd = jnp.concatenate([tile[row, half, pl.ds(1, 128, stride=2), :] for half in range(2)], axis=1)
        after = jnp.where(row_at == 127, 0.0, pltpu.roll(even, 127, 0))
        where = pl.ds(pl.multiple_of(at * 128, 128), 128)
        columns[where, pl.ds(row * 768, 256)] = even.astype(BF16)
        columns[where, pl.ds(row * 768 + 256, 256)] = odd.astype(BF16)
        columns[where, pl.ds(row * 768 + 512, 256)] = after.astype(BF16)
        if keep:
            lanes = pl.ds(pl.multiple_of((at - 2) * 128, 128), 128)
            turned[2 * row, :, lanes] = even.T.astype(BF16)
            turned[2 * row + 1, :, lanes] = odd.T.astype(BF16)

    @pl.loop(2, 6)
    def _(at):
        hidden_tile(frames.at[at - 2, 0], at, 0, True)
        hidden_tile(frames.at[at - 2, 1], at, 1, True)

    for copy, step in zip(g_outer, order[1:]):
        copy.wait_recv()
        g_inner += hop_two(middle, landed, gs_sem, step)
    landed[:, slab] = middle[:, slab]
    spread[...] = jnp.zeros_like(spread)
    gain_sum[...] = jnp.zeros_like(gain_sum)
    weight_in.wait()
    for copy in g_inner:
        copy.wait_recv()

    def put_grad(frame, half, value):
        grad[pl.ds(frame * 128, 128), pl.ds(half * 128, 128)] = value

    weave(landed, put_grad)
    only(has_past, grad_late.start)
    only(has_below, above_own.start)

    def step_on(which, source, frames_at):
        for at in frames_at:
            where = pl.ds(at * 128, 128)
            moved = pltpu.roll(source[where, :].astype(F32), 1, 0)
            grad_next[which, where, :] = jnp.where(row_at == 0, 0.0, moved).astype(BF16)

    def weight_taps(chunk):
        for tap in range(chunk * TAPS, min(27, chunk * TAPS + TAPS)):
            tap_t, tap_r, tap_c = tap // 9, tap // 3 % 3, tap % 3
            where = pl.ds((2 - tap_t) * 128, 512)
            left = turned[2 * (tap_r % 2) + tap_c % 2]
            if tap_c == 2:
                right = grad_next[1 if tap_r == 2 else 0, where, :]
            else:
                right = (grad_above if tap_r == 2 else grad)[where, :]
            product = dot_nn(left, right).astype(BF16)
            parts[0, tap] = product[:, :128]
            parts[1, tap] = product[:, 128:]

    pair = {}

    def pair_send(chunk):
        spots = pl.ds(chunk * TAPS, TAPS)
        pair[chunk] = send(parts.at[1 - core, spots], other.at[spots], core_sem, (chunk,), sibling)

    def axes_of(chunk):
        return ("y", "x") if chunk % 2 == 0 else ("x", "y")

    def here(axis, step):
        return (y + step) % NY if axis == "y" else (x + step) % NX

    def piece(ref, chunk, stage, at, taps):
        if stage == 0 and axes_of(chunk)[0] == "x":
            return ref.at[chunk, taps, slice(None), at]
        return ref.at[chunk, taps, at]

    FIRST, LAST, ALL = pl.ds(0, 2), pl.ds(2, 2), pl.ds(0, 4)
    banks = (
        (mine, first_plus, first_minus, second_plus, second_minus, ring_sem, BF16),
        (mid, first_plus2, first_minus2, second_plus2, second_minus2, ring2_sem, F32),
    )

    def ring_open(chunk, stage):
        source, plus, minus, _, _, sems, _ = banks[stage]
        axis = axes_of(chunk)[stage]
        far = here(axis, 2)
        return [
            send(piece(source, chunk, stage, far, FIRST), plus.at[chunk], sems, (chunk, 0), along(axis, 1)),
            send(piece(source, chunk, stage, far, LAST), minus.at[chunk], sems, (chunk, 1), along(axis, 3)),
        ]

    def ring_next(chunk, stage, opened):
        source, plus, minus, plus_in, minus_in, sems, kind = banks[stage]
        axis = axes_of(chunk)[stage]
        opened[0].wait_recv()
        ahead = piece(source, chunk, stage, here(axis, 1), FIRST)
        ahead[...] = (ahead[...].astype(F32) + plus[chunk].astype(F32)).astype(kind)
        one = send(piece(source, chunk, stage, here(axis, 1), ALL), plus_in.at[chunk], sems, (chunk, 2), along(axis, 1))
        opened[1].wait_recv()
        behind = piece(source, chunk, stage, here(axis, 3), LAST)
        behind[...] = (behind[...].astype(F32) + minus[chunk].astype(F32)).astype(kind)
        two = send(piece(source, chunk, stage, here(axis, 3), ALL), minus_in.at[chunk], sems, (chunk, 3), along(axis, 3))
        return [one, two]

    def ring_close(chunk, stage, sent):
        source, _, _, plus_in, minus_in, _, _ = banks[stage]
        axis = axes_of(chunk)[stage]
        sent[0].wait_recv()
        sent[1].wait_recv()
        own = piece(source, chunk, stage, here(axis, 0), ALL)[...].astype(F32)
        summed = own + plus_in[chunk].astype(F32) + minus_in[chunk].astype(F32)
        if stage == 0:
            mid[chunk] = summed
        else:
            low[chunk] = summed.reshape(NZ, 8, 128)

    shares = {}

    def to_owners(chunk):
        shares[chunk] = [
            send(low.at[chunk, (z + step) % NZ], arrive.at[step, chunk], z_sem, (chunk, step), along("z", step))
            for step in order[1:]
        ]

    opened, sent, opened2, sent2 = {}, {}, {}, {}

    def pair_close(chunk):
        pair[chunk].wait_recv()
        spots = pl.ds(chunk * TAPS, TAPS)
        summed = parts[core, spots].astype(F32) + other[spots].astype(F32)
        mine[chunk] = summed.astype(BF16).reshape(TAPS, NY, NX, 16, 128)
        opened[chunk] = ring_open(chunk, 0)

    def next_one(*chunks):
        for chunk in chunks:
            sent[chunk] = ring_next(chunk, 0, opened[chunk])

    def close_one(*chunks):
        for chunk in chunks:
            ring_close(chunk, 0, sent[chunk])
            opened2[chunk] = ring_open(chunk, 1)

    def next_two(*chunks):
        for chunk in chunks:
            sent2[chunk] = ring_next(chunk, 1, opened2[chunk])

    def close_two(*chunks):
        for chunk in chunks:
            ring_close(chunk, 1, sent2[chunk])
            to_owners(chunk)

    step_on(0, grad, range(4))
    weight_taps(5)
    pair_send(5)
    only(has_past, early_on.wait_recv)
    only(has_above, below_early.start)

    @pl.loop(0, 2)
    def _(at):
        hidden_tile(early.at[at, 0], at, 0, False)
        hidden_tile(early.at[at, 1], at, 1, False)

    pair_close(5)
    only(has_future, grad_late.wait_recv)
    only(has_below, above_late.start)
    step_on(0, grad, (4, 5))
    weight_taps(0)
    pair_send(0)
    only(has_above, above_own.wait_recv, above_late.wait_recv)
    step_on(1, grad_above, range(6))
    before = 0
    for chunk in (3, 1, 2, 4):
        weight_taps(chunk)
        pair_send(chunk)
        pair_close(before)
        before = chunk

    def back_taps(tap):
        where = pl.ds((2 - tap) * 128, 512)
        here_g, here_next = grad[where, :], grad_next[0, where, :]
        above, above_next = grad_above[where, :], grad_next[1, where, :]
        spread[0] += dot_nt(here_g, weight[tap, 0]) + dot_nt(here_next, weight[tap, 2])
        spread[0] += dot_nt(above, weight[tap, 6]) + dot_nt(above_next, weight[tap, 8])
        spread[1] += dot_nt(here_g, weight[tap, 1]) + dot_nt(above, weight[tap, 7])
        spread[2] += dot_nt(here_g, weight[tap, 3]) + dot_nt(here_next, weight[tap, 5])
        spread[3] += dot_nt(here_g, weight[tap, 4])

    def frame_back(first, last):
        @pl.loop(first, last)
        def _(at):
            where = pl.ds(pl.multiple_of(at * 128, 128), 128)
            for row in range(2):
                for half in range(2):
                    lanes = pl.ds(half * 128, 128)
                    tile[row, half, pl.ds(0, 128, stride=2), :] = spread[2 * row, where, lanes]
                    tile[row, half, pl.ds(1, 128, stride=2), :] = spread[2 * row + 1, where, lanes]
                for piece_at in range(4):
                    rows = pl.ds(piece_at * 64, 64)
                    signal = frames[at, row, rows, :].astype(F32)
                    inv = inverse_rms(signal)
                    unit = signal * inv
                    normed = unit * gain_row
                    sigma = 1.0 / (1.0 + jnp.exp(-normed))
                    arrived = jnp.concatenate([tile[row, half, rows, :] for half in range(2)], axis=1)
                    normed_grad = arrived * sigma * (1.0 + normed * (1.0 - sigma))
                    gain_sum[...] += jnp.sum((normed_grad * unit).reshape(8, 8, 256), axis=0)
                    unit_grad = normed_grad * gain_row
                    mean = jnp.mean(unit_grad * unit, axis=-1, keepdims=True)
                    frames_grad[at, row, rows, :] = (inv * (unit_grad - unit * mean)).astype(BF16)

    back_taps(0)
    pair_close(before)
    back_taps(1)
    back_taps(2)
    next_one(5, 0)
    frame_back(0, 2)
    next_one(3, 1)
    frame_back(2, 4)

    gain_local = jnp.sum(gain_sum[...], axis=0, keepdims=True)
    bias_local = jnp.sum(grad[pl.ds(0, 512), :].astype(F32), axis=0, keepdims=True)
    gain_rest = gain_local - gain_local.astype(BF16).astype(F32)
    bias_rest = bias_local - bias_local.astype(BF16).astype(F32)
    spot = lax.broadcasted_iota(jnp.int32, (256, 256), 0) % 64
    small = jnp.where(spot == 0, gain_local, jnp.where(spot == 1, bias_local, 0.0))
    small = jnp.where(spot == 2, gain_rest, jnp.where(spot == 3, bias_rest, small)).astype(BF16)
    parts[0, 27] = small[:, :128]
    parts[1, 27] = small[:, 128:]
    weight_taps(6)
    pair_send(6)
    next_one(2, 4)
    only(has_below, below_own.wait_recv, below_early.wait_recv)

    @pl.loop(0, 6)
    def _(at):
        hidden_tile(below.at[at], at, 2, False)

    pair_close(6)
    close_one(5, 0)
    spread[0] = jnp.broadcast_to(bias[...], (512, 256))

    @pl.loop(0, 3)
    def _(tap):
        where = pl.ds(pl.multiple_of(tap * 128, 128), 512)
        spread[0] += dot_nn(columns[where, :], weight[tap].reshape(2304, 256))

    for frame in range(4):
        for half in range(2):
            woven[frame, half] = spread[0, pl.ds(frame * 128, 128), pl.ds(half * 128, 128)]
    unweave(latent_in)
    outer = hop_one(latent_in, latent_mid, lz_sem)
    latent_mid[z] = latent_in[z]
    close_one(3, 1)
    next_one(6)
    close_one(2, 4)
    next_two(5, 0, 3, 1)
    close_one(6)
    inner = hop_two(latent_mid, latent_out, ls_sem, 0)
    next_two(2, 4)
    close_two(5, 0, 3, 1)
    next_two(6)
    close_two(2, 4)
    for copy, step in zip(outer, order[1:]):
        copy.wait_recv()
        inner += hop_two(latent_mid, latent_out, ls_sem, step)
    latent_out[:, slab] = latent_mid[:, slab]
    close_two(6)
    started = list(pair.values()) + outer + inner + g_outer + g_inner
    for table in (opened, sent, opened2, sent2, shares):
        for chunk in range(CHUNKS):
            started += table[chunk]

    for chunk in (5, 0, 3, 1, 2, 4, 6):
        summed = low[chunk, z]
        for copy, step in zip(shares[chunk], order[1:]):
            copy.wait_recv()
            summed += arrive[step, chunk]
        total[z, chunk] = summed.astype(BF16)

    def back(step):
        return copy_to(total.at[z], total.at[z], zback_sem, (step,), along("z", step))

    for step in order[1:]:
        back(step).start()

    right, left, across = (x + 1) % NX, (x + 3) % NX, (x + 2) % NX
    HALF, REST = pl.ds(0, 4), pl.ds(4, 3)

    def to_right(step, at):
        return copy_to(total.at[at], block.at[x, at], x_sem, (0, step), along("x", 1))

    def to_left(step, at):
        return copy_to(total.at[at], block.at[x, at], x_sem, (1, step), along("x", 3))

    def on_right(step, at):
        half = block.at[left, at, HALF]
        return copy_to(half, half, x_sem, (2, step), along("x", 1))

    def on_left(step, at):
        half = block.at[right, at, REST]
        return copy_to(half, half, x_sem, (3, step), along("x", 3))

    def across_core(which, step, at):
        source = total.at[at] if which == 0 else block.at[(left, right, across)[which - 1], at]
        where = (x, left, right, across)[which]
        return copy_to(source, result.at[core, where, at], pair_sem, (which, step), sibling)

    def each(body):
        for step in order:
            body(step, (z - step + NZ) % NZ)

    def fan_one(step, at):
        if step:
            back(step).wait_recv()
        to_right(step, at).start()
        to_left(step, at).start()
        across_core(0, step, at).start()
        result[core, x, at] = total[at]

    def fan_two(step, at):
        to_right(step, at).wait_recv()
        on_right(step, at).start()
        across_core(1, step, at).start()
        result[core, left, at] = block[left, at]
        to_left(step, at).wait_recv()
        on_left(step, at).start()
        across_core(2, step, at).start()
        result[core, right, at] = block[right, at]

    def fan_three(step, at):
        on_right(step, at).wait_recv()
        on_left(step, at).wait_recv()
        across_core(3, step, at).start()
        result[core, across, at] = block[across, at]

    def fan_last(step, at):
        for which in range(4):
            across_core(which, step, at).wait()
        to_right(step, at).wait_send()
        to_left(step, at).wait_send()
        on_right(step, at).wait_send()
        on_left(step, at).wait_send()

    each(fan_one)
    for copy in inner:
        copy.wait_recv()

    def put_latent(frame, half, value):
        latent[frame, :, pl.ds(half * 128, 128)] = value

    weave(latent_out, put_latent)
    each(fan_two)
    each(fan_three)
    for copy in started:
        copy.wait_send()
    each(fan_last)
    only(has_future, early_on.wait_send)
    only(has_above, below_own.wait_send, below_early.wait_send)
    only(has_past, grad_late.wait_send)
    only(has_below, above_own.wait_send, above_late.wait_send)
    for step in order[1:]:
        back(step).wait_send()


def whole(latent_grad, frames, gain, weight, bias):
    dma, vmem = pltpu.SemaphoreType.DMA, pltpu.VMEM
    inside = pl.BlockSpec(memory_space=pltpu.VMEM)
    return pl.pallas_call(
        whole_kernel,
        out_shape=(
            jax.ShapeDtypeStruct((4, 2, 256, 256), BF16),
            jax.ShapeDtypeStruct((4, 128, 256), BF16),
            jax.ShapeDtypeStruct((2, NX, NZ, CHUNKS, 8, 128), BF16),
        ),
        in_specs=[inside, inside, inside, pl.BlockSpec(memory_space=pl.ANY), inside],
        out_specs=[inside] * 3,
        scratch_shapes=[
            vmem((3, 9, 256, 256), BF16),
            vmem((NZ, 2 * NX, 8, 256), BF16),
            vmem((NZ, 2 * NX, 8, 256), BF16),
            vmem((NZ, 2 * NX, 8, 256), BF16),
            vmem((2, 512, 128), F32),
            vmem((4, 2, 128, 128), F32),
            vmem((768, 256), BF16),
            vmem((768, 256), BF16),
            vmem((2, 2, 256, 256), BF16),
            vmem((6, 256, 256), BF16),
            vmem((768, 2304), BF16),
            vmem((4, 256, 512), BF16),
            vmem((2, 768, 256), BF16),
            vmem((4, 512, 256), F32),
            vmem((3, 2, 256, 128), F32),
            vmem((8, 256), F32),
            vmem((2, 28, 256, 128), BF16),
            vmem((CHUNKS * TAPS, 256, 128), BF16),
            vmem((CHUNKS, TAPS, NY, NX, 16, 128), BF16),
            vmem((CHUNKS, 2, 4, 16, 128), BF16),
            vmem((CHUNKS, 2, 4, 16, 128), BF16),
            vmem((CHUNKS, TAPS, 4, 16, 128), BF16),
            vmem((CHUNKS, TAPS, 4, 16, 128), BF16),
            vmem((CHUNKS, TAPS, 4, 16, 128), F32),
            vmem((CHUNKS, 2, 16, 128), F32),
            vmem((CHUNKS, 2, 16, 128), F32),
            vmem((CHUNKS, TAPS, 16, 128), F32),
            vmem((CHUNKS, TAPS, 16, 128), F32),
            vmem((CHUNKS, NZ, 8, 128), F32),
            vmem((NZ, CHUNKS, 8, 128), F32),
            vmem((NZ, CHUNKS, 8, 128), BF16),
            vmem((NX, NZ, CHUNKS, 8, 128), BF16),
            vmem((NZ, 2 * NX, 8, 256), BF16),
            vmem((NZ, 2 * NX, 8, 256), BF16),
            vmem((NZ, 2 * NX, 8, 256), BF16),
            dma((1,)),
            dma((2, NZ)),
            dma((2, NZ, 2 * NX)),
            dma((2, 6)),
            dma((2, CHUNKS)),
            dma((2, CHUNKS, 4)),
            dma((2, CHUNKS, 4)),
            dma((2, CHUNKS, NZ)),
            dma((2, NZ)),
            dma((2, 4, NZ)),
            dma((2, 4, NZ)),
            dma((2, NZ)),
            dma((2, NZ, 2 * NX)),
        ],
        compiler_params=pltpu.CompilerParams(collective_id=1, has_side_effects=True),
        cost_estimate=pl.CostEstimate(flops=5_500_000_000, bytes_accessed=12_000_000, transcendentals=2_000_000),
    )(latent_grad, frames, gain, weight, bias)


def finish_kernel(
    total_far, frames_far, latent_far, weight_grad, frames_grad, latent, gain_grad, bias_grad,
    total, frames_near, latent_near, latent_wide, wide, sems,
):
    copy = pltpu.make_async_copy
    total_in = copy(total_far, total, sems.at[0])
    frames_in = copy(frames_far, frames_near, sems.at[1])
    latent_in = copy(latent_far, latent_near, sems.at[2])
    total_in.start()
    frames_in.start()
    latent_in.start()
    total_in.wait()
    going = []
    for chunk in range(CHUNKS):
        for tap in range(chunk * TAPS, min(27, chunk * TAPS + TAPS)):
            for core in range(2):
                for x in range(NX):
                    for side in range(2):
                        part = total[core, x, 2 * (tap % TAPS) + side, chunk]
                        wide[tap, pl.ds(x * 16 + side * 8, 8), pl.ds(core * 128, 128)] = part.astype(F32)
        taps = pl.ds(chunk * TAPS, min(27, chunk * TAPS + TAPS) - chunk * TAPS)
        going.append(copy(wide.at[taps], weight_grad.at[taps], sems.at[3 + chunk]))
        going[-1].start()
        if chunk == 1:
            frames_in.wait()
            going.append(copy(frames_near, frames_grad, sems.at[10]))
            going[-1].start()
        if chunk == 3:
            latent_in.wait()
            for frame in range(4):
                latent_wide[frame] = latent_near[frame].reshape(64, 2, 256)
            going.append(copy(latent_wide, latent, sems.at[11]))
            going[-1].start()
    for core in range(2):
        sums = total[core, 0, 6, 6].astype(F32)
        row = sums + pltpu.roll(sums, 6, 0)
        for side in range(2):

            @pl.when(lax.axis_index("tm") == 2 * core + side)
            def _():
                gain_grad[...] = row[0:1, 64 * side : 64 * side + 64]
                bias_grad[...] = row[1:2, 64 * side : 64 * side + 64]

    for item in going:
        item.wait()


def finish(total, frames_grad, latent):
    inside, far = pl.BlockSpec(memory_space=pltpu.VMEM), pl.BlockSpec(memory_space=pl.ANY)
    return pl.pallas_call(
        finish_kernel,
        out_shape=(
            jax.ShapeDtypeStruct((27, 64, 256), F32),
            jax.ShapeDtypeStruct((4, 2, 256, 256), BF16),
            jax.ShapeDtypeStruct((4, 64, 2, 256), BF16),
            jax.ShapeDtypeStruct((1, 64), F32),
            jax.ShapeDtypeStruct((1, 64), F32),
        ),
        in_specs=[far] * 3,
        out_specs=[far, far, far, inside, inside],
        scratch_shapes=[
            pltpu.VMEM((2, NX, NZ, CHUNKS, 8, 128), BF16),
            pltpu.VMEM((4, 2, 256, 256), BF16),
            pltpu.VMEM((4, 128, 256), BF16),
            pltpu.VMEM((4, 64, 2, 256), BF16),
            pltpu.VMEM((27, 64, 256), F32),
            pltpu.SemaphoreType.DMA((12,)),
        ],
    )(total, frames_grad, latent)


def on_device(frames, norm_gain, conv_weight, conv_bias, latent_grad):
    frames_grad, latent, total = whole(
        latent_grad, frames, norm_gain.reshape(1, 256), conv_weight.reshape(3, 9, 256, 256), conv_bias.reshape(1, 256),
    )
    weight_grad, frames_grad, latent, gain_grad, bias_grad = finish(total, frames_grad, latent)
    return (
        latent, frames_grad, weight_grad.reshape(3, 3, 3, 64, 256), gain_grad.reshape(64), bias_grad.reshape(64),
    )


def solution(mesh):
    placed = (P("tm", "rows", None, None), P(), P(), P(), P("tm", None, "rows", None))
    return jax.shard_map(
        on_device,
        mesh=mesh,
        in_specs=placed,
        out_specs=(
            P("tm", None, "rows", None),
            P("tm", "rows", None, None),
            P(None, None, None, "tm", None),
            P("tm"),
            P("tm"),
        ),
        check_vma=False,
    )
```

```python
import jax
import jax.numpy as jnp
from jax import lax
from jax.experimental import pallas as pl
from jax.experimental.pallas import tpu as pltpu
from jax.sharding import PartitionSpec as P

F32 = jnp.float32
BF16 = jnp.bfloat16
MESH = pl.DeviceIdType.MESH
EPS = 1e-06
NX, NZ, NY = 4, 8, 4
CHUNKS, TAPS = 7, 4


def dot_nt(left, right):
    return lax.dot_general(left, right, (((1,), (1,)), ((), ())), preferred_element_type=F32)


def dot_nn(left, right):
    return lax.dot_general(left, right, (((1,), (0,)), ((), ())), preferred_element_type=F32)


def inverse_rms(signal):
    return lax.rsqrt(jnp.mean(signal * signal, axis=-1, keepdims=True) + EPS)


def whole_kernel(
    latent_grad_far, frames_far, gain, weight_far, bias,
    frames_grad_far, latent_far, result, note_out,
    latent_grad, frames, frames_grad, latent, sib, note, note_pair, note_y, note_x, note_z, note_end,
    weight, blocks, middle, landed, flat, woven, grad, grad_above, early, below,
    columns, turned, grad_next, spread, tile, gain_sum, parts,
    other, mine, first_plus, first_minus, second_plus, second_minus,
    mid, first_plus2, first_minus2, second_plus2, second_minus2,
    low, arrive, total, block, latent_in, latent_mid, latent_out,
    weight_sem, gz_sem, gs_sem, near_sem,
    core_sem, ring_sem, ring2_sem, z_sem, zback_sem, x_sem, pair_sem, lz_sem, ls_sem, note_sem, out_sem,
):
    rows_at = lax.axis_index("rows")
    y = lax.axis_index("tm")
    core, x, z = rows_at % 2, (rows_at // 2) % NX, rows_at // (2 * NX)
    slab = rows_at % (2 * NX)
    count = NZ * 2 * NX

    def row_of(z_at, x_at, core_at):
        return z_at * (2 * NX) + x_at * 2 + core_at

    sibling = (row_of(z, x, 1 - core), y)

    def along(axis, step):
        if axis == "y":
            return (rows_at, (y + step + NY) % NY)
        if axis == "x":
            return (row_of(z, (x + step) % NX, core), y)
        if axis == "slab":
            return (z * (2 * NX) + (slab + step) % (2 * NX), y)
        if axis == "row":
            return ((rows_at + step + count) % count, y)
        return (row_of((z + step) % NZ, x, core), y)

    barrier = pltpu.get_barrier_semaphore()
    friends = [along("z", step) for step in range(1, NZ)] + [along("slab", step) for step in range(1, 2 * NX)]
    friends += [along("y", 1), along("y", 2), along("y", -1), along("row", 1), along("row", -1)]
    for friend in friends:
        pl.semaphore_signal(barrier, inc=1, device_id=friend, device_id_type=MESH)
    latent_grad_in = pltpu.make_async_copy(latent_grad_far, latent_grad, weight_sem.at[1])
    frames_in = pltpu.make_async_copy(frames_far, frames, weight_sem.at[2])
    weight_in = pltpu.make_async_copy(weight_far, weight, weight_sem.at[0])
    latent_grad_in.start()
    frames_in.start()
    weight_in.start()
    latent_grad_in.wait()

    def unweave(target):
        for frame in range(4):
            for half in range(2):
                for side in range(2):
                    flat[half, pl.ds(2 * frame + side, 64, stride=8), :] = woven[frame, half, pl.ds(side, 64, stride=2), :]
        for half in range(2):
            target[:, :, :, pl.ds(half * 128, 128)] = flat[half].reshape(NZ, 2 * NX, 8, 128).astype(BF16)

    def weave(source, put):
        for half in range(2):
            flat[half] = source[:, :, :, pl.ds(half * 128, 128)].astype(F32).reshape(512, 128)
        for frame in range(4):
            for half in range(2):
                for side in range(2):
                    woven[frame, half, pl.ds(side, 64, stride=2), :] = flat[half, pl.ds(2 * frame + side, 64, stride=8), :]
                put(frame, half, woven[frame, half].astype(BF16))

    for frame in range(4):
        for half in range(2):
            woven[frame, half] = latent_grad[frame, :, :, pl.ds(half * 128, 128)].reshape(128, 128).astype(F32)
    unweave(blocks)

    pl.semaphore_wait(barrier, len(friends))

    def copy_to(source, target, sems, at, device):
        return pltpu.make_async_remote_copy(
            src_ref=source, dst_ref=target, send_sem=sems.at[(0, *at)], recv_sem=sems.at[(1, *at)],
            device_id=device, device_id_type=MESH,
        )

    def send(*args):
        copy = copy_to(*args)
        copy.start()
        return copy

    ahead, own, late = pl.ds(0, 256), pl.ds(0, 512), pl.ds(512, 256)
    early_on = copy_to(frames.at[pl.ds(2, 2)], early, near_sem, (0,), along("y", 1))
    below_own = copy_to(frames.at[:, 0], below.at[pl.ds(2, 4)], near_sem, (1,), along("row", -1))
    below_early = copy_to(early.at[:, 0], below.at[pl.ds(0, 2)], near_sem, (2,), along("row", -1))
    grad_late = copy_to(grad.at[ahead], grad.at[late], near_sem, (3,), along("y", -1))
    above_own = copy_to(grad.at[own], grad_above.at[own], near_sem, (4,), along("row", 1))
    above_late = copy_to(grad.at[late], grad_above.at[late], near_sem, (5,), along("row", 1))
    has_past, has_future = y > 0, y < NY - 1
    has_above, has_below = rows_at > 0, rows_at < count - 1

    def only(condition, *actions):
        @pl.when(condition)
        def _():
            for action in actions:
                action()

    order = (0, 1, 7, 2, 6, 3, 5, 4)

    def hop_one(source, between, sems):
        return [
            send(source.at[(z + step) % NZ], between.at[z], sems, (step,), along("z", step)) for step in order[1:]
        ]

    def hop_two(between, target, sems, step):
        at = (z - step + NZ) % NZ
        return [
            send(between.at[at, (slab + move) % (2 * NX)], target.at[at, slab], sems, (step, move), along("slab", move))
            for move in range(1, 2 * NX)
        ]

    g_outer = hop_one(blocks, middle, gz_sem)
    frames_in.wait()
    only(has_future, early_on.start)
    only(has_above, below_own.start)
    middle[z] = blocks[z]
    g_inner = hop_two(middle, landed, gs_sem, 0)

    @pl.when(jnp.logical_not(has_past))
    def _():
        early[...] = jnp.zeros_like(early)

    @pl.when(jnp.logical_not(has_below))
    def _():
        below[...] = jnp.zeros_like(below)

    @pl.when(jnp.logical_not(has_above))
    def _():
        grad_above[...] = jnp.zeros_like(grad_above)

    @pl.when(jnp.logical_not(has_future))
    def _():
        grad[late, :] = jnp.zeros((256, 256), BF16)

    gain_row = gain[...]
    row_at = lax.broadcasted_iota(jnp.int32, (128, 256), 0)

    def hidden_tile(source, at, row, keep):
        for piece_at in range(4):
            rows = pl.ds(piece_at * 64, 64)
            signal = source[rows, :].astype(F32)
            normed = signal * inverse_rms(signal) * gain_row
            hidden = normed / (1.0 + jnp.exp(-normed))
            tile[row, 0, rows, :] = hidden[:, :128]
            tile[row, 1, rows, :] = hidden[:, 128:]
        even = jnp.concatenate([tile[row, half, pl.ds(0, 128, stride=2), :] for half in range(2)], axis=1)
        odd = jnp.concatenate([tile[row, half, pl.ds(1, 128, stride=2), :] for half in range(2)], axis=1)
        after = jnp.where(row_at == 127, 0.0, pltpu.roll(even, 127, 0))
        where = pl.ds(pl.multiple_of(at * 128, 128), 128)
        columns[where, pl.ds(row * 768, 256)] = even.astype(BF16)
        columns[where, pl.ds(row * 768 + 256, 256)] = odd.astype(BF16)
        columns[where, pl.ds(row * 768 + 512, 256)] = after.astype(BF16)
        if keep:
            lanes = pl.ds(pl.multiple_of((at - 2) * 128, 128), 128)
            turned[2 * row, :, lanes] = even.T.astype(BF16)
            turned[2 * row + 1, :, lanes] = odd.T.astype(BF16)

    @pl.loop(2, 6)
    def _(at):
        hidden_tile(frames.at[at - 2, 0], at, 0, True)
        hidden_tile(frames.at[at - 2, 1], at, 1, True)

    for copy, step in zip(g_outer, order[1:]):
        copy.wait_recv()
        g_inner += hop_two(middle, landed, gs_sem, step)
    landed[:, slab] = middle[:, slab]
    spread[...] = jnp.zeros_like(spread)
    gain_sum[...] = jnp.zeros_like(gain_sum)
    weight_in.wait()
    for copy in g_inner:
        copy.wait_recv()

    def put_grad(frame, half, value):
        grad[pl.ds(frame * 128, 128), pl.ds(half * 128, 128)] = value

    weave(landed, put_grad)
    only(has_past, grad_late.start)
    only(has_below, above_own.start)

    def step_on(which, source, frames_at):
        for at in frames_at:
            where = pl.ds(at * 128, 128)
            moved = pltpu.roll(source[where, :].astype(F32), 1, 0)
            grad_next[which, where, :] = jnp.where(row_at == 0, 0.0, moved).astype(BF16)

    def weight_taps(chunk):
        for tap in range(chunk * TAPS, min(27, chunk * TAPS + TAPS)):
            tap_t, tap_r, tap_c = tap // 9, tap // 3 % 3, tap % 3
            where = pl.ds((2 - tap_t) * 128, 512)
            left = turned[2 * (tap_r % 2) + tap_c % 2]
            if tap_c == 2:
                right = grad_next[1 if tap_r == 2 else 0, where, :]
            else:
                right = (grad_above if tap_r == 2 else grad)[where, :]
            product = dot_nn(left, right).astype(BF16)
            parts[0, tap] = product[:, :128]
            parts[1, tap] = product[:, 128:]

    pair = {}

    def pair_send(chunk):
        spots = pl.ds(chunk * TAPS, TAPS)
        pair[chunk] = send(parts.at[1 - core, spots], other.at[spots], core_sem, (chunk,), sibling)

    def axes_of(chunk):
        return ("y", "x") if chunk % 2 == 0 else ("x", "y")

    def here(axis, step):
        return (y + step) % NY if axis == "y" else (x + step) % NX

    def piece(ref, chunk, stage, at, taps):
        if stage == 0 and axes_of(chunk)[0] == "x":
            return ref.at[chunk, taps, slice(None), at]
        return ref.at[chunk, taps, at]

    FIRST, LAST, ALL = pl.ds(0, 2), pl.ds(2, 2), pl.ds(0, 4)
    banks = (
        (mine, first_plus, first_minus, second_plus, second_minus, ring_sem, BF16),
        (mid, first_plus2, first_minus2, second_plus2, second_minus2, ring2_sem, F32),
    )

    def ring_open(chunk, stage):
        source, plus, minus, _, _, sems, _ = banks[stage]
        axis = axes_of(chunk)[stage]
        far = here(axis, 2)
        return [
            send(piece(source, chunk, stage, far, FIRST), plus.at[chunk], sems, (chunk, 0), along(axis, 1)),
            send(piece(source, chunk, stage, far, LAST), minus.at[chunk], sems, (chunk, 1), along(axis, 3)),
        ]

    def ring_next(chunk, stage, opened):
        source, plus, minus, plus_in, minus_in, sems, kind = banks[stage]
        axis = axes_of(chunk)[stage]
        opened[0].wait_recv()
        ahead = piece(source, chunk, stage, here(axis, 1), FIRST)
        ahead[...] = (ahead[...].astype(F32) + plus[chunk].astype(F32)).astype(kind)
        one = send(piece(source, chunk, stage, here(axis, 1), ALL), plus_in.at[chunk], sems, (chunk, 2), along(axis, 1))
        opened[1].wait_recv()
        behind = piece(source, chunk, stage, here(axis, 3), LAST)
        behind[...] = (behind[...].astype(F32) + minus[chunk].astype(F32)).astype(kind)
        two = send(piece(source, chunk, stage, here(axis, 3), ALL), minus_in.at[chunk], sems, (chunk, 3), along(axis, 3))
        return [one, two]

    def ring_close(chunk, stage, sent):
        source, _, _, plus_in, minus_in, _, _ = banks[stage]
        axis = axes_of(chunk)[stage]
        sent[0].wait_recv()
        sent[1].wait_recv()
        own = piece(source, chunk, stage, here(axis, 0), ALL)[...].astype(F32)
        summed = own + plus_in[chunk].astype(F32) + minus_in[chunk].astype(F32)
        if stage == 0:
            mid[chunk] = summed
        else:
            low[chunk] = summed.reshape(NZ, 8, 128)

    shares = {}

    def to_owners(chunk):
        shares[chunk] = [
            send(low.at[chunk, (z + step) % NZ], arrive.at[step, chunk], z_sem, (chunk, step), along("z", step))
            for step in order[1:]
        ]

    opened, sent, opened2, sent2 = {}, {}, {}, {}

    def pair_close(chunk):
        pair[chunk].wait_recv()
        spots = pl.ds(chunk * TAPS, TAPS)
        summed = parts[core, spots].astype(F32) + other[spots].astype(F32)
        mine[chunk] = summed.astype(BF16).reshape(TAPS, NY, NX, 16, 128)
        opened[chunk] = ring_open(chunk, 0)

    def next_one(*chunks):
        for chunk in chunks:
            sent[chunk] = ring_next(chunk, 0, opened[chunk])

    def close_one(*chunks):
        for chunk in chunks:
            ring_close(chunk, 0, sent[chunk])
            opened2[chunk] = ring_open(chunk, 1)

    def next_two(*chunks):
        for chunk in chunks:
            sent2[chunk] = ring_next(chunk, 1, opened2[chunk])

    def close_two(*chunks):
        for chunk in chunks:
            ring_close(chunk, 1, sent2[chunk])
            to_owners(chunk)

    step_on(0, grad, range(4))
    weight_taps(5)
    pair_send(5)
    only(has_past, early_on.wait_recv)
    only(has_above, below_early.start)

    @pl.loop(0, 2)
    def _(at):
        hidden_tile(early.at[at, 0], at, 0, False)
        hidden_tile(early.at[at, 1], at, 1, False)

    pair_close(5)
    only(has_future, grad_late.wait_recv)
    only(has_below, above_late.start)
    step_on(0, grad, (4, 5))
    weight_taps(0)
    pair_send(0)
    only(has_above, above_own.wait_recv, above_late.wait_recv)
    step_on(1, grad_above, range(6))
    before = 0
    parts[:, 27] = jnp.zeros((2, 256, 128), BF16)
    for chunk in (3, 1, 2, 4, 6):
        weight_taps(chunk)
        pair_send(chunk)
        pair_close(before)
        before = chunk

    def back_taps(tap):
        where = pl.ds((2 - tap) * 128, 512)
        here_g, here_next = grad[where, :], grad_next[0, where, :]
        above, above_next = grad_above[where, :], grad_next[1, where, :]
        spread[0] += dot_nt(here_g, weight[tap, 0]) + dot_nt(here_next, weight[tap, 2])
        spread[0] += dot_nt(above, weight[tap, 6]) + dot_nt(above_next, weight[tap, 8])
        spread[1] += dot_nt(here_g, weight[tap, 1]) + dot_nt(above, weight[tap, 7])
        spread[2] += dot_nt(here_g, weight[tap, 3]) + dot_nt(here_next, weight[tap, 5])
        spread[3] += dot_nt(here_g, weight[tap, 4])

    def frame_back(first, last):
        @pl.loop(first, last)
        def _(at):
            where = pl.ds(pl.multiple_of(at * 128, 128), 128)
            for row in range(2):
                for half in range(2):
                    lanes = pl.ds(half * 128, 128)
                    tile[row, half, pl.ds(0, 128, stride=2), :] = spread[2 * row, where, lanes]
                    tile[row, half, pl.ds(1, 128, stride=2), :] = spread[2 * row + 1, where, lanes]
                for piece_at in range(4):
                    rows = pl.ds(piece_at * 64, 64)
                    signal = frames[at, row, rows, :].astype(F32)
                    inv = inverse_rms(signal)
                    unit = signal * inv
                    normed = unit * gain_row
                    sigma = 1.0 / (1.0 + jnp.exp(-normed))
                    arrived = jnp.concatenate([tile[row, half, rows, :] for half in range(2)], axis=1)
                    normed_grad = arrived * sigma * (1.0 + normed * (1.0 - sigma))
                    gain_sum[...] += jnp.sum((normed_grad * unit).reshape(8, 8, 256), axis=0)
                    unit_grad = normed_grad * gain_row
                    mean = jnp.mean(unit_grad * unit, axis=-1, keepdims=True)
                    frames_grad[at, row, rows, :] = (inv * (unit_grad - unit * mean)).astype(BF16)

    def spread_out(source, bank, me, axis, total_at, stage):
        bank[me] = source
        return [
            send(bank.at[me], bank.at[me], note_sem, (stage, step), along(axis, step)) for step in range(1, total_at)
        ]

    def collect(copies, bank, total_at):
        for copy in copies:
            copy.wait_recv()
        value = bank[0]
        for at in range(1, total_at):
            value = value + bank[at]
        return value

    back_taps(0)
    pair_close(before)
    back_taps(1)
    next_one(5, 0)
    back_taps(2)
    next_one(3, 1)
    frame_back(0, 2)
    next_one(2, 4)
    frame_back(2, 4)
    frames_out = pltpu.make_async_copy(frames_grad, frames_grad_far, out_sem.at[0])
    frames_out.start()
    gain_local = jnp.sum(gain_sum[...], axis=0, keepdims=True)
    bias_local = jnp.sum(grad[pl.ds(0, 512), :].astype(F32), axis=0, keepdims=True)
    spot = lax.broadcasted_iota(jnp.int32, (8, 256), 0)
    small = jnp.where(spot == 0, gain_local, jnp.where(spot == 1, bias_local, 0.0))
    note[0] = small[:, :128]
    note[1] = small[:, 128:]
    notes = [send(note.at[1 - core], note_pair, note_sem, (0, 1), sibling)]
    next_one(6)
    close_one(5, 0, 3, 1)
    notes[0].wait_recv()
    notes_y = spread_out(note[core] + note_pair[...], note_y, y, "y", NY, 1)
    only(has_below, below_own.wait_recv, below_early.wait_recv)

    @pl.loop(0, 6)
    def _(at):
        hidden_tile(below.at[at], at, 2, False)

    close_one(2, 4, 6)
    next_two(5, 0, 3, 1)
    notes_x = spread_out(collect(notes_y, note_y, NY), note_x, x, "x", NX, 2)
    spread[0] = jnp.broadcast_to(bias[...], (512, 256))

    @pl.loop(0, 3)
    def _(tap):
        where = pl.ds(pl.multiple_of(tap * 128, 128), 512)
        spread[0] += dot_nn(columns[where, :], weight[tap].reshape(2304, 256))

    next_two(2, 4, 6)
    close_two(5, 0, 3, 1)
    for frame in range(4):
        for half in range(2):
            woven[frame, half] = spread[0, pl.ds(frame * 128, 128), pl.ds(half * 128, 128)]
    unweave(latent_in)
    close_two(2, 4, 6)
    outer = hop_one(latent_in, latent_mid, lz_sem)
    latent_mid[z] = latent_in[z]
    inner = hop_two(latent_mid, latent_out, ls_sem, 0)
    notes_z = spread_out(collect(notes_x, note_x, NX), note_z, z, "z", NZ, 3)
    started = list(pair.values()) + g_outer + g_inner + notes + notes_y + notes_x + notes_z
    for table in (opened, sent, opened2, sent2, shares):
        for chunk in range(CHUNKS):
            started += table[chunk]

    for chunk in (5, 0, 3, 1, 2, 4, 6):
        summed = low[chunk, z]
        for copy, step in zip(shares[chunk], order[1:]):
            copy.wait_recv()
            summed += arrive[step, chunk]
        total[z, chunk] = summed.astype(BF16)

    def back(step):
        return copy_to(total.at[z], total.at[z], zback_sem, (step,), along("z", step))

    for step in order[1:]:
        back(step).start()

    right, left, across = (x + 1) % NX, (x + 3) % NX, (x + 2) % NX
    HALF, REST = pl.ds(0, 4), pl.ds(4, 3)

    def to_right(step, at):
        return copy_to(total.at[at], block.at[x, at], x_sem, (0, step), along("x", 1))

    def to_left(step, at):
        return copy_to(total.at[at], block.at[x, at], x_sem, (1, step), along("x", 3))

    def on_right(step, at):
        half = block.at[left, at, HALF]
        return copy_to(half, half, x_sem, (2, step), along("x", 1))

    def on_left(step, at):
        half = block.at[right, at, REST]
        return copy_to(half, half, x_sem, (3, step), along("x", 3))

    def across_core(which, step, at):
        source = total.at[at] if which == 0 else block.at[(left, right, across)[which - 1], at]
        where = (x, left, right, across)[which]
        return copy_to(source, sib.at[where, at], pair_sem, (which, step), sibling)

    def each(body):
        for step in order:
            body(step, (z - step + NZ) % NZ)

    def fan_one(step, at):
        if step:
            back(step).wait_recv()
        to_right(step, at).start()
        to_left(step, at).start()
        across_core(0, step, at).start()

    def fan_two(step, at):
        to_right(step, at).wait_recv()
        on_right(step, at).start()
        across_core(1, step, at).start()
        to_left(step, at).wait_recv()
        on_left(step, at).start()
        across_core(2, step, at).start()

    def fan_three(step, at):
        on_right(step, at).wait_recv()
        on_left(step, at).wait_recv()
        across_core(3, step, at).start()

    def keep(source, half, where, at):
        copy = pltpu.make_async_copy(source, result.at[half, where], out_sem.at[at])
        copy.start()
        return copy

    each(fan_one)
    kept = [frames_out, keep(total, core, x, 1)]
    for copy, step in zip(outer, order[1:]):
        copy.wait_recv()
        inner += hop_two(latent_mid, latent_out, ls_sem, step)
    latent_out[:, slab] = latent_mid[:, slab]
    note_end[0] = collect(notes_z, note_z, NZ)
    note_last = send(note_end.at[0], note_end.at[1], note_sem, (0, 2), sibling)
    each(fan_two)
    kept += [keep(block.at[left], core, left, 2), keep(block.at[right], core, right, 3)]
    for copy in inner:
        copy.wait_recv()

    def put_latent(frame, half, value):
        latent[frame, :, pl.ds(half * 128, 128)] = value

    weave(latent_out, put_latent)
    kept.append(pltpu.make_async_copy(latent, latent_far, out_sem.at[4]))
    kept[-1].start()
    each(fan_three)
    kept.append(keep(block.at[across], core, across, 5))
    note_last.wait()
    note_out[core] = note_end[0]
    note_out[1 - core] = note_end[1]
    for which, where in enumerate((x, left, right, across)):
        for step in order:
            across_core(which, step, (z - step + NZ) % NZ).wait_recv()
        kept.append(keep(sib.at[where], 1 - core, where, 6 + which))
    for copy in started + outer + inner:
        copy.wait_send()
    for step in order:
        at = (z - step + NZ) % NZ
        for which in range(4):
            across_core(which, step, at).wait_send()
        to_right(step, at).wait_send()
        to_left(step, at).wait_send()
        on_right(step, at).wait_send()
        on_left(step, at).wait_send()
    only(has_future, early_on.wait_send)
    only(has_above, below_own.wait_send, below_early.wait_send)
    only(has_past, grad_late.wait_send)
    only(has_below, above_own.wait_send, above_late.wait_send)
    for step in order[1:]:
        back(step).wait_send()
    for copy in kept:
        copy.wait()


def whole(latent_grad, frames, gain, weight, bias):
    dma, vmem = pltpu.SemaphoreType.DMA, pltpu.VMEM
    inside, far = pl.BlockSpec(memory_space=pltpu.VMEM), pl.BlockSpec(memory_space=pl.ANY)
    return pl.pallas_call(
        whole_kernel,
        out_shape=(
            jax.ShapeDtypeStruct((4, 2, 256, 256), BF16),
            jax.ShapeDtypeStruct((4, 128, 256), BF16),
            jax.ShapeDtypeStruct((2, NX, NZ, CHUNKS, 8, 128), BF16),
            jax.ShapeDtypeStruct((2, 8, 128), F32),
        ),
        in_specs=[far, far, inside, far, inside],
        out_specs=[far, far, far, inside],
        scratch_shapes=[
            vmem((4, 64, 2, 256), BF16),
            vmem((4, 2, 256, 256), BF16),
            vmem((4, 2, 256, 256), BF16),
            vmem((4, 128, 256), BF16),
            vmem((NX, NZ, CHUNKS, 8, 128), BF16),
            vmem((2, 8, 128), F32),
            vmem((8, 128), F32),
            vmem((NY, 8, 128), F32),
            vmem((NX, 8, 128), F32),
            vmem((NZ, 8, 128), F32),
            vmem((2, 8, 128), F32),
            vmem((3, 9, 256, 256), BF16),
            vmem((NZ, 2 * NX, 8, 256), BF16),
            vmem((NZ, 2 * NX, 8, 256), BF16),
            vmem((NZ, 2 * NX, 8, 256), BF16),
            vmem((2, 512, 128), F32),
            vmem((4, 2, 128, 128), F32),
            vmem((768, 256), BF16),
            vmem((768, 256), BF16),
            vmem((2, 2, 256, 256), BF16),
            vmem((6, 256, 256), BF16),
            vmem((768, 2304), BF16),
            vmem((4, 256, 512), BF16),
            vmem((2, 768, 256), BF16),
            vmem((4, 512, 256), F32),
            vmem((3, 2, 256, 128), F32),
            vmem((8, 256), F32),
            vmem((2, 28, 256, 128), BF16),
            vmem((CHUNKS * TAPS, 256, 128), BF16),
            vmem((CHUNKS, TAPS, NY, NX, 16, 128), BF16),
            vmem((CHUNKS, 2, 4, 16, 128), BF16),
            vmem((CHUNKS, 2, 4, 16, 128), BF16),
            vmem((CHUNKS, TAPS, 4, 16, 128), BF16),
            vmem((CHUNKS, TAPS, 4, 16, 128), BF16),
            vmem((CHUNKS, TAPS, 4, 16, 128), F32),
            vmem((CHUNKS, 2, 16, 128), F32),
            vmem((CHUNKS, 2, 16, 128), F32),
            vmem((CHUNKS, TAPS, 16, 128), F32),
            vmem((CHUNKS, TAPS, 16, 128), F32),
            vmem((CHUNKS, NZ, 8, 128), F32),
            vmem((NZ, CHUNKS, 8, 128), F32),
            vmem((NZ, CHUNKS, 8, 128), BF16),
            vmem((NX, NZ, CHUNKS, 8, 128), BF16),
            vmem((NZ, 2 * NX, 8, 256), BF16),
            vmem((NZ, 2 * NX, 8, 256), BF16),
            vmem((NZ, 2 * NX, 8, 256), BF16),
            dma((3,)),
            dma((2, NZ)),
            dma((2, NZ, 2 * NX)),
            dma((2, 6)),
            dma((2, CHUNKS)),
            dma((2, CHUNKS, 4)),
            dma((2, CHUNKS, 4)),
            dma((2, CHUNKS, NZ)),
            dma((2, NZ)),
            dma((2, 4, NZ)),
            dma((2, 4, NZ)),
            dma((2, NZ)),
            dma((2, NZ, 2 * NX)),
            dma((2, 4, NZ)),
            dma((10,)),
        ],
        compiler_params=pltpu.CompilerParams(collective_id=1, has_side_effects=True),
        cost_estimate=pl.CostEstimate(flops=5_500_000_000, bytes_accessed=12_000_000, transcendentals=2_000_000),
    )(latent_grad, frames, gain, weight, bias)


def finish_kernel(
    total_far, frames_far, latent_far, note, weight_grad, frames_grad, latent, gain_grad, bias_grad,
    total, frames_near, latent_near, latent_wide, wide, sems,
):
    copy = pltpu.make_async_copy
    totals_in = [
        copy(total_far.at[:, :, :, chunk], total.at[:, :, :, chunk], sems.at[12 + chunk]) for chunk in range(CHUNKS)
    ]
    frames_in = copy(frames_far, frames_near, sems.at[1])
    latent_in = copy(latent_far, latent_near, sems.at[2])
    latent_in.start()
    for item in totals_in:
        item.start()
    frames_in.start()
    going = []
    for chunk in range(CHUNKS):
        totals_in[chunk].wait()
        for tap in range(chunk * TAPS, min(27, chunk * TAPS + TAPS)):
            for core in range(2):
                for x in range(NX):
                    for side in range(2):
                        part = total[core, x, 2 * (tap % TAPS) + side, chunk]
                        wide[tap, pl.ds(x * 16 + side * 8, 8), pl.ds(core * 128, 128)] = part.astype(F32)
        taps = pl.ds(chunk * TAPS, min(27, chunk * TAPS + TAPS) - chunk * TAPS)
        going.append(copy(wide.at[taps], weight_grad.at[taps], sems.at[3 + chunk]))
        going[-1].start()
        if chunk == 2:
            frames_in.wait()
            going.append(copy(frames_near, frames_grad, sems.at[10]))
            going[-1].start()
        if chunk == 3:
            latent_in.wait()
            for frame in range(4):
                latent_wide[frame] = latent_near[frame].reshape(64, 2, 256)
            going.append(copy(latent_wide, latent, sems.at[11]))
            going[-1].start()
    for core in range(2):
        row = note[core]
        for side in range(2):

            @pl.when(lax.axis_index("tm") == 2 * core + side)
            def _():
                gain_grad[...] = row[0:1, 64 * side : 64 * side + 64]
                bias_grad[...] = row[1:2, 64 * side : 64 * side + 64]

    for item in going:
        item.wait()


def finish(total, frames_grad, latent, note):
    inside, far = pl.BlockSpec(memory_space=pltpu.VMEM), pl.BlockSpec(memory_space=pl.ANY)
    return pl.pallas_call(
        finish_kernel,
        out_shape=(
            jax.ShapeDtypeStruct((27, 64, 256), F32),
            jax.ShapeDtypeStruct((4, 2, 256, 256), BF16),
            jax.ShapeDtypeStruct((4, 64, 2, 256), BF16),
            jax.ShapeDtypeStruct((1, 64), F32),
            jax.ShapeDtypeStruct((1, 64), F32),
        ),
        in_specs=[far] * 3 + [inside],
        out_specs=[far, far, far, inside, inside],
        scratch_shapes=[
            pltpu.VMEM((2, NX, NZ, CHUNKS, 8, 128), BF16),
            pltpu.VMEM((4, 2, 256, 256), BF16),
            pltpu.VMEM((4, 128, 256), BF16),
            pltpu.VMEM((4, 64, 2, 256), BF16),
            pltpu.VMEM((27, 64, 256), F32),
            pltpu.SemaphoreType.DMA((12 + CHUNKS,)),
        ],
    )(total, frames_grad, latent, note)


def on_device(frames, norm_gain, conv_weight, conv_bias, latent_grad):
    frames_grad, latent, total, note = whole(
        latent_grad, frames, norm_gain.reshape(1, 256), conv_weight.reshape(3, 9, 256, 256), conv_bias.reshape(1, 256),
    )
    weight_grad, frames_grad, latent, gain_grad, bias_grad = finish(total, frames_grad, latent, note)
    return (
        latent, frames_grad, weight_grad.reshape(3, 3, 3, 64, 256), gain_grad.reshape(64), bias_grad.reshape(64),
    )


def solution(mesh):
    placed = (P("tm", "rows", None, None), P(), P(), P(), P("tm", None, "rows", None))
    return jax.shard_map(
        on_device,
        mesh=mesh,
        in_specs=placed,
        out_specs=(
            P("tm", None, "rows", None),
            P("tm", "rows", None, None),
            P(None, None, None, "tm", None),
            P("tm"),
            P("tm"),
        ),
        check_vma=False,
    )
```

```python
import jax
import jax.numpy as jnp
from jax import lax
from jax.experimental import pallas as pl
from jax.experimental.pallas import tpu as pltpu
from jax.sharding import PartitionSpec as P

F32 = jnp.float32
BF16 = jnp.bfloat16
MESH = pl.DeviceIdType.MESH
EPS = 1e-06
NX, NZ, NY = 4, 8, 4
CHUNKS, TAPS = 7, 4


def dot_nt(left, right):
    return lax.dot_general(left, right, (((1,), (1,)), ((), ())), preferred_element_type=F32)


def dot_nn(left, right):
    return lax.dot_general(left, right, (((1,), (0,)), ((), ())), preferred_element_type=F32)


def inverse_rms(signal):
    return lax.rsqrt(jnp.mean(signal * signal, axis=-1, keepdims=True) + EPS)


def whole_kernel(
    latent_grad_far, frames_far, gain, weight_far, bias,
    frames_grad_far, latent_far, result, note_out,
    latent_grad, frames, frames_grad, latent, sib, note, note_pair, note_y, note_x, note_z, note_end,
    weight, blocks, middle, landed, flat, woven, grad, grad_above, early, below,
    columns, turned, grad_next, spread, tile, gain_sum, parts,
    other, mine, first_plus, first_minus, second_plus, second_minus,
    mid, first_plus2, first_minus2, second_plus2, second_minus2,
    low, arrive, total, block, latent_in, latent_mid, latent_out,
    weight_sem, send_sems, near_in, gz_in, gs_in, core_in, ring_in, ring2_in, z_in, zback_in, x_in, pair_in,
    lz_in, ls_in, note_in, out_sem,
):
    gz_sem, gs_sem, core_sem, ring_sem, ring2_sem, z_sem = (
        (0, gz_in), (1, gs_in), (2, core_in), (3, ring_in), (4, ring2_in), (5, z_in),
    )
    zback_sem, x_sem, pair_sem, lz_sem, ls_sem, note_sem, near_sem = (
        (6, zback_in), (7, x_in), (8, pair_in), (9, lz_in), (10, ls_in), (11, note_in), (16, near_in),
    )
    rows_at = lax.axis_index("rows")
    y = lax.axis_index("tm")
    core, x, z = rows_at % 2, (rows_at // 2) % NX, rows_at // (2 * NX)
    slab = rows_at % (2 * NX)
    count = NZ * 2 * NX

    def row_of(z_at, x_at, core_at):
        return z_at * (2 * NX) + x_at * 2 + core_at

    sibling = (row_of(z, x, 1 - core), y)

    def along(axis, step):
        if axis == "y":
            return (rows_at, (y + step + NY) % NY)
        if axis == "x":
            return (row_of(z, (x + step) % NX, core), y)
        if axis == "slab":
            return (z * (2 * NX) + (slab + step) % (2 * NX), y)
        if axis == "row":
            return ((rows_at + step + count) % count, y)
        return (row_of((z + step) % NZ, x, core), y)

    barrier = pltpu.get_barrier_semaphore()
    friends = [along("z", step) for step in range(1, NZ)] + [along("slab", step) for step in range(1, 2 * NX)]
    friends += [along("y", 1), along("y", 2), along("y", -1), along("row", 1), along("row", -1)]
    for friend in friends:
        pl.semaphore_signal(barrier, inc=1, device_id=friend, device_id_type=MESH)
    latent_grad_in = pltpu.make_async_copy(latent_grad_far, latent_grad, weight_sem.at[1])
    frames_in = pltpu.make_async_copy(frames_far, frames, weight_sem.at[2])
    weight_in = pltpu.make_async_copy(weight_far, weight, weight_sem.at[0])
    latent_grad_in.start()
    frames_in.start()
    weight_in.start()
    latent_grad_in.wait()

    def unweave(target):
        for frame in range(4):
            for half in range(2):
                for side in range(2):
                    flat[half, pl.ds(2 * frame + side, 64, stride=8), :] = woven[frame, half, pl.ds(side, 64, stride=2), :]
        for half in range(2):
            target[:, :, :, pl.ds(half * 128, 128)] = flat[half].reshape(NZ, 2 * NX, 8, 128).astype(BF16)

    def weave(source, put):
        for half in range(2):
            flat[half] = source[:, :, :, pl.ds(half * 128, 128)].astype(F32).reshape(512, 128)
        for frame in range(4):
            for half in range(2):
                for side in range(2):
                    woven[frame, half, pl.ds(side, 64, stride=2), :] = flat[half, pl.ds(2 * frame + side, 64, stride=8), :]
                put(frame, half, woven[frame, half].astype(BF16))

    for frame in range(4):
        for half in range(2):
            woven[frame, half] = latent_grad[frame, :, :, pl.ds(half * 128, 128)].reshape(128, 128).astype(F32)
    unweave(blocks)

    pl.semaphore_wait(barrier, len(friends))

    def copy_to(source, target, sems, at, device):
        family, arrivals = sems
        if family == 11 or family == 16:
            family += at[0]
        return pltpu.make_async_remote_copy(
            src_ref=source, dst_ref=target, send_sem=send_sems.at[family], recv_sem=arrivals.at[at],
            device_id=device, device_id_type=MESH,
        )

    def taken(sem, ref):
        pltpu.make_async_remote_copy(
            src_ref=ref, dst_ref=ref, send_sem=sem, recv_sem=sem, device_id=sibling, device_id_type=MESH
        ).wait_recv()

    def send(*args):
        copy = copy_to(*args)
        copy.start()
        return copy

    ahead, own, late = pl.ds(0, 256), pl.ds(0, 512), pl.ds(512, 256)
    early_on = copy_to(frames.at[pl.ds(2, 2)], early, near_sem, (0,), along("y", 1))
    below_own = copy_to(frames.at[:, 0], below.at[pl.ds(2, 4)], near_sem, (1,), along("row", -1))
    below_early = copy_to(early.at[:, 0], below.at[pl.ds(0, 2)], near_sem, (2,), along("row", -1))
    grad_late = copy_to(grad.at[ahead], grad.at[late], near_sem, (3,), along("y", -1))
    above_own = copy_to(grad.at[own], grad_above.at[own], near_sem, (4,), along("row", 1))
    above_late = copy_to(grad.at[late], grad_above.at[late], near_sem, (5,), along("row", 1))
    has_past, has_future = y > 0, y < NY - 1
    has_above, has_below = rows_at > 0, rows_at < count - 1

    def only(condition, *actions):
        @pl.when(condition)
        def _():
            for action in actions:
                action()

    order = (0, 1, 7, 2, 6, 3, 5, 4)

    def hop_one(source, between, sems):
        return [
            send(source.at[(z + step) % NZ], between.at[z], sems, (step,), along("z", step)) for step in order[1:]
        ]

    def hop_two(between, target, sems, step):
        at = (z - step + NZ) % NZ
        return [
            send(between.at[at, (slab + move) % (2 * NX)], target.at[at, slab], sems, (0,), along("slab", move))
            for move in range(1, 2 * NX)
        ]

    g_outer = hop_one(blocks, middle, gz_sem)
    frames_in.wait()
    only(has_future, early_on.start)
    only(has_above, below_own.start)
    middle[z] = blocks[z]
    g_inner = hop_two(middle, landed, gs_sem, 0)

    @pl.when(jnp.logical_not(has_past))
    def _():
        early[...] = jnp.zeros_like(early)

    @pl.when(jnp.logical_not(has_below))
    def _():
        below[...] = jnp.zeros_like(below)

    @pl.when(jnp.logical_not(has_above))
    def _():
        grad_above[...] = jnp.zeros_like(grad_above)

    @pl.when(jnp.logical_not(has_future))
    def _():
        grad[late, :] = jnp.zeros((256, 256), BF16)

    gain_row = gain[...]
    row_at = lax.broadcasted_iota(jnp.int32, (128, 256), 0)

    def hidden_tile(source, at, row, keep):
        for piece_at in range(4):
            rows = pl.ds(piece_at * 64, 64)
            signal = source[rows, :].astype(F32)
            normed = signal * inverse_rms(signal) * gain_row
            hidden = normed / (1.0 + jnp.exp(-normed))
            tile[row, 0, rows, :] = hidden[:, :128]
            tile[row, 1, rows, :] = hidden[:, 128:]
        even = jnp.concatenate([tile[row, half, pl.ds(0, 128, stride=2), :] for half in range(2)], axis=1)
        odd = jnp.concatenate([tile[row, half, pl.ds(1, 128, stride=2), :] for half in range(2)], axis=1)
        after = jnp.where(row_at == 127, 0.0, pltpu.roll(even, 127, 0))
        where = pl.ds(pl.multiple_of(at * 128, 128), 128)
        columns[where, pl.ds(row * 768, 256)] = even.astype(BF16)
        columns[where, pl.ds(row * 768 + 256, 256)] = odd.astype(BF16)
        columns[where, pl.ds(row * 768 + 512, 256)] = after.astype(BF16)
        if keep:
            lanes = pl.ds(pl.multiple_of((at - 2) * 128, 128), 128)
            turned[2 * row, :, lanes] = even.T.astype(BF16)
            turned[2 * row + 1, :, lanes] = odd.T.astype(BF16)

    @pl.loop(2, 6)
    def _(at):
        hidden_tile(frames.at[at - 2, 0], at, 0, True)
        hidden_tile(frames.at[at - 2, 1], at, 1, True)

    for copy, step in zip(g_outer, order[1:]):
        copy.wait_recv()
        g_inner += hop_two(middle, landed, gs_sem, step)
    landed[:, slab] = middle[:, slab]
    spread[...] = jnp.zeros_like(spread)
    gain_sum[...] = jnp.zeros_like(gain_sum)
    weight_in.wait()
    taken(gs_in.at[0], landed.at[pl.ds(0, 7)])

    def put_grad(frame, half, value):
        grad[pl.ds(frame * 128, 128), pl.ds(half * 128, 128)] = value

    weave(landed, put_grad)
    only(has_past, grad_late.start)
    only(has_below, above_own.start)

    def step_on(which, source, frames_at):
        for at in frames_at:
            where = pl.ds(at * 128, 128)
            moved = pltpu.roll(source[where, :].astype(F32), 1, 0)
            grad_next[which, where, :] = jnp.where(row_at == 0, 0.0, moved).astype(BF16)

    def weight_taps(chunk):
        for tap in range(chunk * TAPS, min(27, chunk * TAPS + TAPS)):
            tap_t, tap_r, tap_c = tap // 9, tap // 3 % 3, tap % 3
            where = pl.ds((2 - tap_t) * 128, 512)
            left = turned[2 * (tap_r % 2) + tap_c % 2]
            if tap_c == 2:
                right = grad_next[1 if tap_r == 2 else 0, where, :]
            else:
                right = (grad_above if tap_r == 2 else grad)[where, :]
            product = dot_nn(left, right).astype(BF16)
            parts[0, tap] = product[:, :128]
            parts[1, tap] = product[:, 128:]

    pair = {}

    def pair_send(chunk):
        spots = pl.ds(chunk * TAPS, TAPS)
        pair[chunk] = send(parts.at[1 - core, spots], other.at[spots], core_sem, (chunk,), sibling)

    def axes_of(chunk):
        return ("y", "x") if chunk % 2 == 0 else ("x", "y")

    def here(axis, step):
        return (y + step) % NY if axis == "y" else (x + step) % NX

    def piece(ref, chunk, stage, at, taps):
        if stage == 0 and axes_of(chunk)[0] == "x":
            return ref.at[chunk, taps, slice(None), at]
        return ref.at[chunk, taps, at]

    FIRST, LAST, ALL = pl.ds(0, 2), pl.ds(2, 2), pl.ds(0, 4)
    banks = (
        (mine, first_plus, first_minus, second_plus, second_minus, ring_sem, BF16),
        (mid, first_plus2, first_minus2, second_plus2, second_minus2, ring2_sem, F32),
    )

    def ring_open(chunk, stage):
        source, plus, minus, _, _, sems, _ = banks[stage]
        axis = axes_of(chunk)[stage]
        far = here(axis, 2)
        return [
            send(piece(source, chunk, stage, far, FIRST), plus.at[chunk], sems, (chunk, 0), along(axis, 1)),
            send(piece(source, chunk, stage, far, LAST), minus.at[chunk], sems, (chunk, 1), along(axis, 3)),
        ]

    def ring_next(chunk, stage, opened):
        source, plus, minus, plus_in, minus_in, sems, kind = banks[stage]
        axis = axes_of(chunk)[stage]
        opened[0].wait_recv()
        ahead = piece(source, chunk, stage, here(axis, 1), FIRST)
        ahead[...] = (ahead[...].astype(F32) + plus[chunk].astype(F32)).astype(kind)
        one = send(piece(source, chunk, stage, here(axis, 1), ALL), plus_in.at[chunk], sems, (chunk, 2), along(axis, 1))
        opened[1].wait_recv()
        behind = piece(source, chunk, stage, here(axis, 3), LAST)
        behind[...] = (behind[...].astype(F32) + minus[chunk].astype(F32)).astype(kind)
        two = send(piece(source, chunk, stage, here(axis, 3), ALL), minus_in.at[chunk], sems, (chunk, 3), along(axis, 3))
        return [one, two]

    def ring_close(chunk, stage, sent):
        source, _, _, plus_in, minus_in, _, _ = banks[stage]
        axis = axes_of(chunk)[stage]
        sent[0].wait_recv()
        sent[1].wait_recv()
        own = piece(source, chunk, stage, here(axis, 0), ALL)[...].astype(F32)
        summed = own + plus_in[chunk].astype(F32) + minus_in[chunk].astype(F32)
        if stage == 0:
            mid[chunk] = summed
        else:
            low[chunk] = summed.reshape(NZ, 8, 128)

    shares = {}

    def to_owners(chunk):
        shares[chunk] = [
            send(low.at[chunk, (z + step) % NZ], arrive.at[step, chunk], z_sem, (chunk,), along("z", step))
            for step in order[1:]
        ]

    opened, sent, opened2, sent2 = {}, {}, {}, {}

    def pair_close(chunk):
        pair[chunk].wait_recv()
        spots = pl.ds(chunk * TAPS, TAPS)
        summed = parts[core, spots].astype(F32) + other[spots].astype(F32)
        mine[chunk] = summed.astype(BF16).reshape(TAPS, NY, NX, 16, 128)
        opened[chunk] = ring_open(chunk, 0)

    def next_one(*chunks):
        for chunk in chunks:
            sent[chunk] = ring_next(chunk, 0, opened[chunk])

    def close_one(*chunks):
        for chunk in chunks:
            ring_close(chunk, 0, sent[chunk])
            opened2[chunk] = ring_open(chunk, 1)

    def next_two(*chunks):
        for chunk in chunks:
            sent2[chunk] = ring_next(chunk, 1, opened2[chunk])

    def close_two(*chunks):
        for chunk in chunks:
            ring_close(chunk, 1, sent2[chunk])
            to_owners(chunk)

    step_on(0, grad, range(4))
    weight_taps(5)
    pair_send(5)
    only(has_past, early_on.wait_recv)
    only(has_above, below_early.start)

    @pl.loop(0, 2)
    def _(at):
        hidden_tile(early.at[at, 0], at, 0, False)
        hidden_tile(early.at[at, 1], at, 1, False)

    pair_close(5)
    only(has_future, grad_late.wait_recv)
    only(has_below, above_late.start)
    step_on(0, grad, (4, 5))
    weight_taps(0)
    pair_send(0)
    only(has_above, above_own.wait_recv, above_late.wait_recv)
    step_on(1, grad_above, range(6))
    before = 0
    parts[:, 27] = jnp.zeros((2, 256, 128), BF16)
    for chunk in (3, 1, 2, 4, 6):
        weight_taps(chunk)
        pair_send(chunk)
        pair_close(before)
        before = chunk

    def back_taps(tap):
        where = pl.ds((2 - tap) * 128, 512)
        here_g, here_next = grad[where, :], grad_next[0, where, :]
        above, above_next = grad_above[where, :], grad_next[1, where, :]
        spread[0] += dot_nt(here_g, weight[tap, 0]) + dot_nt(here_next, weight[tap, 2])
        spread[0] += dot_nt(above, weight[tap, 6]) + dot_nt(above_next, weight[tap, 8])
        spread[1] += dot_nt(here_g, weight[tap, 1]) + dot_nt(above, weight[tap, 7])
        spread[2] += dot_nt(here_g, weight[tap, 3]) + dot_nt(here_next, weight[tap, 5])
        spread[3] += dot_nt(here_g, weight[tap, 4])

    def frame_back(first, last):
        @pl.loop(first, last)
        def _(at):
            where = pl.ds(pl.multiple_of(at * 128, 128), 128)
            for row in range(2):
                for half in range(2):
                    lanes = pl.ds(half * 128, 128)
                    tile[row, half, pl.ds(0, 128, stride=2), :] = spread[2 * row, where, lanes]
                    tile[row, half, pl.ds(1, 128, stride=2), :] = spread[2 * row + 1, where, lanes]
                for piece_at in range(4):
                    rows = pl.ds(piece_at * 64, 64)
                    signal = frames[at, row, rows, :].astype(F32)
                    inv = inverse_rms(signal)
                    unit = signal * inv
                    normed = unit * gain_row
                    sigma = 1.0 / (1.0 + jnp.exp(-normed))
                    arrived = jnp.concatenate([tile[row, half, rows, :] for half in range(2)], axis=1)
                    normed_grad = arrived * sigma * (1.0 + normed * (1.0 - sigma))
                    gain_sum[...] += jnp.sum((normed_grad * unit).reshape(8, 8, 256), axis=0)
                    unit_grad = normed_grad * gain_row
                    mean = jnp.mean(unit_grad * unit, axis=-1, keepdims=True)
                    frames_grad[at, row, rows, :] = (inv * (unit_grad - unit * mean)).astype(BF16)

    def spread_out(source, bank, me, axis, total_at, stage):
        bank[me] = source
        return [
            send(bank.at[me], bank.at[me], note_sem, (stage,), along(axis, step)) for step in range(1, total_at)
        ]

    def collect(stage, bank, total_at):
        taken(note_in.at[stage], bank.at[pl.ds(0, total_at - 1)])
        value = bank[0]
        for at in range(1, total_at):
            value = value + bank[at]
        return value

    back_taps(0)
    pair_close(before)
    back_taps(1)
    next_one(5, 0)
    back_taps(2)
    next_one(3, 1)
    frame_back(0, 2)
    next_one(2, 4)
    frame_back(2, 4)
    frames_out = pltpu.make_async_copy(frames_grad, frames_grad_far, out_sem.at[0])
    frames_out.start()
    gain_local = jnp.sum(gain_sum[...], axis=0, keepdims=True)
    bias_local = jnp.sum(grad[pl.ds(0, 512), :].astype(F32), axis=0, keepdims=True)
    spot = lax.broadcasted_iota(jnp.int32, (8, 256), 0)
    small = jnp.where(spot == 0, gain_local, jnp.where(spot == 1, bias_local, 0.0))
    note[0] = small[:, :128]
    note[1] = small[:, 128:]
    notes = [send(note.at[1 - core], note_pair, note_sem, (0,), sibling)]
    next_one(6)
    only(has_below, below_own.wait_recv, below_early.wait_recv)

    @pl.loop(0, 6)
    def _(at):
        hidden_tile(below.at[at], at, 2, False)

    spread[0] = jnp.broadcast_to(bias[...], (512, 256))

    @pl.loop(0, 3)
    def _(tap):
        where = pl.ds(pl.multiple_of(tap * 128, 128), 512)
        spread[0] += dot_nn(columns[where, :], weight[tap].reshape(2304, 256))

    for frame in range(4):
        for half in range(2):
            woven[frame, half] = spread[0, pl.ds(frame * 128, 128), pl.ds(half * 128, 128)]
    unweave(latent_in)
    outer = hop_one(latent_in, latent_mid, lz_sem)
    latent_mid[z] = latent_in[z]
    hop_two(latent_mid, latent_out, ls_sem, 0)
    close_one(5, 0, 3, 1)
    notes[0].wait_recv()
    spread_out(note[core] + note_pair[...], note_y, y, "y", NY, 1)
    close_one(2, 4, 6)
    next_two(5, 0, 3, 1)
    spread_out(collect(1, note_y, NY), note_x, x, "x", NX, 2)
    next_two(2, 4, 6)
    close_two(5, 0, 3, 1)
    for copy, step in zip(outer, order[1:]):
        copy.wait_recv()
        hop_two(latent_mid, latent_out, ls_sem, step)
    latent_out[:, slab] = latent_mid[:, slab]
    close_two(2, 4, 6)
    spread_out(collect(2, note_x, NX), note_z, z, "z", NZ, 3)
    for chunk in (5, 0, 3, 1, 2, 4, 6):
        summed = low[chunk, z]
        taken(z_in.at[chunk], low.at[0, pl.ds(0, 7)])
        for step in order[1:]:
            summed += arrive[step, chunk]
        total[z, chunk] = summed.astype(BF16)

    def back(step):
        return copy_to(total.at[z], total.at[z], zback_sem, (step,), along("z", step))

    for step in order[1:]:
        back(step).start()

    right, left, across = (x + 1) % NX, (x + 3) % NX, (x + 2) % NX
    HALF, REST = pl.ds(0, 4), pl.ds(4, 3)

    def to_right(step, at):
        return copy_to(total.at[at], block.at[x, at], x_sem, (0, step), along("x", 1))

    def to_left(step, at):
        return copy_to(total.at[at], block.at[x, at], x_sem, (1, step), along("x", 3))

    def on_right(step, at):
        half = block.at[left, at, HALF]
        return copy_to(half, half, x_sem, (2, step), along("x", 1))

    def on_left(step, at):
        half = block.at[right, at, REST]
        return copy_to(half, half, x_sem, (3, step), along("x", 3))

    def across_core(which, step, at):
        source = total.at[at] if which == 0 else block.at[(left, right, across)[which - 1], at]
        where = (x, left, right, across)[which]
        return copy_to(source, sib.at[where, at], pair_sem, (which,), sibling)

    def each(body):
        for step in order:
            body(step, (z - step + NZ) % NZ)

    def fan_one(step, at):
        if step:
            back(step).wait_recv()
        to_right(step, at).start()
        to_left(step, at).start()
        across_core(0, step, at).start()

    def fan_two(step, at):
        to_right(step, at).wait_recv()
        on_right(step, at).start()
        across_core(1, step, at).start()
        to_left(step, at).wait_recv()
        on_left(step, at).start()
        across_core(2, step, at).start()

    def fan_three(step, at):
        on_right(step, at).wait_recv()
        on_left(step, at).wait_recv()
        across_core(3, step, at).start()

    def keep(source, half, where, at):
        copy = pltpu.make_async_copy(source, result.at[half, where], out_sem.at[at])
        copy.start()
        return copy

    each(fan_one)
    kept = [frames_out, keep(total, core, x, 1)]
    note_end[0] = collect(3, note_z, NZ)
    note_last = send(note_end.at[0], note_end.at[1], note_sem, (4,), sibling)
    each(fan_two)
    kept += [keep(block.at[left], core, left, 2), keep(block.at[right], core, right, 3)]
    taken(ls_in.at[0], latent_out.at[pl.ds(0, 7)])

    def put_latent(frame, half, value):
        latent[frame, :, pl.ds(half * 128, 128)] = value

    weave(latent_out, put_latent)
    kept.append(pltpu.make_async_copy(latent, latent_far, out_sem.at[4]))
    kept[-1].start()
    each(fan_three)
    kept.append(keep(block.at[across], core, across, 5))
    note_last.wait_recv()
    note_out[core] = note_end[0]
    note_out[1 - core] = note_end[1]
    for which, where in enumerate((x, left, right, across)):
        taken(pair_in.at[which], sib.at[0])
        kept.append(keep(sib.at[where], 1 - core, where, 6 + which))
    seven, three = pl.ds(0, 7), pl.ds(0, 3)
    for family, ref in (
        (0, middle.at[seven]), (1, landed.at[seven]), (2, other), (3, mine.at[:, three]), (4, mid.at[:, three]),
        (5, low.at[:, seven]), (6, total.at[seven]), (7, block.at[three]), (8, sib),
        (9, latent_mid.at[seven]), (10, latent_out.at[seven]),
        (11, note_pair), (12, note_y.at[three]), (13, note_x.at[three]), (14, note_z.at[seven]), (15, note_pair),
    ):
        taken(send_sems.at[family], ref)
    only(has_future, early_on.wait_send)
    only(has_above, below_own.wait_send, below_early.wait_send)
    only(has_past, grad_late.wait_send)
    only(has_below, above_own.wait_send, above_late.wait_send)
    for copy in kept:
        copy.wait()


def whole(latent_grad, frames, gain, weight, bias):
    dma, vmem = pltpu.SemaphoreType.DMA, pltpu.VMEM
    inside, far = pl.BlockSpec(memory_space=pltpu.VMEM), pl.BlockSpec(memory_space=pl.ANY)
    return pl.pallas_call(
        whole_kernel,
        out_shape=(
            jax.ShapeDtypeStruct((4, 2, 256, 256), BF16),
            jax.ShapeDtypeStruct((4, 128, 256), BF16),
            jax.ShapeDtypeStruct((2, NX, NZ, CHUNKS, 8, 128), BF16),
            jax.ShapeDtypeStruct((2, 8, 128), F32),
        ),
        in_specs=[far, far, inside, far, inside],
        out_specs=[far, far, far, inside],
        scratch_shapes=[
            vmem((4, 64, 2, 256), BF16),
            vmem((4, 2, 256, 256), BF16),
            vmem((4, 2, 256, 256), BF16),
            vmem((4, 128, 256), BF16),
            vmem((NX, NZ, CHUNKS, 8, 128), BF16),
            vmem((2, 8, 128), F32),
            vmem((8, 128), F32),
            vmem((NY, 8, 128), F32),
            vmem((NX, 8, 128), F32),
            vmem((NZ, 8, 128), F32),
            vmem((2, 8, 128), F32),
            vmem((3, 9, 256, 256), BF16),
            vmem((NZ, 2 * NX, 8, 256), BF16),
            vmem((NZ, 2 * NX, 8, 256), BF16),
            vmem((NZ, 2 * NX, 8, 256), BF16),
            vmem((2, 512, 128), F32),
            vmem((4, 2, 128, 128), F32),
            vmem((768, 256), BF16),
            vmem((768, 256), BF16),
            vmem((2, 2, 256, 256), BF16),
            vmem((6, 256, 256), BF16),
            vmem((768, 2304), BF16),
            vmem((4, 256, 512), BF16),
            vmem((2, 768, 256), BF16),
            vmem((4, 512, 256), F32),
            vmem((3, 2, 256, 128), F32),
            vmem((8, 256), F32),
            vmem((2, 28, 256, 128), BF16),
            vmem((CHUNKS * TAPS, 256, 128), BF16),
            vmem((CHUNKS, TAPS, NY, NX, 16, 128), BF16),
            vmem((CHUNKS, 2, 4, 16, 128), BF16),
            vmem((CHUNKS, 2, 4, 16, 128), BF16),
            vmem((CHUNKS, TAPS, 4, 16, 128), BF16),
            vmem((CHUNKS, TAPS, 4, 16, 128), BF16),
            vmem((CHUNKS, TAPS, 4, 16, 128), F32),
            vmem((CHUNKS, 2, 16, 128), F32),
            vmem((CHUNKS, 2, 16, 128), F32),
            vmem((CHUNKS, TAPS, 16, 128), F32),
            vmem((CHUNKS, TAPS, 16, 128), F32),
            vmem((CHUNKS, NZ, 8, 128), F32),
            vmem((NZ, CHUNKS, 8, 128), F32),
            vmem((NZ, CHUNKS, 8, 128), BF16),
            vmem((NX, NZ, CHUNKS, 8, 128), BF16),
            vmem((NZ, 2 * NX, 8, 256), BF16),
            vmem((NZ, 2 * NX, 8, 256), BF16),
            vmem((NZ, 2 * NX, 8, 256), BF16),
            dma((3,)),
            dma((22,)),
            dma((6,)),
            dma((NZ,)),
            dma((1,)),
            dma((CHUNKS,)),
            dma((CHUNKS, 4)),
            dma((CHUNKS, 4)),
            dma((CHUNKS,)),
            dma((NZ,)),
            dma((4, NZ)),
            dma((4,)),
            dma((NZ,)),
            dma((1,)),
            dma((5,)),
            dma((10,)),
        ],
        compiler_params=pltpu.CompilerParams(collective_id=1, has_side_effects=True),
        cost_estimate=pl.CostEstimate(flops=5_500_000_000, bytes_accessed=12_000_000, transcendentals=2_000_000),
    )(latent_grad, frames, gain, weight, bias)


def finish_kernel(
    total_far, frames_far, latent_far, note, weight_grad, frames_grad, latent, gain_grad, bias_grad,
    total, frames_near, latent_near, latent_wide, wide, sems,
):
    copy = pltpu.make_async_copy
    total_in = copy(total_far, total, sems.at[0])
    frames_in = copy(frames_far, frames_near, sems.at[1])
    latent_in = copy(latent_far, latent_near, sems.at[2])
    total_in.start()
    frames_in.start()
    latent_in.start()
    total_in.wait()
    going = []
    for chunk in range(CHUNKS):
        for tap in range(chunk * TAPS, min(27, chunk * TAPS + TAPS)):
            for core in range(2):
                for x in range(NX):
                    for side in range(2):
                        part = total[core, x, 2 * (tap % TAPS) + side, chunk]
                        wide[tap, pl.ds(x * 16 + side * 8, 8), pl.ds(core * 128, 128)] = part.astype(F32)
        taps = pl.ds(chunk * TAPS, min(27, chunk * TAPS + TAPS) - chunk * TAPS)
        going.append(copy(wide.at[taps], weight_grad.at[taps], sems.at[3 + chunk]))
        going[-1].start()
        if chunk == 2:
            frames_in.wait()
            going.append(copy(frames_near, frames_grad, sems.at[10]))
            going[-1].start()
        if chunk == 3:
            latent_in.wait()
            for frame in range(4):
                latent_wide[frame] = latent_near[frame].reshape(64, 2, 256)
            going.append(copy(latent_wide, latent, sems.at[11]))
            going[-1].start()
    for core in range(2):
        row = note[core]
        for side in range(2):

            @pl.when(lax.axis_index("tm") == 2 * core + side)
            def _():
                gain_grad[...] = row[0:1, 64 * side : 64 * side + 64]
                bias_grad[...] = row[1:2, 64 * side : 64 * side + 64]

    for item in going:
        item.wait()


def finish(total, frames_grad, latent, note):
    inside, far = pl.BlockSpec(memory_space=pltpu.VMEM), pl.BlockSpec(memory_space=pl.ANY)
    return pl.pallas_call(
        finish_kernel,
        out_shape=(
            jax.ShapeDtypeStruct((27, 64, 256), F32),
            jax.ShapeDtypeStruct((4, 2, 256, 256), BF16),
            jax.ShapeDtypeStruct((4, 64, 2, 256), BF16),
            jax.ShapeDtypeStruct((1, 64), F32),
            jax.ShapeDtypeStruct((1, 64), F32),
        ),
        in_specs=[far] * 3 + [inside],
        out_specs=[far, far, far, inside, inside],
        scratch_shapes=[
            pltpu.VMEM((2, NX, NZ, CHUNKS, 8, 128), BF16),
            pltpu.VMEM((4, 2, 256, 256), BF16),
            pltpu.VMEM((4, 128, 256), BF16),
            pltpu.VMEM((4, 64, 2, 256), BF16),
            pltpu.VMEM((27, 64, 256), F32),
            pltpu.SemaphoreType.DMA((12,)),
        ],
    )(total, frames_grad, latent, note)


def on_device(frames, norm_gain, conv_weight, conv_bias, latent_grad):
    frames_grad, latent, total, note = whole(
        latent_grad, frames, norm_gain.reshape(1, 256), conv_weight.reshape(3, 9, 256, 256), conv_bias.reshape(1, 256),
    )
    weight_grad, frames_grad, latent, gain_grad, bias_grad = finish(total, frames_grad, latent, note)
    return (
        latent, frames_grad, weight_grad.reshape(3, 3, 3, 64, 256), gain_grad.reshape(64), bias_grad.reshape(64),
    )


def solution(mesh):
    placed = (P("tm", "rows", None, None), P(), P(), P(), P("tm", None, "rows", None))
    return jax.shard_map(
        on_device,
        mesh=mesh,
        in_specs=placed,
        out_specs=(
            P("tm", None, "rows", None),
            P("tm", "rows", None, None),
            P(None, None, None, "tm", None),
            P("tm"),
            P("tm"),
        ),
        check_vma=False,
    )
```

```python
import jax
import jax.numpy as jnp
from jax import lax
from jax.experimental import pallas as pl
from jax.experimental.pallas import tpu as pltpu
from jax.sharding import PartitionSpec as P

F32 = jnp.float32
BF16 = jnp.bfloat16
MESH = pl.DeviceIdType.MESH
EPS = 1e-06
NX, NZ, NY = 4, 8, 4
CHUNKS, TAPS = 7, 4


def dot_nt(left, right):
    return lax.dot_general(left, right, (((1,), (1,)), ((), ())), preferred_element_type=F32)


def dot_nn(left, right):
    return lax.dot_general(left, right, (((1,), (0,)), ((), ())), preferred_element_type=F32)


def inverse_rms(signal):
    return lax.rsqrt(jnp.mean(signal * signal, axis=-1, keepdims=True) + EPS)


def whole_kernel(
    latent_grad_far, frames_far, gain, weight_far, bias,
    frames_grad_far, latent_far, result, note_out,
    latent_grad, frames, frames_grad, latent, sib, note, note_pair, note_y, note_x, note_z, note_end,
    weight, blocks, middle, landed, flat, woven, grad, grad_above, early, below,
    columns, turned, grad_next, spread, tile, gain_sum, parts,
    other, mine, first_plus, first_minus, second_plus, second_minus,
    mid, first_plus2, first_minus2, second_plus2, second_minus2,
    low, arrive, total, block, latent_in, latent_mid, latent_out,
    weight_sem, send_sems, near_in, gz_in, gs_in, core_in, ring_in, ring2_in, z_in, zback_in, x_in, pair_in,
    lz_in, ls_in, note_in, out_sem,
):
    gz_sem, gs_sem, core_sem, ring_sem, ring2_sem, z_sem = (
        (0, gz_in), (1, gs_in), (2, core_in), (3, ring_in), (4, ring2_in), (5, z_in),
    )
    zback_sem, x_sem, pair_sem, lz_sem, ls_sem, note_sem, near_sem = (
        (6, zback_in), (7, x_in), (8, pair_in), (9, lz_in), (10, ls_in), (11, note_in), (16, near_in),
    )
    rows_at = lax.axis_index("rows")
    y = lax.axis_index("tm")
    core, x, z = rows_at % 2, (rows_at // 2) % NX, rows_at // (2 * NX)
    slab = rows_at % (2 * NX)
    count = NZ * 2 * NX

    def row_of(z_at, x_at, core_at):
        return z_at * (2 * NX) + x_at * 2 + core_at

    sibling = (row_of(z, x, 1 - core), y)

    def along(axis, step):
        if axis == "y":
            return (rows_at, (y + step + NY) % NY)
        if axis == "x":
            return (row_of(z, (x + step) % NX, core), y)
        if axis == "slab":
            return (z * (2 * NX) + (slab + step) % (2 * NX), y)
        if axis == "row":
            return ((rows_at + step + count) % count, y)
        return (row_of((z + step) % NZ, x, core), y)

    barrier = pltpu.get_barrier_semaphore()
    friends = [along("z", step) for step in range(1, NZ)] + [along("slab", step) for step in range(1, 2 * NX)]
    friends += [along("y", 1), along("y", 2), along("y", -1), along("row", 1), along("row", -1)]
    for friend in friends:
        pl.semaphore_signal(barrier, inc=1, device_id=friend, device_id_type=MESH)
    latent_grad_in = pltpu.make_async_copy(latent_grad_far, latent_grad, weight_sem.at[1])
    frames_in = pltpu.make_async_copy(frames_far, frames, weight_sem.at[2])
    weight_in = pltpu.make_async_copy(weight_far, weight, weight_sem.at[0])
    latent_grad_in.start()
    frames_in.start()
    weight_in.start()
    latent_grad_in.wait()

    def unweave(target):
        for frame in range(4):
            for half in range(2):
                for side in range(2):
                    flat[half, pl.ds(2 * frame + side, 64, stride=8), :] = woven[frame, half, pl.ds(side, 64, stride=2), :]
        for half in range(2):
            target[:, :, :, pl.ds(half * 128, 128)] = flat[half].reshape(NZ, 2 * NX, 8, 128).astype(BF16)

    def weave(source, put):
        for half in range(2):
            flat[half] = source[:, :, :, pl.ds(half * 128, 128)].astype(F32).reshape(512, 128)
        for frame in range(4):
            for half in range(2):
                for side in range(2):
                    woven[frame, half, pl.ds(side, 64, stride=2), :] = flat[half, pl.ds(2 * frame + side, 64, stride=8), :]
                put(frame, half, woven[frame, half].astype(BF16))

    for frame in range(4):
        for half in range(2):
            woven[frame, half] = latent_grad[frame, :, :, pl.ds(half * 128, 128)].reshape(128, 128).astype(F32)
    unweave(blocks)

    pl.semaphore_wait(barrier, len(friends))

    def copy_to(source, target, sems, at, device):
        family, arrivals = sems
        if family == 11 or family == 16:
            family += at[0]
        return pltpu.make_async_remote_copy(
            src_ref=source, dst_ref=target, send_sem=send_sems.at[family], recv_sem=arrivals.at[at],
            device_id=device, device_id_type=MESH,
        )

    def taken(sem, ref):
        pltpu.make_async_remote_copy(
            src_ref=ref, dst_ref=ref, send_sem=sem, recv_sem=sem, device_id=sibling, device_id_type=MESH
        ).wait_recv()

    def send(*args):
        copy = copy_to(*args)
        copy.start()
        return copy

    ahead, own, late = pl.ds(0, 256), pl.ds(0, 512), pl.ds(512, 256)
    early_on = copy_to(frames.at[pl.ds(2, 2)], early, near_sem, (0,), along("y", 1))
    below_own = copy_to(frames.at[:, 0], below.at[pl.ds(2, 4)], near_sem, (1,), along("row", -1))
    below_early = copy_to(early.at[:, 0], below.at[pl.ds(0, 2)], near_sem, (2,), along("row", -1))
    grad_late = copy_to(grad.at[ahead], grad.at[late], near_sem, (3,), along("y", -1))
    above_own = copy_to(grad.at[own], grad_above.at[own], near_sem, (4,), along("row", 1))
    above_late = copy_to(grad.at[late], grad_above.at[late], near_sem, (5,), along("row", 1))
    has_past, has_future = y > 0, y < NY - 1
    has_above, has_below = rows_at > 0, rows_at < count - 1

    def only(condition, *actions):
        @pl.when(condition)
        def _():
            for action in actions:
                action()

    order = (0, 1, 7, 2, 6, 3, 5, 4)

    def hop_one(source, between, sems):
        return [
            send(source.at[(z + step) % NZ], between.at[z], sems, (step,), along("z", step)) for step in order[1:]
        ]

    def hop_two(between, target, sems, step):
        at = (z - step + NZ) % NZ
        return [
            send(between.at[at, (slab + move) % (2 * NX)], target.at[at, slab], sems, (0,), along("slab", move))
            for move in range(1, 2 * NX)
        ]

    g_outer = hop_one(blocks, middle, gz_sem)
    frames_in.wait()
    only(has_future, early_on.start)
    middle[z] = blocks[z]
    g_inner = hop_two(middle, landed, gs_sem, 0)

    @pl.when(jnp.logical_not(has_past))
    def _():
        early[...] = jnp.zeros_like(early)

    @pl.when(jnp.logical_not(has_below))
    def _():
        below[...] = jnp.zeros_like(below)

    @pl.when(jnp.logical_not(has_above))
    def _():
        grad_above[...] = jnp.zeros_like(grad_above)

    @pl.when(jnp.logical_not(has_future))
    def _():
        grad[late, :] = jnp.zeros((256, 256), BF16)

    gain_row = gain[...]
    row_at = lax.broadcasted_iota(jnp.int32, (128, 256), 0)

    def hidden_tile(source, at, row, keep):
        for piece_at in range(4):
            rows = pl.ds(piece_at * 64, 64)
            signal = source[rows, :].astype(F32)
            normed = signal * inverse_rms(signal) * gain_row
            hidden = normed / (1.0 + jnp.exp(-normed))
            tile[row, 0, rows, :] = hidden[:, :128]
            tile[row, 1, rows, :] = hidden[:, 128:]
        even = jnp.concatenate([tile[row, half, pl.ds(0, 128, stride=2), :] for half in range(2)], axis=1)
        odd = jnp.concatenate([tile[row, half, pl.ds(1, 128, stride=2), :] for half in range(2)], axis=1)
        after = jnp.where(row_at == 127, 0.0, pltpu.roll(even, 127, 0))
        where = pl.ds(pl.multiple_of(at * 128, 128), 128)
        columns[where, pl.ds(row * 768, 256)] = even.astype(BF16)
        columns[where, pl.ds(row * 768 + 256, 256)] = odd.astype(BF16)
        columns[where, pl.ds(row * 768 + 512, 256)] = after.astype(BF16)
        if keep:
            lanes = pl.ds(pl.multiple_of((at - 2) * 128, 128), 128)
            turned[2 * row, :, lanes] = even.T.astype(BF16)
            turned[2 * row + 1, :, lanes] = odd.T.astype(BF16)

    @pl.loop(2, 6)
    def _(at):
        hidden_tile(frames.at[at - 2, 0], at, 0, True)
        hidden_tile(frames.at[at - 2, 1], at, 1, True)

    for copy, step in zip(g_outer, order[1:]):
        copy.wait_recv()
        g_inner += hop_two(middle, landed, gs_sem, step)
    landed[:, slab] = middle[:, slab]
    spread[...] = jnp.zeros_like(spread)
    gain_sum[...] = jnp.zeros_like(gain_sum)
    weight_in.wait()
    taken(gs_in.at[0], landed.at[pl.ds(0, 7)])

    def put_grad(frame, half, value):
        grad[pl.ds(frame * 128, 128), pl.ds(half * 128, 128)] = value

    weave(landed, put_grad)
    only(has_past, grad_late.start)
    only(has_below, above_own.start)
    only(has_above, below_own.start)

    def step_on(which, source, frames_at):
        for at in frames_at:
            where = pl.ds(at * 128, 128)
            moved = pltpu.roll(source[where, :].astype(F32), 1, 0)
            grad_next[which, where, :] = jnp.where(row_at == 0, 0.0, moved).astype(BF16)

    def weight_taps(chunk):
        for tap in range(chunk * TAPS, min(27, chunk * TAPS + TAPS)):
            tap_t, tap_r, tap_c = tap // 9, tap // 3 % 3, tap % 3
            where = pl.ds((2 - tap_t) * 128, 512)
            left = turned[2 * (tap_r % 2) + tap_c % 2]
            if tap_c == 2:
                right = grad_next[1 if tap_r == 2 else 0, where, :]
            else:
                right = (grad_above if tap_r == 2 else grad)[where, :]
            product = dot_nn(left, right).astype(BF16)
            parts[0, tap] = product[:, :128]
            parts[1, tap] = product[:, 128:]

    pair = {}

    def pair_send(chunk):
        spots = pl.ds(chunk * TAPS, TAPS)
        pair[chunk] = send(parts.at[1 - core, spots], other.at[spots], core_sem, (chunk,), sibling)

    def axes_of(chunk):
        return ("y", "x") if chunk % 2 == 0 else ("x", "y")

    def here(axis, step):
        return (y + step) % NY if axis == "y" else (x + step) % NX

    def piece(ref, chunk, stage, at, taps):
        if stage == 0 and axes_of(chunk)[0] == "x":
            return ref.at[chunk, taps, slice(None), at]
        return ref.at[chunk, taps, at]

    FIRST, LAST, ALL = pl.ds(0, 2), pl.ds(2, 2), pl.ds(0, 4)
    banks = (
        (mine, first_plus, first_minus, second_plus, second_minus, ring_sem, BF16),
        (mid, first_plus2, first_minus2, second_plus2, second_minus2, ring2_sem, F32),
    )

    def ring_open(chunk, stage):
        source, plus, minus, _, _, sems, _ = banks[stage]
        axis = axes_of(chunk)[stage]
        far = here(axis, 2)
        return [
            send(piece(source, chunk, stage, far, FIRST), plus.at[chunk], sems, (chunk, 0), along(axis, 1)),
            send(piece(source, chunk, stage, far, LAST), minus.at[chunk], sems, (chunk, 1), along(axis, 3)),
        ]

    def ring_next(chunk, stage, opened):
        source, plus, minus, plus_in, minus_in, sems, kind = banks[stage]
        axis = axes_of(chunk)[stage]
        opened[0].wait_recv()
        ahead = piece(source, chunk, stage, here(axis, 1), FIRST)
        ahead[...] = (ahead[...].astype(F32) + plus[chunk].astype(F32)).astype(kind)
        one = send(piece(source, chunk, stage, here(axis, 1), ALL), plus_in.at[chunk], sems, (chunk, 2), along(axis, 1))
        opened[1].wait_recv()
        behind = piece(source, chunk, stage, here(axis, 3), LAST)
        behind[...] = (behind[...].astype(F32) + minus[chunk].astype(F32)).astype(kind)
        two = send(piece(source, chunk, stage, here(axis, 3), ALL), minus_in.at[chunk], sems, (chunk, 3), along(axis, 3))
        return [one, two]

    def ring_close(chunk, stage, sent):
        source, _, _, plus_in, minus_in, _, _ = banks[stage]
        axis = axes_of(chunk)[stage]
        sent[0].wait_recv()
        sent[1].wait_recv()
        own = piece(source, chunk, stage, here(axis, 0), ALL)[...].astype(F32)
        summed = own + plus_in[chunk].astype(F32) + minus_in[chunk].astype(F32)
        if stage == 0:
            mid[chunk] = summed
        else:
            low[chunk] = summed.reshape(NZ, 8, 128)

    shares = {}

    def to_owners(chunk):
        shares[chunk] = [
            send(low.at[chunk, (z + step) % NZ], arrive.at[step, chunk], z_sem, (chunk,), along("z", step))
            for step in order[1:]
        ]

    opened, sent, opened2, sent2 = {}, {}, {}, {}

    def pair_close(chunk):
        pair[chunk].wait_recv()
        spots = pl.ds(chunk * TAPS, TAPS)
        summed = parts[core, spots].astype(F32) + other[spots].astype(F32)
        mine[chunk] = summed.astype(BF16).reshape(TAPS, NY, NX, 16, 128)
        opened[chunk] = ring_open(chunk, 0)

    def next_one(*chunks):
        for chunk in chunks:
            sent[chunk] = ring_next(chunk, 0, opened[chunk])

    def close_one(*chunks):
        for chunk in chunks:
            ring_close(chunk, 0, sent[chunk])
            opened2[chunk] = ring_open(chunk, 1)

    def next_two(*chunks):
        for chunk in chunks:
            sent2[chunk] = ring_next(chunk, 1, opened2[chunk])

    def close_two(*chunks):
        for chunk in chunks:
            ring_close(chunk, 1, sent2[chunk])
            to_owners(chunk)

    step_on(0, grad, range(4))
    weight_taps(5)
    pair_send(5)
    only(has_past, early_on.wait_recv)
    only(has_above, below_early.start)

    @pl.loop(0, 2)
    def _(at):
        hidden_tile(early.at[at, 0], at, 0, False)
        hidden_tile(early.at[at, 1], at, 1, False)

    pair_close(5)
    only(has_future, grad_late.wait_recv)
    only(has_below, above_late.start)
    step_on(0, grad, (4, 5))
    weight_taps(0)
    pair_send(0)
    only(has_above, above_own.wait_recv, above_late.wait_recv)
    step_on(1, grad_above, range(6))
    before = 0
    parts[:, 27] = jnp.zeros((2, 256, 128), BF16)
    for chunk in (2, 3, 4, 1, 6):
        weight_taps(chunk)
        pair_send(chunk)
        pair_close(before)
        before = chunk

    def back_taps(tap):
        where = pl.ds((2 - tap) * 128, 512)
        here_g, here_next = grad[where, :], grad_next[0, where, :]
        above, above_next = grad_above[where, :], grad_next[1, where, :]
        spread[0] += dot_nt(here_g, weight[tap, 0]) + dot_nt(here_next, weight[tap, 2])
        spread[0] += dot_nt(above, weight[tap, 6]) + dot_nt(above_next, weight[tap, 8])
        spread[1] += dot_nt(here_g, weight[tap, 1]) + dot_nt(above, weight[tap, 7])
        spread[2] += dot_nt(here_g, weight[tap, 3]) + dot_nt(here_next, weight[tap, 5])
        spread[3] += dot_nt(here_g, weight[tap, 4])

    def frame_back(first, last):
        @pl.loop(first, last)
        def _(at):
            where = pl.ds(pl.multiple_of(at * 128, 128), 128)
            for row in range(2):
                for half in range(2):
                    lanes = pl.ds(half * 128, 128)
                    tile[row, half, pl.ds(0, 128, stride=2), :] = spread[2 * row, where, lanes]
                    tile[row, half, pl.ds(1, 128, stride=2), :] = spread[2 * row + 1, where, lanes]
                for piece_at in range(4):
                    rows = pl.ds(piece_at * 64, 64)
                    signal = frames[at, row, rows, :].astype(F32)
                    inv = inverse_rms(signal)
                    unit = signal * inv
                    normed = unit * gain_row
                    sigma = 1.0 / (1.0 + jnp.exp(-normed))
                    arrived = jnp.concatenate([tile[row, half, rows, :] for half in range(2)], axis=1)
                    normed_grad = arrived * sigma * (1.0 + normed * (1.0 - sigma))
                    gain_sum[...] += jnp.sum((normed_grad * unit).reshape(8, 8, 256), axis=0)
                    unit_grad = normed_grad * gain_row
                    mean = jnp.mean(unit_grad * unit, axis=-1, keepdims=True)
                    frames_grad[at, row, rows, :] = (inv * (unit_grad - unit * mean)).astype(BF16)

    def spread_out(source, bank, me, axis, total_at, stage):
        bank[me] = source
        return [
            send(bank.at[me], bank.at[me], note_sem, (stage,), along(axis, step)) for step in range(1, total_at)
        ]

    def collect(stage, bank, total_at):
        taken(note_in.at[stage], bank.at[pl.ds(0, total_at - 1)])
        value = bank[0]
        for at in range(1, total_at):
            value = value + bank[at]
        return value

    back_taps(0)
    pair_close(before)
    back_taps(1)
    next_one(5, 0)
    back_taps(2)
    next_one(2, 3)
    frame_back(0, 2)
    next_one(4, 1)
    frame_back(2, 4)
    frames_out = pltpu.make_async_copy(frames_grad, frames_grad_far, out_sem.at[0])
    frames_out.start()
    gain_local = jnp.sum(gain_sum[...], axis=0, keepdims=True)
    bias_local = jnp.sum(grad[pl.ds(0, 512), :].astype(F32), axis=0, keepdims=True)
    spot = lax.broadcasted_iota(jnp.int32, (8, 256), 0)
    small = jnp.where(spot == 0, gain_local, jnp.where(spot == 1, bias_local, 0.0))
    note[0] = small[:, :128]
    note[1] = small[:, 128:]
    notes = [send(note.at[1 - core], note_pair, note_sem, (0,), sibling)]
    next_one(6)
    only(has_below, below_own.wait_recv, below_early.wait_recv)

    @pl.loop(0, 6)
    def _(at):
        hidden_tile(below.at[at], at, 2, False)

    spread[0] = jnp.broadcast_to(bias[...], (512, 256))

    @pl.loop(0, 3)
    def _(tap):
        where = pl.ds(pl.multiple_of(tap * 128, 128), 512)
        spread[0] += dot_nn(columns[where, :], weight[tap].reshape(2304, 256))

    for frame in range(4):
        for half in range(2):
            woven[frame, half] = spread[0, pl.ds(frame * 128, 128), pl.ds(half * 128, 128)]
    unweave(latent_in)
    outer = hop_one(latent_in, latent_mid, lz_sem)
    latent_mid[z] = latent_in[z]
    hop_two(latent_mid, latent_out, ls_sem, 0)
    close_one(5, 0, 2, 3)
    notes[0].wait_recv()
    spread_out(note[core] + note_pair[...], note_y, y, "y", NY, 1)
    close_one(4, 1, 6)
    next_two(5, 0, 2, 3)
    spread_out(collect(1, note_y, NY), note_x, x, "x", NX, 2)
    next_two(4, 1, 6)
    close_two(5, 0, 2, 3)
    close_two(4, 1, 6)
    spread_out(collect(2, note_x, NX), note_z, z, "z", NZ, 3)
    for chunk in (5, 0, 2, 3, 4, 1, 6):
        summed = low[chunk, z]
        taken(z_in.at[chunk], low.at[0, pl.ds(0, 7)])
        for step in order[1:]:
            summed += arrive[step, chunk]
        total[z, chunk] = summed.astype(BF16)

    def back(step):
        return copy_to(total.at[z], total.at[z], zback_sem, (step,), along("z", step))

    for step in order[1:]:
        back(step).start()
    for copy, step in zip(outer, order[1:]):
        copy.wait_recv()
        hop_two(latent_mid, latent_out, ls_sem, step)
    latent_out[:, slab] = latent_mid[:, slab]

    right, left, across = (x + 1) % NX, (x + 3) % NX, (x + 2) % NX
    HALF, REST = pl.ds(0, 4), pl.ds(4, 3)

    def to_right(step, at):
        return copy_to(total.at[at], block.at[x, at], x_sem, (0, step), along("x", 1))

    def to_left(step, at):
        return copy_to(total.at[at], block.at[x, at], x_sem, (1, step), along("x", 3))

    def on_right(step, at):
        half = block.at[left, at, HALF]
        return copy_to(half, half, x_sem, (2, step), along("x", 1))

    def on_left(step, at):
        half = block.at[right, at, REST]
        return copy_to(half, half, x_sem, (3, step), along("x", 3))

    def across_core(which, step, at):
        source = total.at[at] if which == 0 else block.at[(left, right, across)[which - 1], at]
        where = (x, left, right, across)[which]
        return copy_to(source, sib.at[where, at], pair_sem, (which,), sibling)

    def each(body):
        for step in order:
            body(step, (z - step + NZ) % NZ)

    def fan_one(step, at):
        if step:
            back(step).wait_recv()
        to_right(step, at).start()
        to_left(step, at).start()
        across_core(0, step, at).start()

    def fan_two(step, at):
        to_right(step, at).wait_recv()
        on_right(step, at).start()
        across_core(1, step, at).start()
        to_left(step, at).wait_recv()
        on_left(step, at).start()
        across_core(2, step, at).start()

    def fan_three(step, at):
        on_right(step, at).wait_recv()
        on_left(step, at).wait_recv()
        across_core(3, step, at).start()

    def keep(source, half, where, at):
        copy = pltpu.make_async_copy(source, result.at[half, where], out_sem.at[at])
        copy.start()
        return copy

    each(fan_one)
    kept = [frames_out, keep(total, core, x, 1)]
    note_end[0] = collect(3, note_z, NZ)
    note_last = send(note_end.at[0], note_end.at[1], note_sem, (4,), sibling)
    each(fan_two)
    kept += [keep(block.at[left], core, left, 2), keep(block.at[right], core, right, 3)]
    taken(ls_in.at[0], latent_out.at[pl.ds(0, 7)])

    def put_latent(frame, half, value):
        latent[frame, :, pl.ds(half * 128, 128)] = value

    weave(latent_out, put_latent)
    kept.append(pltpu.make_async_copy(latent, latent_far, out_sem.at[4]))
    kept[-1].start()
    each(fan_three)
    kept.append(keep(block.at[across], core, across, 5))
    note_last.wait_recv()
    note_out[core] = note_end[0]
    note_out[1 - core] = note_end[1]
    for which, where in enumerate((x, left, right, across)):
        taken(pair_in.at[which], sib.at[0])
        kept.append(keep(sib.at[where], 1 - core, where, 6 + which))
    seven, three = pl.ds(0, 7), pl.ds(0, 3)
    for family, ref in (
        (0, middle.at[seven]), (1, landed.at[seven]), (2, other), (3, mine.at[:, three]), (4, mid.at[:, three]),
        (5, low.at[:, seven]), (6, total.at[seven]), (7, block.at[three]), (8, sib),
        (9, latent_mid.at[seven]), (10, latent_out.at[seven]),
        (11, note_pair), (12, note_y.at[three]), (13, note_x.at[three]), (14, note_z.at[seven]), (15, note_pair),
    ):
        taken(send_sems.at[family], ref)
    only(has_future, early_on.wait_send)
    only(has_above, below_own.wait_send, below_early.wait_send)
    only(has_past, grad_late.wait_send)
    only(has_below, above_own.wait_send, above_late.wait_send)
    for copy in kept:
        copy.wait()


def whole(latent_grad, frames, gain, weight, bias):
    dma, vmem = pltpu.SemaphoreType.DMA, pltpu.VMEM
    inside, far = pl.BlockSpec(memory_space=pltpu.VMEM), pl.BlockSpec(memory_space=pl.ANY)
    return pl.pallas_call(
        whole_kernel,
        out_shape=(
            jax.ShapeDtypeStruct((4, 2, 256, 256), BF16),
            jax.ShapeDtypeStruct((4, 128, 256), BF16),
            jax.ShapeDtypeStruct((2, NX, NZ, CHUNKS, 8, 128), BF16),
            jax.ShapeDtypeStruct((2, 8, 128), F32),
        ),
        in_specs=[far, far, inside, far, inside],
        out_specs=[far, far, far, inside],
        scratch_shapes=[
            vmem((4, 64, 2, 256), BF16),
            vmem((4, 2, 256, 256), BF16),
            vmem((4, 2, 256, 256), BF16),
            vmem((4, 128, 256), BF16),
            vmem((NX, NZ, CHUNKS, 8, 128), BF16),
            vmem((2, 8, 128), F32),
            vmem((8, 128), F32),
            vmem((NY, 8, 128), F32),
            vmem((NX, 8, 128), F32),
            vmem((NZ, 8, 128), F32),
            vmem((2, 8, 128), F32),
            vmem((3, 9, 256, 256), BF16),
            vmem((NZ, 2 * NX, 8, 256), BF16),
            vmem((NZ, 2 * NX, 8, 256), BF16),
            vmem((NZ, 2 * NX, 8, 256), BF16),
            vmem((2, 512, 128), F32),
            vmem((4, 2, 128, 128), F32),
            vmem((768, 256), BF16),
            vmem((768, 256), BF16),
            vmem((2, 2, 256, 256), BF16),
            vmem((6, 256, 256), BF16),
            vmem((768, 2304), BF16),
            vmem((4, 256, 512), BF16),
            vmem((2, 768, 256), BF16),
            vmem((4, 512, 256), F32),
            vmem((3, 2, 256, 128), F32),
            vmem((8, 256), F32),
            vmem((2, 28, 256, 128), BF16),
            vmem((CHUNKS * TAPS, 256, 128), BF16),
            vmem((CHUNKS, TAPS, NY, NX, 16, 128), BF16),
            vmem((CHUNKS, 2, 4, 16, 128), BF16),
            vmem((CHUNKS, 2, 4, 16, 128), BF16),
            vmem((CHUNKS, TAPS, 4, 16, 128), BF16),
            vmem((CHUNKS, TAPS, 4, 16, 128), BF16),
            vmem((CHUNKS, TAPS, 4, 16, 128), F32),
            vmem((CHUNKS, 2, 16, 128), F32),
            vmem((CHUNKS, 2, 16, 128), F32),
            vmem((CHUNKS, TAPS, 16, 128), F32),
            vmem((CHUNKS, TAPS, 16, 128), F32),
            vmem((CHUNKS, NZ, 8, 128), F32),
            vmem((NZ, CHUNKS, 8, 128), F32),
            vmem((NZ, CHUNKS, 8, 128), BF16),
            vmem((NX, NZ, CHUNKS, 8, 128), BF16),
            vmem((NZ, 2 * NX, 8, 256), BF16),
            vmem((NZ, 2 * NX, 8, 256), BF16),
            vmem((NZ, 2 * NX, 8, 256), BF16),
            dma((3,)),
            dma((22,)),
            dma((6,)),
            dma((NZ,)),
            dma((1,)),
            dma((CHUNKS,)),
            dma((CHUNKS, 4)),
            dma((CHUNKS, 4)),
            dma((CHUNKS,)),
            dma((NZ,)),
            dma((4, NZ)),
            dma((4,)),
            dma((NZ,)),
            dma((1,)),
            dma((5,)),
            dma((10,)),
        ],
        compiler_params=pltpu.CompilerParams(collective_id=1, has_side_effects=True),
        cost_estimate=pl.CostEstimate(flops=5_500_000_000, bytes_accessed=12_000_000, transcendentals=2_000_000),
    )(latent_grad, frames, gain, weight, bias)


def finish_kernel(
    total_far, frames_far, latent_far, note, weight_grad, frames_grad, latent, gain_grad, bias_grad,
    total, frames_near, latent_near, latent_wide, wide, sems,
):
    copy = pltpu.make_async_copy
    total_in = copy(total_far, total, sems.at[0])
    frames_in = copy(frames_far, frames_near, sems.at[1])
    latent_in = copy(latent_far, latent_near, sems.at[2])
    total_in.start()
    frames_in.start()
    latent_in.start()
    total_in.wait()
    going = []
    for chunk in range(CHUNKS):
        for tap in range(chunk * TAPS, min(27, chunk * TAPS + TAPS)):
            for core in range(2):
                for x in range(NX):
                    for side in range(2):
                        part = total[core, x, 2 * (tap % TAPS) + side, chunk]
                        wide[tap, pl.ds(x * 16 + side * 8, 8), pl.ds(core * 128, 128)] = part.astype(F32)
        taps = pl.ds(chunk * TAPS, min(27, chunk * TAPS + TAPS) - chunk * TAPS)
        going.append(copy(wide.at[taps], weight_grad.at[taps], sems.at[3 + chunk]))
        going[-1].start()
        if chunk == 0:
            frames_in.wait()
            going.append(copy(frames_near, frames_grad, sems.at[10]))
            going[-1].start()
        if chunk == 1:
            latent_in.wait()
            for frame in range(4):
                latent_wide[frame] = latent_near[frame].reshape(64, 2, 256)
            going.append(copy(latent_wide, latent, sems.at[11]))
            going[-1].start()
    for core in range(2):
        row = note[core]
        for side in range(2):

            @pl.when(lax.axis_index("tm") == 2 * core + side)
            def _():
                gain_grad[...] = row[0:1, 64 * side : 64 * side + 64]
                bias_grad[...] = row[1:2, 64 * side : 64 * side + 64]

    for item in going:
        item.wait()


def finish(total, frames_grad, latent, note):
    inside, far = pl.BlockSpec(memory_space=pltpu.VMEM), pl.BlockSpec(memory_space=pl.ANY)
    return pl.pallas_call(
        finish_kernel,
        out_shape=(
            jax.ShapeDtypeStruct((27, 64, 256), F32),
            jax.ShapeDtypeStruct((4, 2, 256, 256), BF16),
            jax.ShapeDtypeStruct((4, 64, 2, 256), BF16),
            jax.ShapeDtypeStruct((1, 64), F32),
            jax.ShapeDtypeStruct((1, 64), F32),
        ),
        in_specs=[far] * 3 + [inside],
        out_specs=[far, far, far, inside, inside],
        scratch_shapes=[
            pltpu.VMEM((2, NX, NZ, CHUNKS, 8, 128), BF16),
            pltpu.VMEM((4, 2, 256, 256), BF16),
            pltpu.VMEM((4, 128, 256), BF16),
            pltpu.VMEM((4, 64, 2, 256), BF16),
            pltpu.VMEM((27, 64, 256), F32),
            pltpu.SemaphoreType.DMA((12,)),
        ],
    )(total, frames_grad, latent, note)


def on_device(frames, norm_gain, conv_weight, conv_bias, latent_grad):
    frames_grad, latent, total, note = whole(
        latent_grad, frames, norm_gain.reshape(1, 256), conv_weight.reshape(3, 9, 256, 256), conv_bias.reshape(1, 256),
    )
    weight_grad, frames_grad, latent, gain_grad, bias_grad = finish(total, frames_grad, latent, note)
    return (
        latent, frames_grad, weight_grad.reshape(3, 3, 3, 64, 256), gain_grad.reshape(64), bias_grad.reshape(64),
    )


def solution(mesh):
    placed = (P("tm", "rows", None, None), P(), P(), P(), P("tm", None, "rows", None))
    return jax.shard_map(
        on_device,
        mesh=mesh,
        in_specs=placed,
        out_specs=(
            P("tm", None, "rows", None),
            P("tm", "rows", None, None),
            P(None, None, None, "tm", None),
            P("tm"),
            P("tm"),
        ),
        check_vma=False,
    )
```

```python
import jax
import jax.numpy as jnp
from jax import lax
from jax.experimental import pallas as pl
from jax.experimental.pallas import tpu as pltpu
from jax.sharding import PartitionSpec as P

F32 = jnp.float32
BF16 = jnp.bfloat16
MESH = pl.DeviceIdType.MESH
EPS = 1e-06
NX, NZ, NY = 4, 8, 4
CHUNKS, TAPS = 7, 4


def dot_nt(left, right):
    return lax.dot_general(left, right, (((1,), (1,)), ((), ())), preferred_element_type=F32)


def dot_nn(left, right):
    return lax.dot_general(left, right, (((1,), (0,)), ((), ())), preferred_element_type=F32)


def inverse_rms(signal):
    return lax.rsqrt(jnp.mean(signal * signal, axis=-1, keepdims=True) + EPS)


def whole_kernel(
    latent_grad_far, frames_far, gain_far, weight_far, bias_far,
    frames_grad_far, latent_far, result, note_out,
    gain, bias, latent_grad, frames, frames_grad, latent, sib, note, note_pair, note_y, note_x, note_z, note_end,
    weight, blocks, middle, landed, flat, woven, grad, grad_above, early, below,
    columns, turned, grad_next, spread, tile, gain_sum, parts,
    other, mine, first_plus, first_minus, second_plus, second_minus,
    mid, first_plus2, first_minus2, second_plus2, second_minus2,
    low, arrive, total, block, latent_in, latent_mid, latent_out,
    weight_sem, send_sems, near_in, gz_in, gs_in, core_in, ring_in, ring2_in, z_in, zback_in, x_in, pair_in,
    lz_in, ls_in, note_in, out_sem,
):
    gz_sem, gs_sem, core_sem, ring_sem, ring2_sem, z_sem = (
        (0, gz_in), (1, gs_in), (2, core_in), (3, ring_in), (4, ring2_in), (5, z_in),
    )
    zback_sem, x_sem, pair_sem, lz_sem, ls_sem, note_sem, near_sem = (
        (6, zback_in), (7, x_in), (8, pair_in), (9, lz_in), (10, ls_in), (11, note_in), (16, near_in),
    )
    rows_at = lax.axis_index("rows")
    y = lax.axis_index("tm")
    core, x, z = rows_at % 2, (rows_at // 2) % NX, rows_at // (2 * NX)
    slab = rows_at % (2 * NX)
    count = NZ * 2 * NX

    def row_of(z_at, x_at, core_at):
        return z_at * (2 * NX) + x_at * 2 + core_at

    sibling = (row_of(z, x, 1 - core), y)

    def along(axis, step):
        if axis == "y":
            return (rows_at, (y + step + NY) % NY)
        if axis == "x":
            return (row_of(z, (x + step) % NX, core), y)
        if axis == "slab":
            return (z * (2 * NX) + (slab + step) % (2 * NX), y)
        if axis == "row":
            return ((rows_at + step + count) % count, y)
        return (row_of((z + step) % NZ, x, core), y)

    barrier = pltpu.get_barrier_semaphore()
    friends = [along("z", step) for step in range(1, NZ)] + [along("slab", step) for step in range(1, 2 * NX)]
    friends += [along("y", 1), along("y", 2), along("y", -1), along("row", 1), along("row", -1)]
    for friend in friends:
        pl.semaphore_signal(barrier, inc=1, device_id=friend, device_id_type=MESH)
    latent_grad_in = pltpu.make_async_copy(latent_grad_far, latent_grad, weight_sem.at[1])
    frames_in = pltpu.make_async_copy(frames_far, frames, weight_sem.at[2])
    weight_in = pltpu.make_async_copy(weight_far, weight, weight_sem.at[0])
    gain_in = pltpu.make_async_copy(gain_far, gain, weight_sem.at[3])
    bias_in = pltpu.make_async_copy(bias_far, bias, weight_sem.at[4])
    latent_grad_in.start()
    frames_in.start()
    gain_in.start()
    bias_in.start()
    weight_in.start()
    latent_grad_in.wait()

    def unweave(target):
        for frame in range(4):
            for half in range(2):
                for side in range(2):
                    flat[half, pl.ds(2 * frame + side, 64, stride=8), :] = woven[frame, half, pl.ds(side, 64, stride=2), :]
        for half in range(2):
            target[:, :, :, pl.ds(half * 128, 128)] = flat[half].reshape(NZ, 2 * NX, 8, 128).astype(BF16)

    def weave(source, put):
        for half in range(2):
            flat[half] = source[:, :, :, pl.ds(half * 128, 128)].astype(F32).reshape(512, 128)
        for frame in range(4):
            for half in range(2):
                for side in range(2):
                    woven[frame, half, pl.ds(side, 64, stride=2), :] = flat[half, pl.ds(2 * frame + side, 64, stride=8), :]
                put(frame, half, woven[frame, half].astype(BF16))

    for frame in range(4):
        for half in range(2):
            woven[frame, half] = latent_grad[frame, :, :, pl.ds(half * 128, 128)].reshape(128, 128).astype(F32)
    unweave(blocks)

    pl.semaphore_wait(barrier, len(friends))

    def copy_to(source, target, sems, at, device):
        family, arrivals = sems
        if family == 11 or family == 16:
            family += at[0]
        return pltpu.make_async_remote_copy(
            src_ref=source, dst_ref=target, send_sem=send_sems.at[family], recv_sem=arrivals.at[at],
            device_id=device, device_id_type=MESH,
        )

    def taken(sem, ref):
        pltpu.make_async_remote_copy(
            src_ref=ref, dst_ref=ref, send_sem=sem, recv_sem=sem, device_id=sibling, device_id_type=MESH
        ).wait_recv()

    def send(*args):
        copy = copy_to(*args)
        copy.start()
        return copy

    ahead, own, late = pl.ds(0, 256), pl.ds(0, 512), pl.ds(512, 256)
    early_on = copy_to(frames.at[pl.ds(2, 2)], early, near_sem, (0,), along("y", 1))
    below_own = copy_to(frames.at[:, 0], below.at[pl.ds(2, 4)], near_sem, (1,), along("row", -1))
    below_early = copy_to(early.at[:, 0], below.at[pl.ds(0, 2)], near_sem, (2,), along("row", -1))
    grad_late = copy_to(grad.at[ahead], grad.at[late], near_sem, (3,), along("y", -1))
    above_own = copy_to(grad.at[own], grad_above.at[own], near_sem, (4,), along("row", 1))
    above_late = copy_to(grad.at[late], grad_above.at[late], near_sem, (5,), along("row", 1))
    has_past, has_future = y > 0, y < NY - 1
    has_above, has_below = rows_at > 0, rows_at < count - 1

    def only(condition, *actions):
        @pl.when(condition)
        def _():
            for action in actions:
                action()

    order = (0, 1, 7, 2, 6, 3, 5, 4)

    def hop_one(source, between, sems):
        return [
            send(source.at[(z + step) % NZ], between.at[z], sems, (step,), along("z", step)) for step in order[1:]
        ]

    def hop_two(between, target, sems, step):
        at = (z - step + NZ) % NZ
        return [
            send(between.at[at, (slab + move) % (2 * NX)], target.at[at, slab], sems, (0,), along("slab", move))
            for move in range(1, 2 * NX)
        ]

    g_outer = hop_one(blocks, middle, gz_sem)
    frames_in.wait()
    gain_in.wait()
    bias_in.wait()
    only(has_future, early_on.start)
    middle[z] = blocks[z]
    g_inner = hop_two(middle, landed, gs_sem, 0)

    @pl.when(jnp.logical_not(has_past))
    def _():
        early[...] = jnp.zeros_like(early)

    @pl.when(jnp.logical_not(has_below))
    def _():
        below[...] = jnp.zeros_like(below)

    @pl.when(jnp.logical_not(has_above))
    def _():
        grad_above[...] = jnp.zeros_like(grad_above)

    @pl.when(jnp.logical_not(has_future))
    def _():
        grad[late, :] = jnp.zeros((256, 256), BF16)

    gain_row = gain[...]
    row_at = lax.broadcasted_iota(jnp.int32, (128, 256), 0)

    def hidden_tile(source, at, row, keep):
        for piece_at in range(4):
            rows = pl.ds(piece_at * 64, 64)
            signal = source[rows, :].astype(F32)
            normed = signal * inverse_rms(signal) * gain_row
            hidden = normed / (1.0 + jnp.exp(-normed))
            tile[row, 0, rows, :] = hidden[:, :128]
            tile[row, 1, rows, :] = hidden[:, 128:]
        even = jnp.concatenate([tile[row, half, pl.ds(0, 128, stride=2), :] for half in range(2)], axis=1)
        odd = jnp.concatenate([tile[row, half, pl.ds(1, 128, stride=2), :] for half in range(2)], axis=1)
        after = jnp.where(row_at == 127, 0.0, pltpu.roll(even, 127, 0))
        where = pl.ds(pl.multiple_of(at * 128, 128), 128)
        columns[where, pl.ds(row * 768, 256)] = even.astype(BF16)
        columns[where, pl.ds(row * 768 + 256, 256)] = odd.astype(BF16)
        columns[where, pl.ds(row * 768 + 512, 256)] = after.astype(BF16)
        if keep:
            lanes = pl.ds(pl.multiple_of((at - 2) * 128, 128), 128)
            turned[2 * row, :, lanes] = even.T.astype(BF16)
            turned[2 * row + 1, :, lanes] = odd.T.astype(BF16)

    @pl.loop(2, 6)
    def _(at):
        hidden_tile(frames.at[at - 2, 0], at, 0, True)
        hidden_tile(frames.at[at - 2, 1], at, 1, True)

    for copy, step in zip(g_outer, order[1:]):
        copy.wait_recv()
        g_inner += hop_two(middle, landed, gs_sem, step)
    landed[:, slab] = middle[:, slab]
    spread[...] = jnp.zeros_like(spread)
    gain_sum[...] = jnp.zeros_like(gain_sum)
    weight_in.wait()
    taken(gs_in.at[0], landed.at[pl.ds(0, 7)])

    def put_grad(frame, half, value):
        grad[pl.ds(frame * 128, 128), pl.ds(half * 128, 128)] = value

    weave(landed, put_grad)
    only(has_past, grad_late.start)
    only(has_below, above_own.start)
    only(has_above, below_own.start)

    def step_on(which, source, frames_at):
        for at in frames_at:
            where = pl.ds(at * 128, 128)
            moved = pltpu.roll(source[where, :].astype(F32), 1, 0)
            grad_next[which, where, :] = jnp.where(row_at == 0, 0.0, moved).astype(BF16)

    def weight_taps(chunk):
        for tap in range(chunk * TAPS, min(27, chunk * TAPS + TAPS)):
            tap_t, tap_r, tap_c = tap // 9, tap // 3 % 3, tap % 3
            where = pl.ds((2 - tap_t) * 128, 512)
            left = turned[2 * (tap_r % 2) + tap_c % 2]
            if tap_c == 2:
                right = grad_next[1 if tap_r == 2 else 0, where, :]
            else:
                right = (grad_above if tap_r == 2 else grad)[where, :]
            product = dot_nn(left, right).astype(BF16)
            parts[0, tap] = product[:, :128]
            parts[1, tap] = product[:, 128:]

    pair = {}

    def pair_send(chunk):
        spots = pl.ds(chunk * TAPS, TAPS)
        pair[chunk] = send(parts.at[1 - core, spots], other.at[spots], core_sem, (chunk,), sibling)

    def axes_of(chunk):
        return ("y", "x") if chunk % 2 == 0 else ("x", "y")

    def here(axis, step):
        return (y + step) % NY if axis == "y" else (x + step) % NX

    def piece(ref, chunk, stage, at, taps):
        if stage == 0 and axes_of(chunk)[0] == "x":
            return ref.at[chunk, taps, slice(None), at]
        return ref.at[chunk, taps, at]

    FIRST, LAST, ALL = pl.ds(0, 2), pl.ds(2, 2), pl.ds(0, 4)
    banks = (
        (mine, first_plus, first_minus, second_plus, second_minus, ring_sem, BF16),
        (mid, first_plus2, first_minus2, second_plus2, second_minus2, ring2_sem, F32),
    )

    def ring_open(chunk, stage):
        source, plus, minus, _, _, sems, _ = banks[stage]
        axis = axes_of(chunk)[stage]
        far = here(axis, 2)
        return [
            send(piece(source, chunk, stage, far, FIRST), plus.at[chunk], sems, (chunk, 0), along(axis, 1)),
            send(piece(source, chunk, stage, far, LAST), minus.at[chunk], sems, (chunk, 1), along(axis, 3)),
        ]

    def ring_next(chunk, stage, opened):
        source, plus, minus, plus_in, minus_in, sems, kind = banks[stage]
        axis = axes_of(chunk)[stage]
        opened[0].wait_recv()
        ahead = piece(source, chunk, stage, here(axis, 1), FIRST)
        ahead[...] = (ahead[...].astype(F32) + plus[chunk].astype(F32)).astype(kind)
        one = send(piece(source, chunk, stage, here(axis, 1), ALL), plus_in.at[chunk], sems, (chunk, 2), along(axis, 1))
        opened[1].wait_recv()
        behind = piece(source, chunk, stage, here(axis, 3), LAST)
        behind[...] = (behind[...].astype(F32) + minus[chunk].astype(F32)).astype(kind)
        two = send(piece(source, chunk, stage, here(axis, 3), ALL), minus_in.at[chunk], sems, (chunk, 3), along(axis, 3))
        return [one, two]

    def ring_close(chunk, stage, sent):
        source, _, _, plus_in, minus_in, _, _ = banks[stage]
        axis = axes_of(chunk)[stage]
        sent[0].wait_recv()
        sent[1].wait_recv()
        own = piece(source, chunk, stage, here(axis, 0), ALL)[...].astype(F32)
        summed = own + plus_in[chunk].astype(F32) + minus_in[chunk].astype(F32)
        if stage == 0:
            mid[chunk] = summed
        else:
            low[chunk] = summed.reshape(NZ, 8, 128)

    shares = {}

    def to_owners(chunk):
        shares[chunk] = [
            send(low.at[chunk, (z + step) % NZ], arrive.at[step, chunk], z_sem, (chunk,), along("z", step))
            for step in order[1:]
        ]

    opened, sent, opened2, sent2 = {}, {}, {}, {}

    def pair_close(chunk):
        pair[chunk].wait_recv()
        spots = pl.ds(chunk * TAPS, TAPS)
        summed = parts[core, spots].astype(F32) + other[spots].astype(F32)
        mine[chunk] = summed.astype(BF16).reshape(TAPS, NY, NX, 16, 128)
        opened[chunk] = ring_open(chunk, 0)

    def next_one(*chunks):
        for chunk in chunks:
            sent[chunk] = ring_next(chunk, 0, opened[chunk])

    def close_one(*chunks):
        for chunk in chunks:
            ring_close(chunk, 0, sent[chunk])
            opened2[chunk] = ring_open(chunk, 1)

    def next_two(*chunks):
        for chunk in chunks:
            sent2[chunk] = ring_next(chunk, 1, opened2[chunk])

    def close_two(*chunks):
        for chunk in chunks:
            ring_close(chunk, 1, sent2[chunk])
            to_owners(chunk)

    step_on(0, grad, range(4))
    weight_taps(5)
    pair_send(5)
    only(has_past, early_on.wait_recv)
    only(has_above, below_early.start)

    @pl.loop(0, 2)
    def _(at):
        hidden_tile(early.at[at, 0], at, 0, False)
        hidden_tile(early.at[at, 1], at, 1, False)

    pair_close(5)
    only(has_future, grad_late.wait_recv)
    only(has_below, above_late.start)
    step_on(0, grad, (4, 5))
    weight_taps(0)
    pair_send(0)
    only(has_above, above_own.wait_recv, above_late.wait_recv)
    step_on(1, grad_above, range(6))
    before = 0
    parts[:, 27] = jnp.zeros((2, 256, 128), BF16)
    for chunk in (2, 3, 4, 1, 6):
        weight_taps(chunk)
        pair_send(chunk)
        pair_close(before)
        before = chunk

    def back_taps(tap):
        where = pl.ds((2 - tap) * 128, 512)
        here_g, here_next = grad[where, :], grad_next[0, where, :]
        above, above_next = grad_above[where, :], grad_next[1, where, :]
        spread[0] += dot_nt(here_g, weight[tap, 0]) + dot_nt(here_next, weight[tap, 2])
        spread[0] += dot_nt(above, weight[tap, 6]) + dot_nt(above_next, weight[tap, 8])
        spread[1] += dot_nt(here_g, weight[tap, 1]) + dot_nt(above, weight[tap, 7])
        spread[2] += dot_nt(here_g, weight[tap, 3]) + dot_nt(here_next, weight[tap, 5])
        spread[3] += dot_nt(here_g, weight[tap, 4])

    def frame_back(first, last):
        @pl.loop(first, last)
        def _(at):
            where = pl.ds(pl.multiple_of(at * 128, 128), 128)
            for row in range(2):
                for half in range(2):
                    lanes = pl.ds(half * 128, 128)
                    tile[row, half, pl.ds(0, 128, stride=2), :] = spread[2 * row, where, lanes]
                    tile[row, half, pl.ds(1, 128, stride=2), :] = spread[2 * row + 1, where, lanes]
                for piece_at in range(4):
                    rows = pl.ds(piece_at * 64, 64)
                    signal = frames[at, row, rows, :].astype(F32)
                    inv = inverse_rms(signal)
                    unit = signal * inv
                    normed = unit * gain_row
                    sigma = 1.0 / (1.0 + jnp.exp(-normed))
                    arrived = jnp.concatenate([tile[row, half, rows, :] for half in range(2)], axis=1)
                    normed_grad = arrived * sigma * (1.0 + normed * (1.0 - sigma))
                    gain_sum[...] += jnp.sum((normed_grad * unit).reshape(8, 8, 256), axis=0)
                    unit_grad = normed_grad * gain_row
                    mean = jnp.mean(unit_grad * unit, axis=-1, keepdims=True)
                    frames_grad[at, row, rows, :] = (inv * (unit_grad - unit * mean)).astype(BF16)

    def spread_out(source, bank, me, axis, total_at, stage):
        bank[me] = source
        return [
            send(bank.at[me], bank.at[me], note_sem, (stage,), along(axis, step)) for step in range(1, total_at)
        ]

    def collect(stage, bank, total_at):
        taken(note_in.at[stage], bank.at[pl.ds(0, total_at - 1)])
        value = bank[0]
        for at in range(1, total_at):
            value = value + bank[at]
        return value

    back_taps(0)
    pair_close(before)
    back_taps(1)
    next_one(5, 0)
    back_taps(2)
    next_one(2, 3)
    frame_back(0, 2)
    next_one(4, 1)
    frame_back(2, 4)
    frames_out = pltpu.make_async_copy(frames_grad, frames_grad_far, out_sem.at[0])
    frames_out.start()
    gain_local = jnp.sum(gain_sum[...], axis=0, keepdims=True)
    bias_local = jnp.sum(grad[pl.ds(0, 512), :].astype(F32), axis=0, keepdims=True)
    spot = lax.broadcasted_iota(jnp.int32, (8, 256), 0)
    small = jnp.where(spot == 0, gain_local, jnp.where(spot == 1, bias_local, 0.0))
    note[0] = small[:, :128]
    note[1] = small[:, 128:]
    notes = [send(note.at[1 - core], note_pair, note_sem, (0,), sibling)]
    next_one(6)
    only(has_below, below_own.wait_recv, below_early.wait_recv)

    @pl.loop(0, 6)
    def _(at):
        hidden_tile(below.at[at], at, 2, False)

    close_one(5, 0, 2, 3)
    notes[0].wait_recv()
    spread_out(note[core] + note_pair[...], note_y, y, "y", NY, 1)
    spread[0] = jnp.broadcast_to(bias[...], (512, 256))

    @pl.loop(0, 3)
    def _(tap):
        where = pl.ds(pl.multiple_of(tap * 128, 128), 512)
        spread[0] += dot_nn(columns[where, :], weight[tap].reshape(2304, 256))

    for frame in range(4):
        for half in range(2):
            woven[frame, half] = spread[0, pl.ds(frame * 128, 128), pl.ds(half * 128, 128)]
    unweave(latent_in)
    outer = hop_one(latent_in, latent_mid, lz_sem)
    latent_mid[z] = latent_in[z]
    hop_two(latent_mid, latent_out, ls_sem, 0)
    close_one(4, 1, 6)
    next_two(5, 0, 2, 3)
    spread_out(collect(1, note_y, NY), note_x, x, "x", NX, 2)
    next_two(4, 1, 6)
    close_two(5, 0, 2, 3)
    close_two(4, 1, 6)
    spread_out(collect(2, note_x, NX), note_z, z, "z", NZ, 3)
    for chunk in (5, 0, 2, 3, 4, 1, 6):
        summed = low[chunk, z]
        taken(z_in.at[chunk], low.at[0, pl.ds(0, 7)])
        for step in order[1:]:
            summed += arrive[step, chunk]
        total[z, chunk] = summed.astype(BF16)

    def back(step):
        return copy_to(total.at[z], total.at[z], zback_sem, (step,), along("z", step))

    for step in order[1:]:
        back(step).start()
    for copy, step in zip(outer, order[1:]):
        copy.wait_recv()
        hop_two(latent_mid, latent_out, ls_sem, step)
    latent_out[:, slab] = latent_mid[:, slab]

    right, left, across = (x + 1) % NX, (x + 3) % NX, (x + 2) % NX
    HALF, REST = pl.ds(0, 4), pl.ds(4, 3)

    def to_right(step, at):
        return copy_to(total.at[at], block.at[x, at], x_sem, (0, step), along("x", 1))

    def to_left(step, at):
        return copy_to(total.at[at], block.at[x, at], x_sem, (1, step), along("x", 3))

    def on_right(step, at):
        half = block.at[left, at, HALF]
        return copy_to(half, half, x_sem, (2, step), along("x", 1))

    def on_left(step, at):
        half = block.at[right, at, REST]
        return copy_to(half, half, x_sem, (3, step), along("x", 3))

    def across_core(which, step, at):
        source = total.at[at] if which == 0 else block.at[(left, right, across)[which - 1], at]
        where = (x, left, right, across)[which]
        return copy_to(source, sib.at[where, at], pair_sem, (which,), sibling)

    def each(body):
        for step in order:
            body(step, (z - step + NZ) % NZ)

    def fan_one(step, at):
        if step:
            back(step).wait_recv()
        to_right(step, at).start()
        to_left(step, at).start()
        across_core(0, step, at).start()

    def fan_two(step, at):
        to_right(step, at).wait_recv()
        on_right(step, at).start()
        across_core(1, step, at).start()
        to_left(step, at).wait_recv()
        on_left(step, at).start()
        across_core(2, step, at).start()

    def fan_three(step, at):
        on_right(step, at).wait_recv()
        on_left(step, at).wait_recv()
        across_core(3, step, at).start()

    def keep(source, half, where, at):
        copy = pltpu.make_async_copy(source, result.at[half, where], out_sem.at[at])
        copy.start()
        return copy

    each(fan_one)
    kept = [frames_out, keep(total, core, x, 1)]
    note_end[0] = collect(3, note_z, NZ)
    note_last = send(note_end.at[0], note_end.at[1], note_sem, (4,), sibling)
    each(fan_two)
    kept += [keep(block.at[left], core, left, 2), keep(block.at[right], core, right, 3)]
    taken(ls_in.at[0], latent_out.at[pl.ds(0, 7)])

    def put_latent(frame, half, value):
        latent[frame, :, pl.ds(half * 128, 128)] = value

    weave(latent_out, put_latent)
    kept.append(pltpu.make_async_copy(latent, latent_far, out_sem.at[4]))
    kept[-1].start()
    each(fan_three)
    kept.append(keep(block.at[across], core, across, 5))
    note_last.wait_recv()
    for at in range(2):
        half = core if at == 0 else 1 - core
        kept.append(pltpu.make_async_copy(note_end.at[at], note_out.at[half], out_sem.at[10 + at]))
        kept[-1].start()
    for which, where in enumerate((x, left, right, across)):
        taken(pair_in.at[which], sib.at[0])
        kept.append(keep(sib.at[where], 1 - core, where, 6 + which))
    seven, three = pl.ds(0, 7), pl.ds(0, 3)
    for family, ref in (
        (0, middle.at[seven]), (1, landed.at[seven]), (2, other), (3, mine.at[:, three]), (4, mid.at[:, three]),
        (5, low.at[:, seven]), (6, total.at[seven]), (7, block.at[three]), (8, sib),
        (9, latent_mid.at[seven]), (10, latent_out.at[seven]),
        (11, note_pair), (12, note_y.at[three]), (13, note_x.at[three]), (14, note_z.at[seven]), (15, note_pair),
    ):
        taken(send_sems.at[family], ref)
    only(has_future, early_on.wait_send)
    only(has_above, below_own.wait_send, below_early.wait_send)
    only(has_past, grad_late.wait_send)
    only(has_below, above_own.wait_send, above_late.wait_send)
    for copy in kept:
        copy.wait()


def whole(latent_grad, frames, gain, weight, bias):
    dma, vmem = pltpu.SemaphoreType.DMA, pltpu.VMEM
    far = pl.BlockSpec(memory_space=pl.ANY)
    return pl.pallas_call(
        whole_kernel,
        out_shape=(
            jax.ShapeDtypeStruct((4, 2, 256, 256), BF16),
            jax.ShapeDtypeStruct((4, 128, 256), BF16),
            jax.ShapeDtypeStruct((2, NX, NZ, CHUNKS, 8, 128), BF16),
            jax.ShapeDtypeStruct((2, 8, 128), F32),
        ),
        in_specs=[far] * 5,
        out_specs=[far] * 4,
        scratch_shapes=[
            vmem((1, 256), F32),
            vmem((1, 256), F32),
            vmem((4, 64, 2, 256), BF16),
            vmem((4, 2, 256, 256), BF16),
            vmem((4, 2, 256, 256), BF16),
            vmem((4, 128, 256), BF16),
            vmem((NX, NZ, CHUNKS, 8, 128), BF16),
            vmem((2, 8, 128), F32),
            vmem((8, 128), F32),
            vmem((NY, 8, 128), F32),
            vmem((NX, 8, 128), F32),
            vmem((NZ, 8, 128), F32),
            vmem((2, 8, 128), F32),
            vmem((3, 9, 256, 256), BF16),
            vmem((NZ, 2 * NX, 8, 256), BF16),
            vmem((NZ, 2 * NX, 8, 256), BF16),
            vmem((NZ, 2 * NX, 8, 256), BF16),
            vmem((2, 512, 128), F32),
            vmem((4, 2, 128, 128), F32),
            vmem((768, 256), BF16),
            vmem((768, 256), BF16),
            vmem((2, 2, 256, 256), BF16),
            vmem((6, 256, 256), BF16),
            vmem((768, 2304), BF16),
            vmem((4, 256, 512), BF16),
            vmem((2, 768, 256), BF16),
            vmem((4, 512, 256), F32),
            vmem((3, 2, 256, 128), F32),
            vmem((8, 256), F32),
            vmem((2, 28, 256, 128), BF16),
            vmem((CHUNKS * TAPS, 256, 128), BF16),
            vmem((CHUNKS, TAPS, NY, NX, 16, 128), BF16),
            vmem((CHUNKS, 2, 4, 16, 128), BF16),
            vmem((CHUNKS, 2, 4, 16, 128), BF16),
            vmem((CHUNKS, TAPS, 4, 16, 128), BF16),
            vmem((CHUNKS, TAPS, 4, 16, 128), BF16),
            vmem((CHUNKS, TAPS, 4, 16, 128), F32),
            vmem((CHUNKS, 2, 16, 128), F32),
            vmem((CHUNKS, 2, 16, 128), F32),
            vmem((CHUNKS, TAPS, 16, 128), F32),
            vmem((CHUNKS, TAPS, 16, 128), F32),
            vmem((CHUNKS, NZ, 8, 128), F32),
            vmem((NZ, CHUNKS, 8, 128), F32),
            vmem((NZ, CHUNKS, 8, 128), BF16),
            vmem((NX, NZ, CHUNKS, 8, 128), BF16),
            vmem((NZ, 2 * NX, 8, 256), BF16),
            vmem((NZ, 2 * NX, 8, 256), BF16),
            vmem((NZ, 2 * NX, 8, 256), BF16),
            dma((5,)),
            dma((22,)),
            dma((6,)),
            dma((NZ,)),
            dma((1,)),
            dma((CHUNKS,)),
            dma((CHUNKS, 4)),
            dma((CHUNKS, 4)),
            dma((CHUNKS,)),
            dma((NZ,)),
            dma((4, NZ)),
            dma((4,)),
            dma((NZ,)),
            dma((1,)),
            dma((5,)),
            dma((12,)),
        ],
        compiler_params=pltpu.CompilerParams(collective_id=1, has_side_effects=True),
        cost_estimate=pl.CostEstimate(flops=5_500_000_000, bytes_accessed=12_000_000, transcendentals=2_000_000),
    )(latent_grad, frames, gain, weight, bias)


def finish_kernel(
    total_far, frames_far, latent_far, note_far, weight_grad, frames_grad, latent, gain_far, bias_far,
    note, gain_grad, bias_grad, total, frames_near, latent_near, latent_wide, wide, sems,
):
    copy = pltpu.make_async_copy
    total_in = copy(total_far, total, sems.at[0])
    frames_in = copy(frames_far, frames_near, sems.at[1])
    latent_in = copy(latent_far, latent_near, sems.at[2])
    note_in = copy(note_far, note, sems.at[12])
    note_in.start()
    total_in.start()
    frames_in.start()
    latent_in.start()
    note_in.wait()
    for core in range(2):
        row = note[core]
        for side in range(2):

            @pl.when(lax.axis_index("tm") == 2 * core + side)
            def _():
                gain_grad[...] = row[0:1, 64 * side : 64 * side + 64]
                bias_grad[...] = row[1:2, 64 * side : 64 * side + 64]

    going = [copy(gain_grad, gain_far, sems.at[13]), copy(bias_grad, bias_far, sems.at[14])]
    for item in going:
        item.start()
    total_in.wait()
    for chunk in range(CHUNKS):
        for tap in range(chunk * TAPS, min(27, chunk * TAPS + TAPS)):
            for core in range(2):
                for x in range(NX):
                    for side in range(2):
                        part = total[core, x, 2 * (tap % TAPS) + side, chunk]
                        wide[tap, pl.ds(x * 16 + side * 8, 8), pl.ds(core * 128, 128)] = part.astype(F32)
        taps = pl.ds(chunk * TAPS, min(27, chunk * TAPS + TAPS) - chunk * TAPS)
        going.append(copy(wide.at[taps], weight_grad.at[taps], sems.at[3 + chunk]))
        going[-1].start()
        if chunk == 1:
            frames_in.wait()
            going.append(copy(frames_near, frames_grad, sems.at[10]))
            going[-1].start()
        if chunk == 3:
            latent_in.wait()
            for frame in range(4):
                latent_wide[frame] = latent_near[frame].reshape(64, 2, 256)
            going.append(copy(latent_wide, latent, sems.at[11]))
            going[-1].start()
    for item in going:
        item.wait()


def finish(total, frames_grad, latent, note):
    far = pl.BlockSpec(memory_space=pl.ANY)
    return pl.pallas_call(
        finish_kernel,
        out_shape=(
            jax.ShapeDtypeStruct((27, 64, 256), F32),
            jax.ShapeDtypeStruct((4, 2, 256, 256), BF16),
            jax.ShapeDtypeStruct((4, 64, 2, 256), BF16),
            jax.ShapeDtypeStruct((1, 64), F32),
            jax.ShapeDtypeStruct((1, 64), F32),
        ),
        in_specs=[far] * 4,
        out_specs=[far] * 5,
        scratch_shapes=[
            pltpu.VMEM((2, 8, 128), F32),
            pltpu.VMEM((1, 64), F32),
            pltpu.VMEM((1, 64), F32),
            pltpu.VMEM((2, NX, NZ, CHUNKS, 8, 128), BF16),
            pltpu.VMEM((4, 2, 256, 256), BF16),
            pltpu.VMEM((4, 128, 256), BF16),
            pltpu.VMEM((4, 64, 2, 256), BF16),
            pltpu.VMEM((27, 64, 256), F32),
            pltpu.SemaphoreType.DMA((15,)),
        ],
    )(total, frames_grad, latent, note)


def on_device(frames, norm_gain, conv_weight, conv_bias, latent_grad):
    frames_grad, latent, total, note = whole(
        latent_grad, frames, norm_gain.reshape(1, 256), conv_weight.reshape(3, 9, 256, 256), conv_bias.reshape(1, 256),
    )
    weight_grad, frames_grad, latent, gain_grad, bias_grad = finish(total, frames_grad, latent, note)
    return (
        latent, frames_grad, weight_grad.reshape(3, 3, 3, 64, 256), gain_grad.reshape(64), bias_grad.reshape(64),
    )


def solution(mesh):
    placed = (P("tm", "rows", None, None), P(), P(), P(), P("tm", None, "rows", None))
    return jax.shard_map(
        on_device,
        mesh=mesh,
        in_specs=placed,
        out_specs=(
            P("tm", None, "rows", None),
            P("tm", "rows", None, None),
            P(None, None, None, "tm", None),
            P("tm"),
            P("tm"),
        ),
        check_vma=False,
    )
```
